128 devices in a mesh: tm: 32 (over z, x, core), word: 4 (over y).
Axes of the slice: x: 4, y: 4, z: 4, core: 2. Of those that a mesh axis runs over, the one named last changes fastest.
Arguments:
- pseudo_obs: float32 [64, 100, 10240], P('tm', None, 'word'), may hold values from -12 to 12
- filter_decay: float32 [64, 100], P('tm'), may hold values from 0.45 to 1
- smooth_gain: float32 [64, 100], P('tm'), may hold values from 0.45 to 1
- log_norm: float32 [64, 100], P('tm'), may hold values from 8.7 to 9.9
- doc_weights: bfloat16 [64, 100, 512], P('tm'), may hold values from 0.0009994507 to 0.099609375
- doc_ids: int32 [64, 65536], P('tm', 'word'), may hold values from 0 to 511
- word_ids: int32 [64, 65536], P('tm', 'word'), may hold values from 0 to 10239, as said below
- counts: int32 [64, 65536], P('tm', 'word'), may hold values from 1 to 11, as said below
Outputs:
- grad_obs: float32 [64, 100, 10240], P('tm', None, 'word')
- topic_counts: float32 [64, 100, 512], P('tm', None, 'word')
The draws below stay inside these ranges and needn't reach their ends.
Inputs may be any that keep to these rules, and one draw needn't show every extreme that they name: `word_ids`: entry e of a slice names a word from (e // 16384) * 2560 to (e // 16384 + 1) * 2560 - 1; a slice may repeat a document and word, and their counts add. `counts`: the count of entry e lies from 1 to 2 + 3 * (e // 16384).
All inputs are finite; a program needn't handle non-finite values.
Results may differ from the reference program's by a relative error of at most 0.00066.
Values sent between devices are 32-bit elements; how exact they have to be, the bound alone decides.
A program may use at most 192 MiB of HBM per device.

```python
import math
import jax
import jax.numpy as jnp
from jax import lax

TOPIC_COUNT = 100
VOCAB_DEV = 2560
DOCS = 512
NNZ_DEV = 16384
NNZ = 65536
MONTH_SLICES = 64
VOCAB = 10240


def decay_rates(key, salt):
    salted = jax.random.fold_in(key, salt)
    random_subkey_list = jax.random.split(salted, 6)
    slow_share = 0.5
    slow_topic = jax.random.uniform(random_subkey_list[0], (TOPIC_COUNT,)) < slow_share
    slow_rate = jax.random.uniform(random_subkey_list[1], (TOPIC_COUNT,), minval=0.3, maxval=0.9) / MONTH_SLICES
    fast_rate = jnp.exp(jax.random.uniform(random_subkey_list[2], (TOPIC_COUNT,), minval=-3.9, maxval=-3.0))
    base_rate = jnp.where(slow_topic, slow_rate, fast_rate)
    wobble = jnp.exp(jax.random.uniform(random_subkey_list[3], (MONTH_SLICES, TOPIC_COUNT), minval=-0.69, maxval=0.69))
    retained_mask = 1.0 - base_rate[None, :] * wobble
    spike_position = jax.random.randint(random_subkey_list[4], (2,), 0, MONTH_SLICES)
    spike_row_list = jnp.any(jnp.arange(MONTH_SLICES)[:, None] == spike_position[None, :], axis=1)
    spike_threshold = jax.random.uniform(random_subkey_list[5], (MONTH_SLICES, TOPIC_COUNT), minval=0.55, maxval=0.8)
    return jnp.where(spike_row_list[:, None], retained_mask * spike_threshold, retained_mask).astype(jnp.float32)


def draw_filter_decay(key, part):
    return decay_rates(key, 11)


def draw_smooth_gain(key, part):
    return decay_rates(key, 23)


def draw_word_ids(key, part):
    shard_of = jnp.arange(NNZ, dtype=jnp.int32) // NNZ_DEV
    offsets = jax.random.randint(key, (MONTH_SLICES, NNZ), 0, VOCAB_DEV)
    return (shard_of[None, :] * VOCAB_DEV + offsets).astype(jnp.int32)


def draw_counts(key, part):
    shard_of = jnp.arange(NNZ, dtype=jnp.int32) // NNZ_DEV
    upper_end = 2 + 3 * shard_of
    raw_values = jax.random.randint(key, (MONTH_SLICES, NNZ), 0, 1 << 20)
    return (1 + raw_values % upper_end[None, :]).astype(jnp.int32)


def touch_ends(entries, rng, least, largest):
    shape = entries.shape
    place = [jax.random.randint(jax.random.fold_in(rng, axis), (), 0, shape[axis]) for axis in range(len(shape))]
    entries = entries.at[tuple(place)].set(least)
    longest = shape.index(max(shape))
    place[longest] = (place[longest] + 1) % shape[longest]
    return entries.at[tuple(place)].set(largest)


def level_of(key, dims, shards, least, top_value):
    gain = 1.0
    for position, shards_of in shards:
        draws = jax.random.uniform(jax.random.fold_in(jax.random.fold_in(key, 6), position), (shards_of,), jnp.float32, least / len(shards), top_value / len(shards))
        gain = gain * jnp.repeat(jnp.exp(draws), dims[position] // shards_of).reshape((-1,) + (1,) * (len(dims) - 1 - position))
    return gain


def normal_values(key, dims, width, bound, cuts=(), kind=jnp.bfloat16):
    drawn = jax.random.normal(key, dims, jnp.float32) * width
    if len(cuts) > 0:
        drawn = level_of(key, dims, cuts, -0.22, 0.18) * drawn
    return jnp.clip(drawn, min=-bound, max=bound).astype(kind)


def setup_inputs(seed: int = 0) -> dict:
    keys = jax.random.split(jax.random.key(seed), 9)
    pseudo_obs = normal_values(keys[0], (MONTH_SLICES, TOPIC_COUNT, VOCAB), 3.0, 12.0, ((0, 32), (2, 4)), jnp.float32)
    filter_decay = draw_filter_decay(jax.random.fold_in(keys[8], 71), 0)
    smooth_gain = draw_smooth_gain(jax.random.fold_in(keys[8], 71), 0)
    log_norm = jnp.clip(8.7 + 1.1999998 * jax.random.uniform(keys[3], (MONTH_SLICES, TOPIC_COUNT), jnp.float32) ** level_of(keys[3], (MONTH_SLICES, TOPIC_COUNT), ((0, 32),), -0.2, 0.2), 8.7, 9.9)
    doc_weights = jnp.clip(jnp.exp(math.log(0.099609375) - 4.6018058 * jax.random.uniform(keys[4], (MONTH_SLICES, TOPIC_COUNT, DOCS), jnp.float32) ** level_of(keys[4], (MONTH_SLICES, TOPIC_COUNT, DOCS), ((0, 32),), -0.2, 0.2)), 0.0009994507, 0.099609375).astype(jnp.bfloat16)
    doc_ids = touch_ends(jax.random.randint(keys[5], (MONTH_SLICES, NNZ), 0, DOCS), jax.random.fold_in(keys[5], 1), 0, DOCS - 1).astype(jnp.int32)
    word_ids = draw_word_ids(jax.random.fold_in(keys[8], 71), 0)
    counts = draw_counts(jax.random.fold_in(keys[8], 71), 0)
    return {"pseudo_obs": pseudo_obs, "filter_decay": filter_decay, "smooth_gain": smooth_gain, "log_norm": log_norm, "doc_weights": doc_weights, "doc_ids": doc_ids, "word_ids": word_ids, "counts": counts}


def recur_forward(factors, added):

    def advance(current, element):
        factor_row, added_row = element
        updated = factor_row[:, None] * current + added_row
        return (updated, updated)
    initial = jnp.zeros(added.shape[1:], jnp.float32)
    return lax.scan(advance, initial, (factors, added))[1]

def smoother(pseudo_obs, filter_decay, smooth_gain, keep_share):
    filtered = recur_forward(filter_decay, (1.0 - filter_decay)[:, :, None] * pseudo_obs)
    return recur_forward(smooth_gain[::-1], (keep_share[:, :, None] * filtered)[::-1])[::-1]

def reference(pseudo_obs, filter_decay, smooth_gain, log_norm, doc_weights, doc_ids, word_ids, counts):
    positions = jnp.arange(MONTH_SLICES, dtype=jnp.int32)
    keep_share = jnp.where((positions == MONTH_SLICES - 1)[:, None], 1.0, 1.0 - smooth_gain)

    def chain_of(values):
        return smoother(values, filter_decay, smooth_gain, keep_share)
    smoothed, pullback = jax.vjp(chain_of, pseudo_obs)

    def slice_terms(inputs):
        smooth_row, norm_row, weight_row, doc_rows, word_cols, count_vals = inputs
        topic_word = jnp.exp(smooth_row - norm_row[:, None])
        topic_round = lax.optimization_barrier(topic_word.astype(jnp.bfloat16))
        flat_counts = jnp.zeros((DOCS * VOCAB,), jnp.float32).at[doc_rows * VOCAB + word_cols].add(count_vals.astype(jnp.float32))
        dense_counts = flat_counts.reshape(DOCS, VOCAB)
        mixture = lax.dot_general(weight_row, topic_round, (((0,), (0,)), ((), ())), preferred_element_type=jnp.float32)
        count_ratio = (dense_counts / mixture).astype(jnp.bfloat16)
        topic_sums = lax.dot_general(topic_round, count_ratio, (((1,), (1,)), ((), ())), preferred_element_type=jnp.float32)
        weighted = jnp.dot(weight_row, count_ratio, preferred_element_type=jnp.float32)
        expected = topic_round.astype(jnp.float32) * weighted
        return (weight_row.astype(jnp.float32) * topic_sums, expected, topic_word)
    topic_counts, expected, topic_word = lax.map(slice_terms, (smoothed, log_norm, doc_weights, doc_ids, word_ids, counts))
    totals = lax.optimization_barrier(jnp.sum(expected, axis=2))
    word_grad = expected - totals[:, :, None] * topic_word
    grad_obs = pullback(word_grad)[0]
    return (grad_obs, topic_counts)
```

```python
import functools

import jax
import jax.numpy as jnp
from jax import lax
from jax.experimental import pallas as pl
from jax.experimental.pallas import tpu as pltpu
from jax.sharding import PartitionSpec as P

MESH = pl.DeviceIdType.MESH
ROWS = 8
LANES = 128
TILE_W = 256
TILE_D = 256
WORD_SPAN = 4096
M_IN, A1, M_OUT, B0, B1, N_IN, C0, N_OUT, E0, E1, X0, X1, DEV_D, DEV_G, DEV_Q = range(15)


def greet(peers):
    barrier = pltpu.get_barrier_semaphore()
    for count, peer in peers:
        def hello(k, _, peer=peer):
            pl.semaphore_signal(barrier, inc=1, device_id=peer(k), device_id_type=MESH)
            return 0
        lax.fori_loop(0, count, hello, 0)
    pl.semaphore_wait(barrier, sum(count for count, _ in peers))


def spread_coefs(coef_ref, table, spread):
    table[...] = jnp.zeros_like(table)
    table[0:16, :] = coef_ref[...]
    row = lambda i: coef_ref[i : i + 1, :]
    entry = row(A1) * row(M_IN)
    table[DEV_D : DEV_D + 1, :] = row(M_OUT) * entry
    table[DEV_G : DEV_G + 1, :] = row(N_OUT) * row(C0) * row(N_IN)
    table[DEV_Q : DEV_Q + 1, :] = row(N_OUT) * (row(C0) * (row(E1) * entry) + row(E0) * row(M_IN))
    spread[...] = table[...].T


def two_sided(chips, chip, core, half, tiles, spread, source, finish, bufs):
    (psend, precv, mine, cbuf, rbuf, obuf, wbuf, gsend, grecv,
     pair_sem, out_send, out_recv, back_send, back_recv, give_send, give_recv) = bufs
    first = core == 0
    partner = {"tm": 2 * chip + 1 - core}
    own = pl.ds(pl.multiple_of(core * half, LANES), half)
    other = pl.ds(pl.multiple_of((1 - core) * half, LANES), half)
    lane = lax.broadcasted_iota(jnp.int32, (ROWS, LANES), 1)

    def rows_of(r):
        return pl.ds(pl.multiple_of(r * ROWS, ROWS), ROWS)

    def col(r, i):
        return spread[rows_of(r), i : i + 1]

    def ends(r, lanes):
        rows = rows_of(r)
        p0 = col(r, B0) * source(0, r, rows, lanes)
        p1 = col(r, A1) * p0 + col(r, B1) * source(1, r, rows, lanes)
        q0 = col(r, C0) * (col(r, E1) * p1) + col(r, E0) * p0
        return col(r, M_OUT) * p1, col(r, N_OUT) * q0

    def give_ends(r, _):
        f, b = ends(r, other)
        psend[rows_of(r), 0:half] = f
        psend[rows_of(r), half : 2 * half] = b
        psend[rows_of(r), 2 * half :] = spread[rows_of(r), :]
        return 0

    lax.fori_loop(0, tiles, give_ends, 0)
    swap = pltpu.make_async_remote_copy(
        src_ref=psend, dst_ref=precv, send_sem=pair_sem.at[0], recv_sem=pair_sem.at[1],
        device_id=partner, device_id_type=MESH)
    swap.start()

    def keep_ends(r, _):
        f, b = ends(r, own)
        mine[rows_of(r), 0:half] = f
        mine[rows_of(r), half : 2 * half] = b
        return 0

    lax.fori_loop(0, tiles, keep_ends, 0)
    swap.wait_recv()

    def scalars(r):
        def both(i):
            a = col(r, i)
            b = precv[rows_of(r), 2 * half + i : 2 * half + i + 1]
            return jnp.where(first, a, b), jnp.where(first, b, a)
        return both(DEV_D), both(DEV_G), both(DEV_Q)

    def halves(r, lo, hi):
        a = mine[rows_of(r), lo:hi]
        b = precv[rows_of(r), lo:hi]
        return a, b

    def out_copy(r):
        return pltpu.make_async_remote_copy(
            src_ref=cbuf.at[rows_of(r)], dst_ref=rbuf.at[chip], send_sem=out_send.at[r], recv_sem=out_recv.at[chip],
            device_id={"tm": 2 * r + core}, device_id_type=MESH)

    def send_chip(k, _):
        r = lax.rem(chip + 1 + k, tiles)
        (d0, d1), (g0, g1), (q0, q1) = scalars(r)
        fa, fb = halves(r, 0, half)
        ba, bb = halves(r, half, 2 * half)
        f0, f1 = jnp.where(first, fa, fb), jnp.where(first, fb, fa)
        b0, b1 = jnp.where(first, ba, bb), jnp.where(first, bb, ba)
        whole = jnp.where(lane == 0, d0 * d1, jnp.where(lane == 1, g0 * g1, g0 * q1 * d0 + q0))
        f_chip = d1 * f0 + f1
        b_chip = g0 * (b1 + q1 * f0) + b0

        @pl.when(r != chip)
        def _():
            cbuf[rows_of(r), 0:half] = f_chip
            cbuf[rows_of(r), half : 2 * half] = b_chip
            cbuf[rows_of(r), 2 * half :] = whole
            out_copy(r).start()

        @pl.when(r == chip)
        def _():
            rbuf[chip, :, 0:half] = f_chip
            rbuf[chip, :, half : 2 * half] = b_chip
            rbuf[chip, :, 2 * half :] = whole

        return 0

    lax.fori_loop(0, tiles, send_chip, 0)

    def back_copy(c):
        return pltpu.make_async_remote_copy(
            src_ref=obuf.at[c], dst_ref=wbuf.at[rows_of(chip)], send_sem=back_send.at[c], recv_sem=back_recv.at[chip],
            device_id={"tm": 2 * c + core}, device_id_type=MESH)

    @pl.when(chip < tiles)
    def _():
        def arrive(k, _):
            src = lax.rem(chip + k, chips)
            pltpu.make_async_remote_copy(
                src_ref=rbuf.at[src], dst_ref=rbuf.at[src], send_sem=out_send.at[0], recv_sem=out_recv.at[src],
                device_id={"tm": 2 * src + core}, device_id_type=MESH).wait_recv()
            return 0

        lax.fori_loop(1, chips, arrive, 0)

        def onward(c, f):
            obuf[c, :, 0:half] = f
            return rbuf[c, :, 2 * half : 2 * half + 1] * f + rbuf[c, :, 0:half]

        lax.fori_loop(0, chips, onward, jnp.zeros((ROWS, half), jnp.float32))

        def homeward(k, s):
            c = chips - 1 - k
            f = obuf[c, :, 0:half]
            obuf[c, :, half : 2 * half] = s

            @pl.when(c != chip)
            def _():
                back_copy(c).start()

            @pl.when(c == chip)
            def _():
                wbuf[rows_of(chip), 0:half] = f
                wbuf[rows_of(chip), half : 2 * half] = s

            return (rbuf[c, :, 2 * half + 1 : 2 * half + 2] * s + rbuf[c, :, half : 2 * half]
                    + rbuf[c, :, 2 * half + 2 : 2 * half + 3] * f)

        lax.fori_loop(0, chips, homeward, jnp.zeros((ROWS, half), jnp.float32))

    def give_copy(r):
        return pltpu.make_async_remote_copy(
            src_ref=gsend.at[rows_of(r)], dst_ref=grecv.at[rows_of(r)], send_sem=give_send.at[r],
            recv_sem=give_recv.at[r], device_id=partner, device_id_type=MESH)

    def resolve(r, lanes, f, s):
        rows = rows_of(r)
        p0 = col(r, M_IN) * f + col(r, B0) * source(0, r, rows, lanes)
        p1 = col(r, A1) * p0 + col(r, B1) * source(1, r, rows, lanes)
        q1 = col(r, N_IN) * s + col(r, E1) * p1
        finish(1, r, rows, lanes, q1)
        finish(0, r, rows, lanes, col(r, C0) * q1 + col(r, E0) * p0)

    def own_half(k, _):
        r = lax.rem(chip + tiles - lax.rem(k, tiles), tiles)

        @pl.when(r != chip)
        def _():
            pltpu.make_async_remote_copy(
                src_ref=wbuf.at[rows_of(r)], dst_ref=wbuf.at[rows_of(r)], send_sem=back_send.at[0],
                recv_sem=back_recv.at[r], device_id={"tm": 2 * r + core}, device_id_type=MESH).wait_recv()

        (d0, _), (_, g1), (_, q1) = scalars(r)
        f = wbuf[rows_of(r), 0:half]
        s = wbuf[rows_of(r), half : 2 * half]
        fa, fb = halves(r, 0, half)
        ba, bb = halves(r, half, 2 * half)
        f_mid = d0 * f + jnp.where(first, fa, fb)
        s_mid = g1 * s + jnp.where(first, bb, ba) + q1 * f_mid
        gsend[rows_of(r), 0:half] = jnp.where(first, f_mid, f)
        gsend[rows_of(r), half : 2 * half] = jnp.where(first, s, s_mid)
        give_copy(r).start()
        resolve(r, own, jnp.where(first, f, f_mid), jnp.where(first, s_mid, s))
        return 0

    lax.fori_loop(0, tiles, own_half, 0)

    def other_half(k, _):
        r = lax.rem(chip + tiles - lax.rem(k, tiles), tiles)
        give_copy(r).wait_recv()
        resolve(r, other, grecv[rows_of(r), 0:half], grecv[rows_of(r), half : 2 * half])
        return 0

    lax.fori_loop(0, tiles, other_half, 0)

    swap.wait_send()

    def drain(r, _):
        give_copy(r).wait_send()

        @pl.when(r != chip)
        def _():
            out_copy(r).wait_send()

        return 0

    lax.fori_loop(0, tiles, drain, 0)

    @pl.when(chip < tiles)
    def _():
        def drain_back(k, _):
            back_copy(lax.rem(chip + k, chips)).wait_send()
            return 0

        lax.fori_loop(1, chips, drain_back, 0)


def chain_peers(chips, chip, core):
    return [
        (chips - 1, lambda k: {"tm": 2 * lax.rem(chip + 1 + k, chips) + core}),
        (1, lambda k: {"tm": 2 * chip + 1 - core}),
    ]


def chain_scratch(chips, half, tiles):
    wide, full = 2 * half + LANES, tiles * ROWS
    f32 = jnp.float32
    dma = pltpu.SemaphoreType.DMA
    return [
        pltpu.VMEM((LANES, LANES), f32), pltpu.VMEM((LANES, LANES), f32),
        pltpu.VMEM((full, wide), f32), pltpu.VMEM((full, wide), f32), pltpu.VMEM((full, 2 * half), f32),
        pltpu.VMEM((full, wide), f32), pltpu.VMEM((chips, ROWS, wide), f32),
        pltpu.VMEM((chips, ROWS, 2 * half), f32), pltpu.VMEM((full, 2 * half), f32),
        pltpu.VMEM((full, 2 * half), f32), pltpu.VMEM((full, 2 * half), f32),
        dma((2,)), dma((tiles,)), dma((chips,)), dma((chips,)), dma((tiles,)), dma((tiles,)), dma((tiles,)),
    ]


def smooth_kernel(chips, topics, x_hbm, coef_ref, tw_ref, raw, xs, load_sem, table, spread, *bufs):
    core, chip = lax.rem(lax.axis_index("tm"), 2), lax.axis_index("tm") // 2
    half, tiles = xs.shape[2] // 2, xs.shape[1] // ROWS
    load = pltpu.make_async_copy(x_hbm, raw, load_sem.at[0])
    load.start()
    spread_coefs(coef_ref, table, spread)
    greet(chain_peers(chips, chip, core))
    load.wait()
    even = topics // ROWS * ROWS

    def move(r, _):
        rows = pl.ds(pl.multiple_of(r * ROWS, ROWS), ROWS)
        for s in range(2):
            xs[s, rows, :] = raw[s, rows, :]
        return 0

    lax.fori_loop(0, topics // ROWS, move, 0)
    if even < topics:
        xs[:, even:, :] = jnp.zeros((2, ROWS, 2 * half), jnp.float32)
        xs[:, even:topics, :] = raw[:, even:, :]

    def source(s, r, rows, lanes):
        return xs[s, rows, lanes]

    def finish(s, r, rows, lanes, q):
        tw_ref[s, rows, lanes] = jnp.exp(q - spread[rows, X0 + s : X0 + s + 1])

    two_sided(chips, chip, core, half, tiles, spread, source, finish, bufs)


def adjoint_kernel(chips, shares, e_hbm, t_hbm, tot_ref, sums_ref, coef_ref, out_ref, own_ref,
                   es, ts, load_sem, totals, tot_in, sums_in, tot_sem, sum_sem, table, spread, *bufs):
    core, chip = lax.rem(lax.axis_index("tm"), 2), lax.axis_index("tm") // 2
    share = lax.axis_index("word")
    half, tiles = es.shape[2] // 2, es.shape[1] // ROWS
    loads = [pltpu.make_async_copy(e_hbm, es, load_sem.at[0]), pltpu.make_async_copy(t_hbm, ts, load_sem.at[1])]
    for load in loads:
        load.start()
    spread_coefs(coef_ref, table, spread)
    neighbour = lambda k: {"word": lax.rem(share + 1 + k, shares)}
    greet(chain_peers(chips, chip, core) + [(shares - 1, neighbour)])

    def tot_copy(k):
        return pltpu.make_async_remote_copy(
            src_ref=tot_ref, dst_ref=tot_in.at[shares - 2 - k], send_sem=tot_sem.at[0, k],
            recv_sem=tot_sem.at[1, shares - 2 - k], device_id=neighbour(k), device_id_type=MESH)

    def sum_copy(k):
        return pltpu.make_async_remote_copy(
            src_ref=sums_ref.at[lax.rem(share + 1 + k, shares)], dst_ref=sums_in.at[shares - 2 - k],
            send_sem=sum_sem.at[0, k], recv_sem=sum_sem.at[1, shares - 2 - k],
            device_id=neighbour(k), device_id_type=MESH)

    for k in range(shares - 1):
        tot_copy(k).start()
    for k in range(shares - 1):
        sum_copy(k).start()
    for load in loads:
        load.wait()
    total = tot_ref[...]
    for k in range(shares - 1):
        tot_copy(shares - 2 - k).wait_recv()
        total = total + tot_in[k]
    totals[...] = total

    def source(s, r, rows, lanes):
        return es[s, rows, lanes] - totals[rows, s : s + 1] * ts[s, rows, lanes]

    def finish(s, r, rows, lanes, q):
        out_ref[s, rows, lanes] = spread[rows, X0 + s : X0 + s + 1] * q

    two_sided(chips, chip, core, half, tiles, spread, source, finish, bufs)
    sums = sums_ref[share]
    for k in range(shares - 1):
        sum_copy(shares - 2 - k).wait_recv()
        sums = sums + sums_in[k]
    own_ref[...] = sums
    for k in range(shares - 1):
        tot_copy(k).wait_send()
        sum_copy(k).wait_send()


def sort_entries(x):
    groups = x.shape[0]
    shape = (groups * 16, 8, 128)
    x = x.reshape(shape)
    sub = lax.broadcasted_iota(jnp.int32, (8, 128), 0)
    lane = lax.broadcasted_iota(jnp.int32, (8, 128), 1)

    def bit_of(j):
        return (sub >> (j - 4)) & 1 if j < 7 else (lane >> (j - 7)) & 1

    def flip(x, k):
        if k >= 14:
            return x
        if k >= 4:
            return x ^ (-bit_of(k))[None]
        pieces = x.reshape((groups * 16 >> (k + 1), 2, 1 << k, 8, 128))
        return jnp.stack([pieces[:, 0], ~pieces[:, 1]], axis=1).reshape(shape)

    def exchange(x, j):
        if j < 4:
            pieces = x.reshape((groups * 16 >> (j + 1), 2, 1 << j, 8, 128))
            a, b = pieces[:, 0], pieces[:, 1]
            return jnp.stack([jnp.minimum(a, b), jnp.maximum(a, b)], axis=1).reshape(shape)
        low = (bit_of(j) == 0)[None]
        if j < 7:
            step, size, axis = 1 << (j - 4), 8, 1
            y = x
        else:
            step, size, axis = 1 << (j - 7), 128, 1
            y = x.reshape((groups * 16 * 8, 128))
        ahead = pltpu.roll(y, size - step, axis).reshape(shape)
        partner = ahead
        if 2 * step != size:
            partner = jnp.where(low, ahead, pltpu.roll(y, step, axis).reshape(shape))
        return jnp.where(low, jnp.minimum(x, partner), jnp.maximum(x, partner))

    for k in range(1, 15):
        x = flip(x, k)
        for j in range(k - 1, -1, -1):
            x = exchange(x, j)
        x = flip(x, k)
    return x.reshape((groups, 16, 8, 128))


def tally_kernel(topics, tw_ref, w_ref, keys_ref, exp_ref, tot_ref, sums_ref,
                 ordered, bounds, w32, wt, wb, tr, acc, ratio, sums, tots):
    slices, full, words = tw_ref.shape
    docs = w_ref.shape[2]
    shares = sums_ref.shape[0]
    keys = sort_entries(keys_ref[...].reshape((slices, 16, 8, 128)))
    ordered[:, 128:, :] = jnp.full((slices, ordered.shape[1] - 128, 128), -1, jnp.int32)
    tiles = words // TILE_W
    blocks = docs // TILE_D
    for s in range(slices):
        ordered[s, 0:128, :] = keys[s].reshape((128, 128)).T
        least, most = keys[s, 0, 0:1, :], keys[s, 15, 7:8, :]
        for h in range(blocks):
            for j in range(tiles):
                low = (h * WORD_SPAN + j * TILE_W) << 12
                bounds[s, h, j, 0] = jnp.sum((most < low).astype(jnp.int32))
                bounds[s, h, j, 1] = jnp.sum((least < low + (TILE_W << 12)).astype(jnp.int32))

    w32[...] = jnp.zeros_like(w32)
    tr[topics // 16 * 16 :, :] = jnp.zeros((128 - topics // 16 * 16, words), jnp.bfloat16)
    lane = lax.broadcasted_iota(jnp.int32, tot_ref.shape, 1)
    place = lax.broadcasted_iota(jnp.int32, (TILE_W, 1), 0).astype(jnp.float32)

    def one_slice(s, _):
        w32[0:topics, :] = w_ref[s].astype(jnp.float32)
        wb[...] = w32[...].astype(jnp.bfloat16)
        wt[...] = w32[...].T.astype(jnp.bfloat16)
        tr[0:full, :] = tw_ref[s].astype(jnp.bfloat16)
        sums[...] = jnp.zeros_like(sums)
        tots[...] = jnp.zeros_like(tots)

        def one_tile(j, _):
            lanes = pl.ds(pl.multiple_of(j * TILE_W, TILE_W), TILE_W)
            topic = tr[:, lanes]
            for h in range(blocks):
                base = h * WORD_SPAN + j * TILE_W
                start, stop = bounds[s, h, j, 0], bounds[s, h, j, 1]
                acc[...] = jnp.zeros_like(acc)

                def pair(i, _):
                    at = start + 2 * i
                    key = jnp.concatenate(
                        [ordered[s, pl.ds(at, 1), :], ordered[s, pl.ds(at + 1, 1), :]], axis=1)
                    word = ((key >> 12) - base).astype(jnp.float32)
                    doc = ((key >> 4) & 255).astype(jnp.float32)
                    count = (key & 15).astype(jnp.float32)
                    docs_hot = jnp.where(place == doc, count, 0.0).astype(jnp.bfloat16)
                    words_hot = jnp.where(place == word, 1.0, 0.0).astype(jnp.bfloat16)
                    acc[...] += lax.dot_general(
                        docs_hot, words_hot, (((1,), (1,)), ((), ())), preferred_element_type=jnp.float32)
                    return 0

                lax.fori_loop(0, (stop - start + 1) // 2, pair, 0)
                mixture = jnp.dot(
                    wt[h * TILE_D : (h + 1) * TILE_D, :], topic, preferred_element_type=jnp.float32)
                ratio[h * TILE_D : (h + 1) * TILE_D, :] = (acc[...] / mixture).astype(jnp.bfloat16)
            sums[...] += lax.dot_general(
                topic, ratio[...], (((1,), (1,)), ((), ())), preferred_element_type=jnp.float32)
            weighted = jnp.dot(wb[...], ratio[...], preferred_element_type=jnp.float32)
            expected = topic[0:full].astype(jnp.float32) * weighted[0:full]
            exp_ref[s, :, lanes] = expected
            tots[...] += expected
            return 0

        lax.fori_loop(0, tiles, one_tile, 0)
        for y in range(shares):
            sums_ref[y, s] = sums[0:full, y * (docs // shares) : (y + 1) * (docs // shares)]
        total = jnp.sum(tots[...], axis=1, keepdims=True)
        tot_ref[...] = jnp.where(lane == s, total, jnp.where(s == 0, 0.0, tot_ref[...]))
        return 0

    lax.fori_loop(0, slices, one_slice, 0)


VMEM_SPEC = pl.BlockSpec(memory_space=pltpu.VMEM)
ANY_SPEC = pl.BlockSpec(memory_space=pl.ANY)
LIMIT = 60 * 1024 * 1024


def tally(topic_word, doc_weights, keys, topics, shares):
    slices, full, words = topic_word.shape
    docs = doc_weights.shape[2]
    f32, bf16 = jnp.float32, jnp.bfloat16
    return pl.pallas_call(
        functools.partial(tally_kernel, topics),
        out_shape=(
            jax.ShapeDtypeStruct((slices, full, words), f32),
            jax.ShapeDtypeStruct((full, LANES), f32),
            jax.ShapeDtypeStruct((shares, slices, full, docs // shares), f32),
        ),
        in_specs=[VMEM_SPEC] * 3,
        out_specs=(VMEM_SPEC,) * 3,
        scratch_shapes=[
            pltpu.VMEM((slices, 136, 128), jnp.int32),
            pltpu.SMEM((slices, docs // TILE_D, words // TILE_W, 2), jnp.int32),
            pltpu.VMEM((128, docs), f32), pltpu.VMEM((docs, 128), bf16), pltpu.VMEM((128, docs), bf16),
            pltpu.VMEM((128, words), bf16), pltpu.VMEM((TILE_D, TILE_W), f32), pltpu.VMEM((docs, TILE_W), bf16),
            pltpu.VMEM((128, docs), f32), pltpu.VMEM((full, TILE_W), f32),
        ],
        compiler_params=pltpu.CompilerParams(vmem_limit_bytes=LIMIT),
        name="tally",
    )(topic_word, doc_weights, keys)


def coef_rows(rows, topics):
    table = jnp.concatenate([r[None] for r in rows], axis=0)
    return jnp.pad(table, ((0, 16 - len(rows)), (0, LANES - topics)))


def make_local(chips, shares):
    def local(pseudo_obs, filter_decay, smooth_gain, log_norm, doc_weights, doc_ids, word_ids, counts):
        slices, topics, words = pseudo_obs.shape
        tiles, half = -(-topics // ROWS), words // 2
        full = tiles * ROWS
        docs = doc_weights.shape[2]
        entries = doc_ids.shape[1]
        f32 = jnp.float32
        positions = lax.axis_index("tm") * slices + jnp.arange(slices, dtype=jnp.int32)
        keep = jnp.where((positions == slices * 2 * chips - 1)[:, None], 1.0, 1.0 - smooth_gain)
        one = jnp.ones((topics,), f32)
        d0, d1 = filter_decay[0], filter_decay[1]
        g0, g1 = smooth_gain[0], smooth_gain[1]
        coef_a = coef_rows(
            [d0, d1, one, 1.0 - d0, 1.0 - d1, g1, g0, one, keep[0], keep[1], log_norm[0], log_norm[1]], topics)
        coef_b = coef_rows(
            [one, g0, g1, one, one, one, d1, d0, keep[0], keep[1], 1.0 - d0, 1.0 - d1], topics)
        word = word_ids - lax.axis_index("word") * words
        keys = ((doc_ids // TILE_D * WORD_SPAN + word) << 12) | ((doc_ids % TILE_D) << 4) | counts
        keys = keys.reshape((slices, 128, entries // 128))

        topic_word = pl.pallas_call(
            functools.partial(smooth_kernel, chips, topics),
            out_shape=jax.ShapeDtypeStruct((slices, full, words), f32),
            in_specs=[ANY_SPEC, VMEM_SPEC],
            out_specs=VMEM_SPEC,
            scratch_shapes=[
                pltpu.VMEM((slices, topics, words), f32), pltpu.VMEM((slices, full, words), f32),
                pltpu.SemaphoreType.DMA((1,)),
            ]
            + chain_scratch(chips, half, tiles),
            compiler_params=pltpu.CompilerParams(
                collective_id=0, has_side_effects=True, vmem_limit_bytes=LIMIT),
            name="smooth",
        )(pseudo_obs, coef_a)
        expected, totals, sums = tally(topic_word, doc_weights, keys, topics, shares)
        dma = pltpu.SemaphoreType.DMA
        grad, own_sums = pl.pallas_call(
            functools.partial(adjoint_kernel, chips, shares),
            out_shape=(
                jax.ShapeDtypeStruct((slices, full, words), f32),
                jax.ShapeDtypeStruct((slices, full, docs // shares), f32),
            ),
            in_specs=[ANY_SPEC, ANY_SPEC, VMEM_SPEC, VMEM_SPEC, VMEM_SPEC],
            out_specs=(VMEM_SPEC, VMEM_SPEC),
            scratch_shapes=[
                pltpu.VMEM((slices, full, words), f32), pltpu.VMEM((slices, full, words), f32), dma((2,)),
                pltpu.VMEM((full, LANES), f32), pltpu.VMEM((shares - 1, full, LANES), f32),
                pltpu.VMEM((shares - 1, slices, full, docs // shares), f32),
                dma((2, shares - 1)), dma((2, shares - 1)),
            ] + chain_scratch(chips, half, tiles),
            compiler_params=pltpu.CompilerParams(
                collective_id=1, has_side_effects=True, vmem_limit_bytes=LIMIT),
            name="adjoint",
        )(expected, topic_word, totals, sums, coef_b)
        own_docs = docs // shares
        own_weights = lax.dynamic_slice_in_dim(doc_weights, lax.axis_index("word") * own_docs, own_docs, 2)
        return grad[:, :topics], own_weights.astype(f32) * own_sums[:, :topics]

    return local


def solution(mesh):
    return jax.shard_map(
        make_local(mesh.shape["tm"] // 2, mesh.shape["word"]),
        mesh=mesh,
        in_specs=(
            P("tm", None, "word"),
            P("tm", None),
            P("tm", None),
            P("tm", None),
            P("tm", None, None),
            P("tm", "word"),
            P("tm", "word"),
            P("tm", "word"),
        ),
        out_specs=(P("tm", None, "word"), P("tm", None, "word")),
        check_vma=False,
    )
```

```python
import functools

import jax
import jax.numpy as jnp
from jax import lax
from jax.experimental import pallas as pl
from jax.experimental.pallas import tpu as pltpu
from jax.sharding import PartitionSpec as P

MESH = pl.DeviceIdType.MESH
ROWS = 8
LANES = 128
TILE_W = 256
TILE_D = 256
WORD_SPAN = 4096
SPARE = 136
DEEP = 4
CHUNKS = 2
M_IN, A1, M_OUT, B0, B1, N_IN, C0, N_OUT, E0, E1, X0, X1, DEV_D, DEV_G, DEV_Q = range(15)


def greet(peers):
    barrier = pltpu.get_barrier_semaphore()
    for count, peer in peers:
        def hello(k, _, peer=peer):
            pl.semaphore_signal(barrier, inc=1, device_id=peer(k), device_id_type=MESH)
            return 0
        lax.fori_loop(0, count, hello, 0)
    pl.semaphore_wait(barrier, sum(count for count, _ in peers))


def spread_coefs(rows, table, spread):
    entry = rows[A1] * rows[M_IN]
    rows = rows + [
        rows[M_OUT] * entry,
        rows[N_OUT] * rows[C0] * rows[N_IN],
        rows[N_OUT] * (rows[C0] * (rows[E1] * entry) + rows[E0] * rows[M_IN]),
    ]
    table[...] = jnp.zeros_like(table)
    for i, row in enumerate(rows):
        table[i : i + 1, 0 : row.shape[1]] = row
    spread[...] = table[...].T


def keep_rows(gain_ref, slices_all):
    slices = gain_ref.shape[0]
    at = lax.axis_index("tm") * slices
    return [
        jnp.where(at + s == slices_all - 1, 1.0, 1.0 - gain_ref[s : s + 1, :]) for s in range(slices)
    ]


def owner_maps(chips, tiles):
    if chips == 16 and tiles == 13:
        return lambda r: r + (r + 3) // 4, lambda c: c - (c + 3) // 5, lambda c: lax.rem(c, 5) != 1
    return lambda r: r, lambda c: c, lambda c: c < tiles


def two_sided(chips, chip, core, half, tiles, spread, source, finish, meanwhile, bufs):
    (psend, precv, mine, cbuf, rbuf, obuf, wbuf, gsend, grecv,
     pair_send, pair_recv, out_send, out_recv, back_send, back_recv, give_send, give_recv) = bufs
    first = core == 0
    width = half // CHUNKS
    partner = {"tm": 2 * chip + 1 - core}
    chip_of, tile_of, owns = owner_maps(chips, tiles)
    is_owner = owns(chip)
    my_tile = tile_of(chip)
    lane = lax.broadcasted_iota(jnp.int32, (ROWS, LANES), 1)

    def rows_of(r):
        return pl.ds(pl.multiple_of(r * ROWS, ROWS), ROWS)

    def col(r, i):
        return spread[rows_of(r), i : i + 1]

    def span(ch):
        return 2 * width + (LANES if ch == 0 else 0)

    def ends(r, side, ch):
        p0 = col(r, B0) * source(0, r, side, ch)
        p1 = col(r, A1) * p0 + col(r, B1) * source(1, r, side, ch)
        q0 = col(r, C0) * (col(r, E1) * p1) + col(r, E0) * p0
        return col(r, M_OUT) * p1, col(r, N_OUT) * q0

    def swap(ch):
        return pltpu.make_async_remote_copy(
            src_ref=psend.at[ch, :, 0 : span(ch)], dst_ref=precv.at[ch, :, 0 : span(ch)],
            send_sem=pair_send.at[ch], recv_sem=pair_recv.at[ch], device_id=partner, device_id_type=MESH)

    for ch in range(CHUNKS):
        def give_ends(r, _, ch=ch):
            f, b = ends(r, 1 - core, ch)
            psend[ch, rows_of(r), 0:width] = f
            psend[ch, rows_of(r), width : 2 * width] = b
            if ch == 0:
                psend[ch, rows_of(r), 2 * width :] = spread[rows_of(r), :]
            return 0

        lax.fori_loop(0, tiles, give_ends, 0)
        swap(ch).start()

    for ch in range(CHUNKS):
        def keep_ends(r, _, ch=ch):
            f, b = ends(r, core, ch)
            mine[ch, rows_of(r), 0:width] = f
            mine[ch, rows_of(r), width : 2 * width] = b
            return 0

        lax.fori_loop(0, tiles, keep_ends, 0)

    def scalars(r):
        def both(i):
            a = col(r, i)
            b = precv[0, rows_of(r), 2 * width + i : 2 * width + i + 1]
            return jnp.where(first, a, b), jnp.where(first, b, a)
        return both(DEV_D), both(DEV_G), both(DEV_Q)

    def ordered_pair(r, ch, lo, hi):
        a = mine[ch, rows_of(r), lo:hi]
        b = precv[ch, rows_of(r), lo:hi]
        return jnp.where(first, a, b), jnp.where(first, b, a)

    def out_copy(r, ch):
        return pltpu.make_async_remote_copy(
            src_ref=cbuf.at[ch, rows_of(r), 0 : span(ch)], dst_ref=rbuf.at[ch, chip, :, 0 : span(ch)],
            send_sem=out_send.at[ch, r], recv_sem=out_recv.at[ch, chip],
            device_id={"tm": 2 * chip_of(r) + core}, device_id_type=MESH)

    for ch in range(CHUNKS):
        swap(ch).wait_recv()

        def send_chip(k, _, ch=ch):
            r = lax.rem(chip + 1 + k, tiles)
            (d0, d1), (g0, g1), (q0, q1) = scalars(r)
            f0, f1 = ordered_pair(r, ch, 0, width)
            b0, b1 = ordered_pair(r, ch, width, 2 * width)
            f_chip = d1 * f0 + f1
            b_chip = g0 * (b1 + q1 * f0) + b0
            cbuf[ch, rows_of(r), 0:width] = f_chip
            cbuf[ch, rows_of(r), width : 2 * width] = b_chip
            if ch == 0:
                cbuf[ch, rows_of(r), 2 * width :] = jnp.where(
                    lane == 0, d0 * d1, jnp.where(lane == 1, g0 * g1, g0 * q1 * d0 + q0))

            @pl.when(chip_of(r) != chip)
            def _():
                out_copy(r, ch).start()

            return 0

        lax.fori_loop(0, tiles, send_chip, 0)

    meanwhile()

    def back_copy(c, ch):
        return pltpu.make_async_remote_copy(
            src_ref=obuf.at[ch, c], dst_ref=wbuf.at[ch, rows_of(my_tile)],
            send_sem=back_send.at[ch, c], recv_sem=back_recv.at[ch, my_tile],
            device_id={"tm": 2 * c + core}, device_id_type=MESH)

    @pl.when(is_owner)
    def _():
        for ch in range(CHUNKS):
            rbuf[ch, chip, :, 0 : span(ch)] = cbuf[ch, rows_of(my_tile), 0 : span(ch)]

            def arrive(k, _, ch=ch):
                src = lax.rem(chip + k, chips)
                pltpu.make_async_remote_copy(
                    src_ref=cbuf.at[ch, 0:ROWS, 0 : span(ch)], dst_ref=rbuf.at[ch, src, :, 0 : span(ch)],
                    send_sem=out_send.at[ch, 0], recv_sem=out_recv.at[ch, src],
                    device_id={"tm": 2 * src + core}, device_id_type=MESH).wait_recv()
                return 0

            lax.fori_loop(1, chips, arrive, 0)

            def scalar(c, i):
                return rbuf[0, c, :, 2 * width + i : 2 * width + i + 1]

            def onward(c, f, ch=ch):
                obuf[ch, c, :, 0:width] = f
                return scalar(c, 0) * f + rbuf[ch, c, :, 0:width]

            lax.fori_loop(0, chips, onward, jnp.zeros((ROWS, width), jnp.float32))

            def homeward(k, s, ch=ch):
                c = chips - 1 - k
                f = obuf[ch, c, :, 0:width]
                obuf[ch, c, :, width : 2 * width] = s

                @pl.when(c != chip)
                def _():
                    back_copy(c, ch).start()

                return scalar(c, 1) * s + rbuf[ch, c, :, width : 2 * width] + scalar(c, 2) * f

            lax.fori_loop(0, chips, homeward, jnp.zeros((ROWS, width), jnp.float32))
            wbuf[ch, rows_of(my_tile), :] = obuf[ch, chip]

    def give_copy(r, ch):
        return pltpu.make_async_remote_copy(
            src_ref=gsend.at[ch, rows_of(r)], dst_ref=grecv.at[ch, rows_of(r)], send_sem=give_send.at[ch, r],
            recv_sem=give_recv.at[ch, r], device_id=partner, device_id_type=MESH)

    def resolve(r, side, ch, f, s):
        p0 = col(r, M_IN) * f + col(r, B0) * source(0, r, side, ch)
        p1 = col(r, A1) * p0 + col(r, B1) * source(1, r, side, ch)
        q1 = col(r, N_IN) * s + col(r, E1) * p1
        finish(1, r, side, ch, q1)
        finish(0, r, side, ch, col(r, C0) * q1 + col(r, E0) * p0)

    def turn(k):
        return lax.rem(my_tile + tiles - k, tiles)

    for ch in range(CHUNKS):
        def own_half(k, _, ch=ch):
            r = turn(k)

            @pl.when(chip_of(r) != chip)
            def _():
                pltpu.make_async_remote_copy(
                    src_ref=obuf.at[ch, 0], dst_ref=wbuf.at[ch, rows_of(r)], send_sem=back_send.at[ch, 0],
                    recv_sem=back_recv.at[ch, r], device_id=partner, device_id_type=MESH).wait_recv()

            (d0, _), (_, g1), (_, q1) = scalars(r)
            f = wbuf[ch, rows_of(r), 0:width]
            s = wbuf[ch, rows_of(r), width : 2 * width]
            f_mid = d0 * f + ordered_pair(r, ch, 0, width)[0]
            s_mid = g1 * s + ordered_pair(r, ch, width, 2 * width)[1] + q1 * f_mid
            gsend[ch, rows_of(r), 0:width] = jnp.where(first, f_mid, f)
            gsend[ch, rows_of(r), width : 2 * width] = jnp.where(first, s, s_mid)
            give_copy(r, ch).start()
            resolve(r, core, ch, jnp.where(first, f, f_mid), jnp.where(first, s_mid, s))
            return 0

        lax.fori_loop(0, tiles, own_half, 0)

    for ch in range(CHUNKS):
        def other_half(k, _, ch=ch):
            r = turn(k)
            give_copy(r, ch).wait_recv()
            resolve(r, 1 - core, ch, grecv[ch, rows_of(r), 0:width], grecv[ch, rows_of(r), width : 2 * width])
            return 0

        lax.fori_loop(0, tiles, other_half, 0)

    for ch in range(CHUNKS):
        swap(ch).wait_send()

        def drain(r, _, ch=ch):
            give_copy(r, ch).wait_send()

            @pl.when(chip_of(r) != chip)
            def _():
                out_copy(r, ch).wait_send()

            return 0

        lax.fori_loop(0, tiles, drain, 0)

        @pl.when(is_owner)
        def _(ch=ch):
            def drain_back(k, _):
                back_copy(lax.rem(chip + k, chips), ch).wait_send()
                return 0

            lax.fori_loop(1, chips, drain_back, 0)


def chain_peers(chips, chip, core):
    return [
        (chips - 1, lambda k: {"tm": 2 * lax.rem(chip + 1 + k, chips) + core}),
        (1, lambda k: {"tm": 2 * chip + 1 - core}),
    ]


def chain_scratch(chips, half, tiles):
    width, full = half // CHUNKS, tiles * ROWS
    wide = 2 * width + LANES
    f32 = jnp.float32
    dma = pltpu.SemaphoreType.DMA
    return [
        pltpu.VMEM((LANES, LANES), f32), pltpu.VMEM((LANES, LANES), f32),
        pltpu.VMEM((CHUNKS, full, wide), f32), pltpu.VMEM((CHUNKS, full, wide), f32),
        pltpu.VMEM((CHUNKS, full, 2 * width), f32),
        pltpu.VMEM((CHUNKS, full, wide), f32), pltpu.VMEM((CHUNKS, chips, ROWS, wide), f32),
        pltpu.VMEM((CHUNKS, chips, ROWS, 2 * width), f32), pltpu.VMEM((CHUNKS, full, 2 * width), f32),
        pltpu.VMEM((CHUNKS, full, 2 * width), f32), pltpu.VMEM((CHUNKS, full, 2 * width), f32),
        dma((CHUNKS,)), dma((CHUNKS,)), dma((CHUNKS, tiles)), dma((CHUNKS, chips)), dma((CHUNKS, chips)),
        dma((CHUNKS, tiles)), dma((CHUNKS, tiles)), dma((CHUNKS, tiles)),
    ]


def lanes_of(side, ch, half):
    width = half // CHUNKS
    return pl.ds(pl.multiple_of(side * half + ch * width, LANES), width)


def smooth_kernel(chips, x_hbm, decay_ref, gain_ref, norm_ref, doc_ref, word_ref, count_ref,
                  tw_ref, order_ref, edge_ref, raw, xs, load_sem, flat, table, spread, *bufs):
    core, chip = lax.rem(lax.axis_index("tm"), 2), lax.axis_index("tm") // 2
    slices, full, words = xs.shape
    half, tiles, blocks = words // 2, full // ROWS, words // LANES
    pitch = slices * blocks
    load = pltpu.make_async_copy(x_hbm, raw.at[0 : x_hbm.shape[0]], load_sem.at[0])
    load.start()
    decay = [decay_ref[s : s + 1, :] for s in range(2)]
    gain = [gain_ref[s : s + 1, :] for s in range(2)]
    norm = [norm_ref[s : s + 1, :] for s in range(2)]
    keep = keep_rows(gain_ref, slices * 2 * chips)
    one = jnp.ones_like(decay[0])
    spread_coefs(
        [decay[0], decay[1], one, 1.0 - decay[0], 1.0 - decay[1], gain[1], gain[0], one,
         keep[0], keep[1], norm[0], norm[1]], table, spread)
    if x_hbm.shape[0] < raw.shape[0]:
        raw[x_hbm.shape[0] :, :] = jnp.zeros((raw.shape[0] - x_hbm.shape[0], LANES), jnp.float32)
    greet(chain_peers(chips, chip, core))
    load.wait()

    def move(r, _):
        rows = pl.ds(pl.multiple_of(r * ROWS, ROWS), ROWS)
        for s in range(slices):
            for i in range(blocks):
                xs[s, rows, i * LANES : (i + 1) * LANES] = raw[
                    pl.ds(r * (ROWS * pitch) + i * slices + s, ROWS, stride=pitch), :]
        return 0

    lax.fori_loop(0, tiles, move, 0)

    def source(s, r, side, ch):
        return xs[s, pl.ds(pl.multiple_of(r * ROWS, ROWS), ROWS), lanes_of(side, ch, half)]

    def finish(s, r, side, ch, q):
        rows = pl.ds(pl.multiple_of(r * ROWS, ROWS), ROWS)
        tw_ref[s, rows, lanes_of(side, ch, half)] = jnp.exp(q - spread[rows, X0 + s : X0 + s + 1])

    def order():
        word = word_ref[...] - lax.axis_index("word") * words
        doc = doc_ref[...]
        keys = (((doc >> 8) * WORD_SPAN + word) << 12) | ((doc & 255) << 4) | count_ref[...]
        keys = sort_entries(keys)
        edge_ref[0:8, :] = keys[0:8]
        edge_ref[8:16, :] = keys[-8:]
        flat[...] = keys
        for s in range(slices):
            order_ref[s, 0:128, :] = flat[pl.ds(s, 128, stride=slices), :].T
            order_ref[s, 128:, :] = jnp.full((SPARE - 128, 128), -1, jnp.int32)

    two_sided(chips, chip, core, half, tiles, spread, source, finish, order, bufs)


def adjoint_kernel(chips, shares, e_hbm, t_hbm, tot_ref, sums_ref, decay_ref, gain_ref, out_ref, own_ref,
                   es, ts, load_sem, totals, tot_in, sums_in, tot_sem, sum_sem, table, spread, *bufs):
    core, chip = lax.rem(lax.axis_index("tm"), 2), lax.axis_index("tm") // 2
    share = lax.axis_index("word")
    slices, full, words = es.shape
    half, tiles, blocks = words // 2, full // ROWS, words // LANES
    pitch = slices * blocks
    loads = [pltpu.make_async_copy(e_hbm, es, load_sem.at[0]), pltpu.make_async_copy(t_hbm, ts, load_sem.at[1])]
    for load in loads:
        load.start()
    decay = [decay_ref[s : s + 1, :] for s in range(2)]
    gain = [gain_ref[s : s + 1, :] for s in range(2)]
    keep = keep_rows(gain_ref, slices * 2 * chips)
    one = jnp.ones_like(decay[0])
    spread_coefs(
        [one, gain[0], gain[1], one, one, one, decay[1], decay[0],
         keep[0], keep[1], 1.0 - decay[0], 1.0 - decay[1]], table, spread)
    neighbour = lambda k: {"word": lax.rem(share + 1 + k, shares)}
    greet(chain_peers(chips, chip, core) + [(shares - 1, neighbour)])

    def tot_copy(k):
        return pltpu.make_async_remote_copy(
            src_ref=tot_ref, dst_ref=tot_in.at[shares - 2 - k], send_sem=tot_sem.at[0, k],
            recv_sem=tot_sem.at[1, shares - 2 - k], device_id=neighbour(k), device_id_type=MESH)

    def sum_copy(k):
        return pltpu.make_async_remote_copy(
            src_ref=sums_ref.at[lax.rem(share + 1 + k, shares)], dst_ref=sums_in.at[shares - 2 - k],
            send_sem=sum_sem.at[0, k], recv_sem=sum_sem.at[1, shares - 2 - k],
            device_id=neighbour(k), device_id_type=MESH)

    for k in range(shares - 1):
        tot_copy(k).start()
    for k in range(shares - 1):
        sum_copy(k).start()
    for load in loads:
        load.wait()
    total = tot_ref[...]
    for k in range(shares - 1):
        tot_copy(shares - 2 - k).wait_recv()
        total = total + tot_in[k]
    totals[...] = total

    def source(s, r, side, ch):
        rows, lanes = pl.ds(pl.multiple_of(r * ROWS, ROWS), ROWS), lanes_of(side, ch, half)
        return es[s, rows, lanes] - totals[rows, s : s + 1] * ts[s, rows, lanes]

    def finish(s, r, side, ch, q):
        rows = pl.ds(pl.multiple_of(r * ROWS, ROWS), ROWS)
        grad = spread[rows, X0 + s : X0 + s + 1] * q
        width = half // CHUNKS
        at = r * (ROWS * pitch) + (side * half + ch * width) // LANES * slices + s
        for i in range(width // LANES):
            out_ref[pl.ds(at + i * slices, ROWS, stride=pitch), :] = grad[:, i * LANES : (i + 1) * LANES]

    def gather_sums():
        for s in range(slices):
            sums = sums_ref[share, s]
            for k in range(shares - 1):
                if s == 0:
                    sum_copy(shares - 2 - k).wait_recv()
                sums = sums + sums_in[k, s]
            own_ref[pl.ds(s, full, stride=slices), :] = sums

    two_sided(chips, chip, core, half, tiles, spread, source, finish, gather_sums, bufs)
    for k in range(shares - 1):
        tot_copy(k).wait_send()
        sum_copy(k).wait_send()


def sort_entries(x):
    shape = (x.shape[0] // 8, 8, 128)
    x = x.reshape(shape)
    high = shape[0].bit_length() - 1
    depth = high + 2 + 7
    sub = lax.broadcasted_iota(jnp.int32, (8, 128), 0)
    lane = lax.broadcasted_iota(jnp.int32, (8, 128), 1)

    def bit_of(j):
        return (sub >> (j - high + 1)) & 1 if j < high + 2 else (lane >> (j - high - 2)) & 1

    def parts(x, j):
        pieces = x.reshape((shape[0] >> (j + 1), 2, 1 << j, 8, 128))
        return pieces[:, 0], pieces[:, 1]

    def joined(a, b):
        return jnp.stack([a, b], axis=1).reshape(shape)

    def flip(x, k):
        if k >= depth:
            return x
        if k >= high:
            return x ^ (-bit_of(k))[None]
        a, b = parts(x, k)
        return joined(a, ~b)

    def exchange(x, j):
        if j < high:
            a, b = parts(x, j)
            return joined(jnp.minimum(a, b), jnp.maximum(a, b))
        low = (bit_of(j) == 0)[None]
        if j < high + 2:
            step, size = 1 << (j - high + 1), 8
            y = x
        else:
            step, size = 1 << (j - high - 2), 128
            y = x.reshape((shape[0] * 8, 128))
        partner = ahead = pltpu.roll(y, size - step, 1).reshape(shape)
        if 2 * step != size:
            partner = jnp.where(low, ahead, pltpu.roll(y, step, 1).reshape(shape))
        return jnp.where(low, jnp.minimum(x, partner), jnp.maximum(x, partner))

    for k in range(1, depth + 1):
        x = flip(x, k)
        for j in range(k - 1, -1, -1):
            x = exchange(x, j)
        x = flip(x, k)
    return x.reshape((shape[0] * 8, 128))


def tally_kernel(topics, tw_hbm, w_ref, order_ref, edge_ref, exp_hbm, tot_ref, sums_ref,
                 tws, exps, load_sem, save_sem, bounds, wraw, w32, wt, wb, tr, acc, ratio, sums, tots, place):
    slices, full, words = tws.shape
    shares = sums_ref.shape[0]
    docs = w32.shape[1]
    tiles, blocks, pieces = words // TILE_W, docs // TILE_D, docs // LANES

    def load(s):
        return pltpu.make_async_copy(tw_hbm.at[s], tws.at[s], load_sem.at[s])

    def save(s):
        return pltpu.make_async_copy(exps.at[s], exp_hbm.at[s], save_sem.at[s])

    for s in range(slices):
        load(s).start()
    for s in range(slices):
        least, most = edge_ref[s : s + 1, :], edge_ref[16 - slices + s : 17 - slices + s, :]
        for h in range(blocks):
            for j in range(tiles):
                low = (h * WORD_SPAN + j * TILE_W) << 12
                bounds[s, h, j, 0] = jnp.sum((most < low).astype(jnp.int32))
                bounds[s, h, j, 1] = jnp.sum((least < low + (TILE_W << 12)).astype(jnp.int32))

    wraw[w_ref.shape[0] :, :] = jnp.zeros((wraw.shape[0] - w_ref.shape[0], LANES), jnp.float32)
    wraw[0 : w_ref.shape[0], :] = w_ref[...].astype(jnp.float32)
    w32[...] = jnp.zeros_like(w32)
    tr[full // 16 * 16 :, :] = jnp.zeros((128 - full // 16 * 16, words), jnp.bfloat16)
    lane = lax.broadcasted_iota(jnp.int32, tot_ref.shape, 1)
    place[...] = lax.broadcasted_iota(jnp.int32, place.shape, 0).astype(jnp.float32).astype(jnp.bfloat16)
    pitch = slices * pieces

    def one_slice(s, _):
        for i in range(pieces):
            w32[0:full, i * LANES : (i + 1) * LANES] = wraw[pl.ds(i * slices + s, full, stride=pitch), :]
        wb[...] = w32[...].astype(jnp.bfloat16)
        wt[...] = w32[...].T.astype(jnp.bfloat16)
        load(s).wait()
        tr[0:full, :] = tws[s].astype(jnp.bfloat16)
        sums[...] = jnp.zeros_like(sums)
        tots[...] = jnp.zeros_like(tots)

        def one_tile(j, _):
            lanes = pl.ds(pl.multiple_of(j * TILE_W, TILE_W), TILE_W)
            topic = tr[:, lanes]
            acc[...] = jnp.zeros_like(acc)
            starts = [bounds[s, h, j, 0] for h in range(blocks)]
            longest = starts[0] * 0
            for h in range(blocks):
                longest = jnp.maximum(longest, (bounds[s, h, j, 1] - starts[h] + DEEP - 1) // DEEP)

            def batch(i, _):
                for h in range(blocks):
                    base = h * WORD_SPAN + j * TILE_W
                    at = jnp.minimum(starts[h] + DEEP * i, SPARE - DEEP)
                    key = jnp.concatenate(
                        [order_ref[s, pl.ds(at + n, 1), :] for n in range(DEEP)], axis=1)
                    word = ((key >> 12) - base).astype(jnp.float32).astype(jnp.bfloat16)
                    doc = ((key >> 4) & 255).astype(jnp.float32).astype(jnp.bfloat16)
                    count = (key & 15).astype(jnp.float32).astype(jnp.bfloat16)
                    docs_hot = jnp.where(place[...] == doc, count, jnp.bfloat16(0))
                    words_hot = jnp.where(place[...] == word, jnp.bfloat16(1), jnp.bfloat16(0))
                    acc[h] += lax.dot_general(
                        docs_hot, words_hot, (((1,), (1,)), ((), ())), preferred_element_type=jnp.float32)
                return 0

            lax.fori_loop(0, longest, batch, 0)
            for h in range(blocks):
                mixture = jnp.dot(
                    wt[h * TILE_D : (h + 1) * TILE_D, :], topic, preferred_element_type=jnp.float32)
                ratio[h * TILE_D : (h + 1) * TILE_D, :] = (acc[h] / mixture).astype(jnp.bfloat16)
            sums[...] += lax.dot_general(
                topic, ratio[...], (((1,), (1,)), ((), ())), preferred_element_type=jnp.float32)
            weighted = jnp.dot(wb[...], ratio[...], preferred_element_type=jnp.float32)
            expected = topic[0:full].astype(jnp.float32) * weighted[0:full]
            exps[s, :, lanes] = expected
            tots[...] += expected
            return 0

        lax.fori_loop(0, tiles, one_tile, 0)
        save(s).start()
        for y in range(shares):
            own = slice(y * (docs // shares), (y + 1) * (docs // shares))
            sums_ref[y, s] = sums[0:full, own] * w32[0:full, own]
        total = jnp.sum(tots[...], axis=1, keepdims=True)
        tot_ref[...] = jnp.where(lane == s, total, jnp.where(s == 0, 0.0, tot_ref[...]))
        return 0

    lax.fori_loop(0, slices, one_slice, 0)
    for s in range(slices):
        save(s).wait()


VMEM_SPEC = pl.BlockSpec(memory_space=pltpu.VMEM)
ANY_SPEC = pl.BlockSpec(memory_space=pl.ANY)
LIMIT = 60 * 1024 * 1024


def tally(topic_word, weights, order, edges, topics, shares):
    slices, full, words = topic_word.shape
    docs = weights.shape[0] * LANES // (slices * topics)
    f32, bf16 = jnp.float32, jnp.bfloat16
    dma = pltpu.SemaphoreType.DMA
    return pl.pallas_call(
        functools.partial(tally_kernel, topics),
        out_shape=(
            jax.ShapeDtypeStruct((slices, full, words), f32),
            jax.ShapeDtypeStruct((full, LANES), f32),
            jax.ShapeDtypeStruct((shares, slices, full, docs // shares), f32),
        ),
        in_specs=[ANY_SPEC] + [VMEM_SPEC] * 3,
        out_specs=(ANY_SPEC, VMEM_SPEC, VMEM_SPEC),
        scratch_shapes=[
            pltpu.VMEM((slices, full, words), f32), pltpu.VMEM((slices, full, words), f32),
            dma((slices,)), dma((slices,)),
            pltpu.SMEM((slices, docs // TILE_D, words // TILE_W, 2), jnp.int32),
            pltpu.VMEM((full * slices * docs // LANES, LANES), f32),
            pltpu.VMEM((128, docs), f32), pltpu.VMEM((docs, 128), bf16), pltpu.VMEM((128, docs), bf16),
            pltpu.VMEM((128, words), bf16), pltpu.VMEM((docs // TILE_D, TILE_D, TILE_W), f32),
            pltpu.VMEM((docs, TILE_W), bf16), pltpu.VMEM((128, docs), f32), pltpu.VMEM((full, TILE_W), f32),
            pltpu.VMEM((TILE_W, DEEP * 128), bf16),
        ],
        compiler_params=pltpu.CompilerParams(vmem_limit_bytes=LIMIT),
        name="tally",
    )(topic_word, weights, order, edges)


def interleaved(x):
    slices, rows, columns = x.shape
    group = 4 if columns % (4 * LANES) == 0 else 1
    x = x.transpose((1, 0, 2)).reshape((rows, slices, columns // LANES // group, group, LANES))
    x = x.transpose((0, 2, 3, 1, 4))
    return x.reshape((rows * columns // LANES * slices, LANES))


def separated(x, slices, rows, columns):
    x = x[: rows * columns // LANES * slices].reshape((rows, columns // LANES, slices, LANES))
    return x.transpose((0, 2, 1, 3)).reshape((rows, slices, columns)).transpose((1, 0, 2))


def make_local(chips, shares):
    def local(pseudo_obs, filter_decay, smooth_gain, log_norm, doc_weights, doc_ids, word_ids, counts):
        slices, topics, words = pseudo_obs.shape
        tiles, half = -(-topics // ROWS), words // 2
        full = tiles * ROWS
        docs = doc_weights.shape[2]
        entries = doc_ids.shape[1]
        f32 = jnp.float32
        dma = pltpu.SemaphoreType.DMA
        flat_rows = full * slices * words // LANES
        ids = [interleaved(a[:, None, :]) for a in (doc_ids, word_ids, counts)]
        topic_word, order, edges = pl.pallas_call(
            functools.partial(smooth_kernel, chips),
            out_shape=(
                jax.ShapeDtypeStruct((slices, full, words), f32),
                jax.ShapeDtypeStruct((slices, SPARE, LANES), jnp.int32),
                jax.ShapeDtypeStruct((16, LANES), jnp.int32),
            ),
            in_specs=[ANY_SPEC] + [VMEM_SPEC] * 6,
            out_specs=(VMEM_SPEC,) * 3,
            scratch_shapes=[
                pltpu.VMEM((flat_rows, LANES), f32), pltpu.VMEM((slices, full, words), f32), dma((1,)),
                pltpu.VMEM((slices * entries // LANES, LANES), jnp.int32),
            ] + chain_scratch(chips, half, tiles),
            compiler_params=pltpu.CompilerParams(
                collective_id=0, has_side_effects=True, vmem_limit_bytes=LIMIT),
            name="smooth",
        )(interleaved(pseudo_obs), filter_decay, smooth_gain, log_norm, *ids)
        expected, totals, sums = tally(topic_word, interleaved(doc_weights), order, edges, topics, shares)
        grad, own = pl.pallas_call(
            functools.partial(adjoint_kernel, chips, shares),
            out_shape=(
                jax.ShapeDtypeStruct((flat_rows, LANES), f32),
                jax.ShapeDtypeStruct((slices * full, docs // shares), f32),
            ),
            in_specs=[ANY_SPEC, ANY_SPEC] + [VMEM_SPEC] * 4,
            out_specs=(VMEM_SPEC, VMEM_SPEC),
            scratch_shapes=[
                pltpu.VMEM((slices, full, words), f32), pltpu.VMEM((slices, full, words), f32), dma((2,)),
                pltpu.VMEM((full, LANES), f32), pltpu.VMEM((shares - 1, full, LANES), f32),
                pltpu.VMEM((shares - 1, slices, full, docs // shares), f32),
                dma((2, shares - 1)), dma((2, shares - 1)),
            ] + chain_scratch(chips, half, tiles),
            compiler_params=pltpu.CompilerParams(
                collective_id=1, has_side_effects=True, vmem_limit_bytes=LIMIT),
            name="adjoint",
        )(expected, topic_word, totals, sums, filter_decay, smooth_gain)
        return separated(grad, slices, topics, words), separated(own, slices, topics, docs // shares)

    return local


def solution(mesh):
    return jax.shard_map(
        make_local(mesh.shape["tm"] // 2, mesh.shape["word"]),
        mesh=mesh,
        in_specs=(
            P("tm", None, "word"),
            P("tm", None),
            P("tm", None),
            P("tm", None),
            P("tm", None, None),
            P("tm", "word"),
            P("tm", "word"),
            P("tm", "word"),
        ),
        out_specs=(P("tm", None, "word"), P("tm", None, "word")),
        check_vma=False,
    )
```

```python
import functools

import jax
import jax.numpy as jnp
from jax import lax
from jax.experimental import pallas as pl
from jax.experimental.pallas import tpu as pltpu
from jax.sharding import PartitionSpec as P

MESH = pl.DeviceIdType.MESH
ROWS = 8
LANES = 128
TILE_W = 256
TILE_D = 256
WORD_SPAN = 4096
SPARE = 136
DEEP = 4
TOGETHER = 2
CHUNKS = 2
M_IN, A1, M_OUT, B0, B1, N_IN, C0, N_OUT, E0, E1, X0, X1, DEV_D, DEV_G, DEV_Q = range(15)


def greet(peers):
    barrier = pltpu.get_barrier_semaphore()
    for count, peer in peers:
        def hello(k, _, peer=peer):
            pl.semaphore_signal(barrier, inc=1, device_id=peer(k), device_id_type=MESH)
            return 0
        lax.fori_loop(0, count, hello, 0)
    return lambda: pl.semaphore_wait(barrier, sum(count for count, _ in peers))


def spread_coefs(rows, table, spread):
    entry = rows[A1] * rows[M_IN]
    rows = rows + [
        rows[M_OUT] * entry,
        rows[N_OUT] * rows[C0] * rows[N_IN],
        rows[N_OUT] * (rows[C0] * (rows[E1] * entry) + rows[E0] * rows[M_IN]),
    ]
    table[...] = jnp.zeros_like(table)
    for i, row in enumerate(rows):
        table[i : i + 1, 0 : row.shape[1]] = row
    spread[...] = table[...].T


def keep_rows(gain_ref, slices_all):
    slices = gain_ref.shape[0]
    at = lax.axis_index("tm") * slices
    return [
        jnp.where(at + s == slices_all - 1, 1.0, 1.0 - gain_ref[s : s + 1, :]) for s in range(slices)
    ]


def owner_maps(chips, tiles):
    if chips == 16 and tiles == 13:
        return lambda r: r + (r + 3) // 4, lambda c: c - (c + 3) // 5, lambda c: lax.rem(c, 5) != 1
    return lambda r: r, lambda c: c, lambda c: c < tiles


def two_sided(chips, chip, core, half, tiles, spread, source, finish, meanwhile, meet, bufs):
    (psend, precv, mine, cbuf, rbuf, obuf, wbuf, gsend, grecv,
     pair_send, pair_recv, out_send, out_recv, back_send, back_recv, give_send, give_recv) = bufs
    first = core == 0
    width = half // CHUNKS
    partner = {"tm": 2 * chip + 1 - core}
    chip_of, tile_of, owns = owner_maps(chips, tiles)
    is_owner = owns(chip)
    my_tile = tile_of(chip)
    lane = lax.broadcasted_iota(jnp.int32, (ROWS, LANES), 1)

    def rows_of(r):
        return pl.ds(pl.multiple_of(r * ROWS, ROWS), ROWS)

    def col(r, i):
        return spread[rows_of(r), i : i + 1]

    def span(ch):
        return 2 * width + (LANES if ch == 0 else 0)

    def ends(r, side, ch):
        p0 = col(r, B0) * source(0, r, side, ch)
        p1 = col(r, A1) * p0 + col(r, B1) * source(1, r, side, ch)
        q0 = col(r, C0) * (col(r, E1) * p1) + col(r, E0) * p0
        return col(r, M_OUT) * p1, col(r, N_OUT) * q0

    def swap(ch):
        return pltpu.make_async_remote_copy(
            src_ref=psend.at[ch, :, 0 : span(ch)], dst_ref=precv.at[ch, :, 0 : span(ch)],
            send_sem=pair_send.at[ch], recv_sem=pair_recv.at[ch], device_id=partner, device_id_type=MESH)

    for ch in range(CHUNKS):
        def give_ends(r, _, ch=ch):
            f, b = ends(r, 1 - core, ch)
            psend[ch, rows_of(r), 0:width] = f
            psend[ch, rows_of(r), width : 2 * width] = b
            if ch == 0:
                psend[ch, rows_of(r), 2 * width :] = spread[rows_of(r), :]
            return 0

        lax.fori_loop(0, tiles, give_ends, 0)
        if ch == 0 and meet is not None:
            meet()
        swap(ch).start()

    for ch in range(CHUNKS):
        def keep_ends(r, _, ch=ch):
            f, b = ends(r, core, ch)
            mine[ch, rows_of(r), 0:width] = f
            mine[ch, rows_of(r), width : 2 * width] = b
            return 0

        lax.fori_loop(0, tiles, keep_ends, 0)

    def scalars(r):
        def both(i):
            a = col(r, i)
            b = precv[0, rows_of(r), 2 * width + i : 2 * width + i + 1]
            return jnp.where(first, a, b), jnp.where(first, b, a)
        return both(DEV_D), both(DEV_G), both(DEV_Q)

    def ordered_pair(r, ch, lo, hi):
        a = mine[ch, rows_of(r), lo:hi]
        b = precv[ch, rows_of(r), lo:hi]
        return jnp.where(first, a, b), jnp.where(first, b, a)

    def out_copy(r, ch):
        return pltpu.make_async_remote_copy(
            src_ref=cbuf.at[ch, rows_of(r), 0 : span(ch)], dst_ref=rbuf.at[ch, chip, :, 0 : span(ch)],
            send_sem=out_send.at[ch, r], recv_sem=out_recv.at[ch, chip],
            device_id={"tm": 2 * chip_of(r) + core}, device_id_type=MESH)

    for ch in range(CHUNKS):
        swap(ch).wait_recv()

        def send_chip(k, _, ch=ch):
            r = lax.rem(chip + 1 + k, tiles)
            (d0, d1), (g0, g1), (q0, q1) = scalars(r)
            f0, f1 = ordered_pair(r, ch, 0, width)
            b0, b1 = ordered_pair(r, ch, width, 2 * width)
            f_chip = d1 * f0 + f1
            b_chip = g0 * (b1 + q1 * f0) + b0
            cbuf[ch, rows_of(r), 0:width] = f_chip
            cbuf[ch, rows_of(r), width : 2 * width] = b_chip
            if ch == 0:
                cbuf[ch, rows_of(r), 2 * width :] = jnp.where(
                    lane == 0, d0 * d1, jnp.where(lane == 1, g0 * g1, g0 * q1 * d0 + q0))

            @pl.when(chip_of(r) != chip)
            def _():
                out_copy(r, ch).start()

            return 0

        lax.fori_loop(0, tiles, send_chip, 0)

    meanwhile()

    def back_copy(c, ch):
        return pltpu.make_async_remote_copy(
            src_ref=obuf.at[ch, c], dst_ref=wbuf.at[ch, rows_of(my_tile)],
            send_sem=back_send.at[ch, c], recv_sem=back_recv.at[ch, my_tile],
            device_id={"tm": 2 * c + core}, device_id_type=MESH)

    @pl.when(is_owner)
    def _():
        for ch in range(CHUNKS):
            rbuf[ch, chip, :, 0 : span(ch)] = cbuf[ch, rows_of(my_tile), 0 : span(ch)]

            def arrive(k, _, ch=ch):
                src = lax.rem(chip + k, chips)
                pltpu.make_async_remote_copy(
                    src_ref=cbuf.at[ch, 0:ROWS, 0 : span(ch)], dst_ref=rbuf.at[ch, src, :, 0 : span(ch)],
                    send_sem=out_send.at[ch, 0], recv_sem=out_recv.at[ch, src],
                    device_id={"tm": 2 * src + core}, device_id_type=MESH).wait_recv()
                return 0

            lax.fori_loop(1, chips, arrive, 0)

            def scalar(c, i):
                return rbuf[0, c, :, 2 * width + i : 2 * width + i + 1]

            def onward(c, f, ch=ch):
                obuf[ch, c, :, 0:width] = f
                return scalar(c, 0) * f + rbuf[ch, c, :, 0:width]

            lax.fori_loop(0, chips, onward, jnp.zeros((ROWS, width), jnp.float32))

            def homeward(k, s, ch=ch):
                c = chips - 1 - k
                f = obuf[ch, c, :, 0:width]
                obuf[ch, c, :, width : 2 * width] = s

                @pl.when(c != chip)
                def _():
                    back_copy(c, ch).start()

                return scalar(c, 1) * s + rbuf[ch, c, :, width : 2 * width] + scalar(c, 2) * f

            lax.fori_loop(0, chips, homeward, jnp.zeros((ROWS, width), jnp.float32))
            wbuf[ch, rows_of(my_tile), :] = obuf[ch, chip]

    def give_copy(r, ch):
        return pltpu.make_async_remote_copy(
            src_ref=gsend.at[ch, rows_of(r)], dst_ref=grecv.at[ch, rows_of(r)], send_sem=give_send.at[ch, r],
            recv_sem=give_recv.at[ch, r], device_id=partner, device_id_type=MESH)

    def resolve(r, side, ch, f, s):
        p0 = col(r, M_IN) * f + col(r, B0) * source(0, r, side, ch)
        p1 = col(r, A1) * p0 + col(r, B1) * source(1, r, side, ch)
        q1 = col(r, N_IN) * s + col(r, E1) * p1
        finish(1, r, side, ch, q1)
        finish(0, r, side, ch, col(r, C0) * q1 + col(r, E0) * p0)

    def turn(k):
        return lax.rem(my_tile + tiles - k, tiles)

    for ch in range(CHUNKS):
        def own_half(k, _, ch=ch):
            r = turn(k)

            @pl.when(chip_of(r) != chip)
            def _():
                pltpu.make_async_remote_copy(
                    src_ref=obuf.at[ch, 0], dst_ref=wbuf.at[ch, rows_of(r)], send_sem=back_send.at[ch, 0],
                    recv_sem=back_recv.at[ch, r], device_id=partner, device_id_type=MESH).wait_recv()

            (d0, _), (_, g1), (_, q1) = scalars(r)
            f = wbuf[ch, rows_of(r), 0:width]
            s = wbuf[ch, rows_of(r), width : 2 * width]
            f_mid = d0 * f + ordered_pair(r, ch, 0, width)[0]
            s_mid = g1 * s + ordered_pair(r, ch, width, 2 * width)[1] + q1 * f_mid
            gsend[ch, rows_of(r), 0:width] = jnp.where(first, f_mid, f)
            gsend[ch, rows_of(r), width : 2 * width] = jnp.where(first, s, s_mid)
            give_copy(r, ch).start()
            resolve(r, core, ch, jnp.where(first, f, f_mid), jnp.where(first, s_mid, s))
            return 0

        lax.fori_loop(0, tiles, own_half, 0)

        def other_half(k, _, ch=ch):
            r = turn(k)
            give_copy(r, ch).wait_recv()
            resolve(r, 1 - core, ch, grecv[ch, rows_of(r), 0:width], grecv[ch, rows_of(r), width : 2 * width])
            return 0

        lax.fori_loop(0, tiles, other_half, 0)

    for ch in range(CHUNKS):
        swap(ch).wait_send()

        def drain(r, _, ch=ch):
            give_copy(r, ch).wait_send()

            @pl.when(chip_of(r) != chip)
            def _():
                out_copy(r, ch).wait_send()

            return 0

        lax.fori_loop(0, tiles, drain, 0)

        @pl.when(is_owner)
        def _(ch=ch):
            def drain_back(k, _):
                back_copy(lax.rem(chip + k, chips), ch).wait_send()
                return 0

            lax.fori_loop(1, chips, drain_back, 0)


def chain_peers(chips, chip, core):
    return [
        (chips - 1, lambda k: {"tm": 2 * lax.rem(chip + 1 + k, chips) + core}),
        (1, lambda k: {"tm": 2 * chip + 1 - core}),
    ]


def chain_scratch(chips, half, tiles):
    width, full = half // CHUNKS, tiles * ROWS
    wide = 2 * width + LANES
    f32 = jnp.float32
    dma = pltpu.SemaphoreType.DMA
    return [
        pltpu.VMEM((LANES, LANES), f32), pltpu.VMEM((LANES, LANES), f32),
        pltpu.VMEM((CHUNKS, full, wide), f32), pltpu.VMEM((CHUNKS, full, wide), f32),
        pltpu.VMEM((CHUNKS, full, 2 * width), f32),
        pltpu.VMEM((CHUNKS, full, wide), f32), pltpu.VMEM((CHUNKS, chips, ROWS, wide), f32),
        pltpu.VMEM((CHUNKS, chips, ROWS, 2 * width), f32), pltpu.VMEM((CHUNKS, full, 2 * width), f32),
        pltpu.VMEM((CHUNKS, full, 2 * width), f32), pltpu.VMEM((CHUNKS, full, 2 * width), f32),
        dma((CHUNKS,)), dma((CHUNKS,)), dma((CHUNKS, tiles)), dma((CHUNKS, chips)), dma((CHUNKS, chips)),
        dma((CHUNKS, tiles)), dma((CHUNKS, tiles)), dma((CHUNKS, tiles)),
    ]


def lanes_of(side, ch, half):
    width = half // CHUNKS
    return pl.ds(pl.multiple_of(side * half + ch * width, LANES), width)


def smooth_kernel(chips, x_hbm, decay_ref, gain_ref, norm_ref, doc_ref, word_ref, count_ref,
                  tw_ref, order_ref, edge_ref, raw, xs, load_sem, flat, table, spread, *bufs):
    core, chip = lax.rem(lax.axis_index("tm"), 2), lax.axis_index("tm") // 2
    slices, full, words = xs.shape
    half, tiles, blocks = words // 2, full // ROWS, words // LANES
    pitch = slices * blocks
    meet = greet(chain_peers(chips, chip, core))
    load = pltpu.make_async_copy(x_hbm, raw.at[0 : x_hbm.shape[0]], load_sem.at[0])
    load.start()
    decay = [decay_ref[s : s + 1, :] for s in range(2)]
    gain = [gain_ref[s : s + 1, :] for s in range(2)]
    norm = [norm_ref[s : s + 1, :] for s in range(2)]
    keep = keep_rows(gain_ref, slices * 2 * chips)
    one = jnp.ones_like(decay[0])
    spread_coefs(
        [decay[0], decay[1], one, 1.0 - decay[0], 1.0 - decay[1], gain[1], gain[0], one,
         keep[0], keep[1], norm[0], norm[1]], table, spread)
    if x_hbm.shape[0] < raw.shape[0]:
        raw[x_hbm.shape[0] :, :] = jnp.zeros((raw.shape[0] - x_hbm.shape[0], LANES), jnp.float32)
    load.wait()

    def move(r, _):
        rows = pl.ds(pl.multiple_of(r * ROWS, ROWS), ROWS)
        for s in range(slices):
            for i in range(blocks):
                xs[s, rows, i * LANES : (i + 1) * LANES] = raw[
                    pl.ds(r * (ROWS * pitch) + i * slices + s, ROWS, stride=pitch), :]
        return 0

    lax.fori_loop(0, tiles, move, 0)

    def source(s, r, side, ch):
        return xs[s, pl.ds(pl.multiple_of(r * ROWS, ROWS), ROWS), lanes_of(side, ch, half)]

    def finish(s, r, side, ch, q):
        rows = pl.ds(pl.multiple_of(r * ROWS, ROWS), ROWS)
        tw_ref[s, rows, lanes_of(side, ch, half)] = jnp.exp(q - spread[rows, X0 + s : X0 + s + 1])

    def order():
        word = word_ref[...] - lax.axis_index("word") * words
        doc = doc_ref[...]
        keys = (((doc >> 8) * WORD_SPAN + word) << 12) | ((doc & 255) << 4) | count_ref[...]
        keys = sort_entries(keys)
        edge_ref[0:8, :] = keys[0:8]
        edge_ref[8:16, :] = keys[-8:]
        flat[...] = keys
        for s in range(slices):
            order_ref[s, 0:128, :] = flat[pl.ds(s, 128, stride=slices), :].T
            order_ref[s, 128:, :] = jnp.full((SPARE - 128, 128), -1, jnp.int32)

    two_sided(chips, chip, core, half, tiles, spread, source, finish, order, meet, bufs)


def adjoint_kernel(chips, shares, t_hbm, dense_hbm, w_ref, decay_ref, gain_ref, out_ref, own_ref,
                   es, ts, tot_ref, sums_ref, load_sem, dense, dense_sem, wraw, w32, wb, wt, tr, ratio, sums, tots,
                   totals, tot_in, sums_in, tot_sem, sum_sem, table, spread, *bufs):
    core, chip = lax.rem(lax.axis_index("tm"), 2), lax.axis_index("tm") // 2
    share = lax.axis_index("word")
    slices, full, words = es.shape
    half, tiles, blocks = words // 2, full // ROWS, words // LANES
    pitch = slices * blocks
    neighbour = lambda k: {"word": lax.rem(share + 1 + k, shares)}
    meet = greet(chain_peers(chips, chip, core) + [(shares - 1, neighbour)])
    expect(t_hbm, dense_hbm, w_ref, es, ts, tot_ref, sums_ref, load_sem, dense, dense_sem,
           wraw, w32, wb, wt, tr, ratio, sums, tots)
    decay = [decay_ref[s : s + 1, :] for s in range(2)]
    gain = [gain_ref[s : s + 1, :] for s in range(2)]
    keep = keep_rows(gain_ref, slices * 2 * chips)
    one = jnp.ones_like(decay[0])
    spread_coefs(
        [one, gain[0], gain[1], one, one, one, decay[1], decay[0],
         keep[0], keep[1], 1.0 - decay[0], 1.0 - decay[1]], table, spread)
    meet()

    def tot_copy(k):
        return pltpu.make_async_remote_copy(
            src_ref=tot_ref, dst_ref=tot_in.at[shares - 2 - k], send_sem=tot_sem.at[0, k],
            recv_sem=tot_sem.at[1, shares - 2 - k], device_id=neighbour(k), device_id_type=MESH)

    def sum_copy(k):
        return pltpu.make_async_remote_copy(
            src_ref=sums_ref.at[lax.rem(share + 1 + k, shares)], dst_ref=sums_in.at[shares - 2 - k],
            send_sem=sum_sem.at[0, k], recv_sem=sum_sem.at[1, shares - 2 - k],
            device_id=neighbour(k), device_id_type=MESH)

    for k in range(shares - 1):
        tot_copy(k).start()
    for k in range(shares - 1):
        sum_copy(k).start()
    total = tot_ref[...]
    for k in range(shares - 1):
        tot_copy(shares - 2 - k).wait_recv()
        total = total + tot_in[k]
    totals[...] = total

    def source(s, r, side, ch):
        rows, lanes = pl.ds(pl.multiple_of(r * ROWS, ROWS), ROWS), lanes_of(side, ch, half)
        return es[s, rows, lanes] - totals[rows, s : s + 1] * ts[s, rows, lanes]

    def finish(s, r, side, ch, q):
        rows = pl.ds(pl.multiple_of(r * ROWS, ROWS), ROWS)
        grad = spread[rows, X0 + s : X0 + s + 1] * q
        width = half // CHUNKS
        at = r * (ROWS * pitch) + (side * half + ch * width) // LANES * slices + s
        for i in range(width // LANES):
            out_ref[pl.ds(at + i * slices, ROWS, stride=pitch), :] = grad[:, i * LANES : (i + 1) * LANES]

    def gather_sums():
        for s in range(slices):
            sums = sums_ref[share, s]
            for k in range(shares - 1):
                if s == 0:
                    sum_copy(shares - 2 - k).wait_recv()
                sums = sums + sums_in[k, s]
            own_ref[pl.ds(s, full, stride=slices), :] = sums

    two_sided(chips, chip, core, half, tiles, spread, source, finish, gather_sums, None, bufs)
    for k in range(shares - 1):
        tot_copy(k).wait_send()
        sum_copy(k).wait_send()


def sort_entries(x):
    shape = (x.shape[0] // 8, 8, 128)
    x = x.reshape(shape)
    high = shape[0].bit_length() - 1
    depth = high + 2 + 7
    sub = lax.broadcasted_iota(jnp.int32, (8, 128), 0)
    lane = lax.broadcasted_iota(jnp.int32, (8, 128), 1)

    def bit_of(j):
        return (sub >> (j - high + 1)) & 1 if j < high + 2 else (lane >> (j - high - 2)) & 1

    def parts(x, j):
        pieces = x.reshape((shape[0] >> (j + 1), 2, 1 << j, 8, 128))
        return pieces[:, 0], pieces[:, 1]

    def joined(a, b):
        return jnp.stack([a, b], axis=1).reshape(shape)

    def flip(x, k):
        if k >= depth:
            return x
        if k >= high:
            return x ^ (-bit_of(k))[None]
        a, b = parts(x, k)
        return joined(a, ~b)

    def exchange(x, j):
        if j < high:
            a, b = parts(x, j)
            return joined(jnp.minimum(a, b), jnp.maximum(a, b))
        low = (bit_of(j) == 0)[None]
        if j < high + 2:
            step, size = 1 << (j - high + 1), 8
            y = x
        else:
            step, size = 1 << (j - high - 2), 128
            y = x.reshape((shape[0] * 8, 128))
        partner = ahead = pltpu.roll(y, size - step, 1).reshape(shape)
        if 2 * step != size:
            partner = jnp.where(low, ahead, pltpu.roll(y, step, 1).reshape(shape))
        return jnp.where(low, jnp.minimum(x, partner), jnp.maximum(x, partner))

    for k in range(1, depth + 1):
        x = flip(x, k)
        for j in range(k - 1, -1, -1):
            x = exchange(x, j)
        x = flip(x, k)
    return x.reshape((shape[0] * 8, 128))


def count_kernel(words, order_ref, edge_ref, dense_hbm, bounds, place, acc, save_sem):
    slices = order_ref.shape[0]
    tiles, blocks = words // TILE_W, acc.shape[1] // TILE_D
    together = acc.shape[0] // 2
    for s in range(slices):
        least, most = edge_ref[s : s + 1, :], edge_ref[16 - slices + s : 17 - slices + s, :]
        for h in range(blocks):
            for j in range(tiles):
                low = (h * WORD_SPAN + j * TILE_W) << 12
                bounds[s * tiles + j, h, 0] = jnp.sum((most < low).astype(jnp.int32))
                bounds[s * tiles + j, h, 1] = jnp.sum((least < low + (TILE_W << 12)).astype(jnp.int32))
    place[...] = lax.broadcasted_iota(jnp.int32, place.shape, 0).astype(jnp.float32).astype(jnp.bfloat16)

    def save(t, slot):
        return pltpu.make_async_copy(
            acc.at[pl.ds(slot * together, together)], dense_hbm.at[pl.ds(t * together, together)], save_sem.at[slot])

    def step(t, _):
        slot = lax.rem(t, 2)
        s = lax.div(t * together, tiles)

        @pl.when(t >= 2)
        def _():
            save(t - 2, slot).wait()

        acc[pl.ds(slot * together, together)] = jnp.zeros((together,) + acc.shape[1:], jnp.float32)
        groups = [(n, h) for n in range(together) for h in range(blocks)]
        starts = [bounds[t * together + n, h, 0] for n, h in groups]
        longest = starts[0] * 0
        for start, (n, h) in zip(starts, groups):
            longest = jnp.maximum(longest, (bounds[t * together + n, h, 1] - start + DEEP - 1) // DEEP)

        def batch(i, _):
            for start, (n, h) in zip(starts, groups):
                base = h * WORD_SPAN + (t * together + n - s * tiles) * TILE_W
                at = jnp.minimum(start + DEEP * i, SPARE - DEEP)
                key = jnp.concatenate([order_ref[s, pl.ds(at + m, 1), :] for m in range(DEEP)], axis=1)
                word = ((key >> 12) - base).astype(jnp.float32).astype(jnp.bfloat16)
                doc = ((key >> 4) & 255).astype(jnp.float32).astype(jnp.bfloat16)
                count = (key & 15).astype(jnp.float32).astype(jnp.bfloat16)
                docs_hot = jnp.where(place[...] == doc, count, jnp.bfloat16(0))
                words_hot = jnp.where(place[...] == word, jnp.bfloat16(1), jnp.bfloat16(0))
                acc[slot * together + n, h * TILE_D : (h + 1) * TILE_D, :] += lax.dot_general(
                    docs_hot, words_hot, (((1,), (1,)), ((), ())), preferred_element_type=jnp.float32)
            return 0

        lax.fori_loop(0, longest, batch, 0)
        save(t, slot).start()
        return 0

    steps = slices * tiles // together
    lax.fori_loop(0, steps, step, 0)
    for t in (steps - 2, steps - 1):
        save(t, t % 2).wait()


def fill_slice(s, wraw, w32, wb, wt):
    slices, pieces = 2, w32.shape[1] // LANES
    full = wraw.shape[0] // (slices * pieces)
    for i in range(pieces):
        w32[0:full, i * LANES : (i + 1) * LANES] = wraw[pl.ds(i * slices + s, full, stride=slices * pieces), :]
    wb[...] = w32[...].astype(jnp.bfloat16)
    wt[...] = w32[...].T.astype(jnp.bfloat16)


def expect(t_hbm, dense_hbm, w_ref, es, ts, tot, sums_out, load_sem, dense, dense_sem,
           wraw, w32, wb, wt, tr, ratio, sums, tots):
    slices, full, words = ts.shape
    shares, docs = sums_out.shape[0], w32.shape[1]
    tiles, blocks = words // TILE_W, docs // TILE_D

    def load(s):
        return pltpu.make_async_copy(t_hbm.at[s], ts.at[s], load_sem.at[s])

    def fetch(t):
        slot = lax.rem(t, 2)
        return pltpu.make_async_copy(dense_hbm.at[t], dense.at[slot], dense_sem.at[slot])

    for s in range(slices):
        load(s).start()
    fetch(0).start()
    wraw[w_ref.shape[0] :, :] = jnp.zeros((wraw.shape[0] - w_ref.shape[0], LANES), jnp.float32)
    wraw[0 : w_ref.shape[0], :] = w_ref[...].astype(jnp.float32)
    w32[...] = jnp.zeros_like(w32)
    tr[full // 16 * 16 :, :] = jnp.zeros((128 - full // 16 * 16, words), jnp.bfloat16)
    lane = lax.broadcasted_iota(jnp.int32, tot.shape, 1)
    tot[...] = jnp.zeros_like(tot)

    for s in range(slices):
        fill_slice(s, wraw, w32, wb, wt)
        load(s).wait()
        tr[0:full, :] = ts[s].astype(jnp.bfloat16)
        sums[...] = jnp.zeros_like(sums)
        tots[...] = jnp.zeros_like(tots)

        def one_tile(j, _, s=s):
            lanes = pl.ds(pl.multiple_of(j * TILE_W, TILE_W), TILE_W)
            topic = tr[:, lanes]
            t = s * tiles + j
            fetch(t).wait()

            @pl.when(t + 1 < slices * tiles)
            def _():
                fetch(t + 1).start()

            for h in range(blocks):
                rows = slice(h * TILE_D, (h + 1) * TILE_D)
                mixture = jnp.dot(wt[rows, :], topic, preferred_element_type=jnp.float32)
                ratio[rows, :] = (dense[lax.rem(t, 2), rows, :] / mixture).astype(jnp.bfloat16)
            sums[...] += lax.dot_general(
                topic, ratio[...], (((1,), (1,)), ((), ())), preferred_element_type=jnp.float32)
            weighted = jnp.dot(wb[...], ratio[...], preferred_element_type=jnp.float32)
            expected = topic[0:full].astype(jnp.float32) * weighted[0:full]
            es[s, :, lanes] = expected
            tots[...] += expected
            return 0

        lax.fori_loop(0, tiles, one_tile, 0)
        for y in range(shares):
            own = slice(y * (docs // shares), (y + 1) * (docs // shares))
            sums_out[y, s] = sums[0:full, own] * w32[0:full, own]
        tot[...] = jnp.where(lane == s, jnp.sum(tots[...], axis=1, keepdims=True), tot[...])


VMEM_SPEC = pl.BlockSpec(memory_space=pltpu.VMEM)
ANY_SPEC = pl.BlockSpec(memory_space=pl.ANY)
LIMIT = 60 * 1024 * 1024


def count_entries(order, edges, words, docs):
    slices = order.shape[0]
    tiles = words // TILE_W
    return pl.pallas_call(
        functools.partial(count_kernel, words),
        out_shape=jax.ShapeDtypeStruct((slices * tiles, docs, TILE_W), jnp.float32),
        in_specs=[VMEM_SPEC] * 2,
        out_specs=ANY_SPEC,
        scratch_shapes=[
            pltpu.SMEM((slices * tiles, docs // TILE_D, 2), jnp.int32),
            pltpu.VMEM((TILE_W, DEEP * 128), jnp.bfloat16),
            pltpu.VMEM((2 * TOGETHER, docs, TILE_W), jnp.float32),
            pltpu.SemaphoreType.DMA((2,)),
        ],
        compiler_params=pltpu.CompilerParams(vmem_limit_bytes=LIMIT),
        name="count",
    )(order, edges)


def interleaved(x):
    slices, rows, columns = x.shape
    group = 4 if columns % (4 * LANES) == 0 else 1
    x = x.transpose((1, 0, 2)).reshape((rows, slices, columns // LANES // group, group, LANES))
    x = x.transpose((0, 2, 3, 1, 4))
    return x.reshape((rows * columns // LANES * slices, LANES))


def separated(x, slices, rows, columns):
    x = x[: rows * columns // LANES * slices].reshape((rows, columns // LANES, slices, LANES))
    return x.transpose((0, 2, 1, 3)).reshape((rows, slices, columns)).transpose((1, 0, 2))


def make_local(chips, shares):
    def local(pseudo_obs, filter_decay, smooth_gain, log_norm, doc_weights, doc_ids, word_ids, counts):
        slices, topics, words = pseudo_obs.shape
        tiles, half = -(-topics // ROWS), words // 2
        full = tiles * ROWS
        docs = doc_weights.shape[2]
        entries = doc_ids.shape[1]
        f32, bf16 = jnp.float32, jnp.bfloat16
        dma = pltpu.SemaphoreType.DMA
        flat_rows = full * slices * words // LANES
        ids = [interleaved(a[:, None, :]) for a in (doc_ids, word_ids, counts)]
        topic_word, order, edges = pl.pallas_call(
            functools.partial(smooth_kernel, chips),
            out_shape=(
                jax.ShapeDtypeStruct((slices, full, words), f32),
                jax.ShapeDtypeStruct((slices, SPARE, LANES), jnp.int32),
                jax.ShapeDtypeStruct((16, LANES), jnp.int32),
            ),
            in_specs=[ANY_SPEC] + [VMEM_SPEC] * 6,
            out_specs=(VMEM_SPEC,) * 3,
            scratch_shapes=[
                pltpu.VMEM((flat_rows, LANES), f32), pltpu.VMEM((slices, full, words), f32), dma((1,)),
                pltpu.VMEM((slices * entries // LANES, LANES), jnp.int32),
            ] + chain_scratch(chips, half, tiles),
            compiler_params=pltpu.CompilerParams(
                collective_id=0, has_side_effects=True, vmem_limit_bytes=LIMIT),
            name="smooth",
        )(interleaved(pseudo_obs), filter_decay, smooth_gain, log_norm, *ids)
        dense = count_entries(order, edges, words, docs)
        grad, own = pl.pallas_call(
            functools.partial(adjoint_kernel, chips, shares),
            out_shape=(
                jax.ShapeDtypeStruct((flat_rows, LANES), f32),
                jax.ShapeDtypeStruct((slices * full, docs // shares), f32),
            ),
            in_specs=[ANY_SPEC, ANY_SPEC] + [VMEM_SPEC] * 3,
            out_specs=(VMEM_SPEC, VMEM_SPEC),
            scratch_shapes=[
                pltpu.VMEM((slices, full, words), f32), pltpu.VMEM((slices, full, words), f32),
                pltpu.VMEM((full, LANES), f32), pltpu.VMEM((shares, slices, full, docs // shares), f32),
                dma((slices,)), pltpu.VMEM((2, docs, TILE_W), f32), dma((2,)),
                pltpu.VMEM((full * slices * docs // LANES, LANES), f32), pltpu.VMEM((128, docs), f32),
                pltpu.VMEM((128, docs), bf16), pltpu.VMEM((docs, 128), bf16), pltpu.VMEM((128, words), bf16),
                pltpu.VMEM((docs, TILE_W), bf16), pltpu.VMEM((128, docs), f32), pltpu.VMEM((full, TILE_W), f32),
                pltpu.VMEM((full, LANES), f32), pltpu.VMEM((shares - 1, full, LANES), f32),
                pltpu.VMEM((shares - 1, slices, full, docs // shares), f32),
                dma((2, shares - 1)), dma((2, shares - 1)),
            ] + chain_scratch(chips, half, tiles),
            compiler_params=pltpu.CompilerParams(
                collective_id=1, has_side_effects=True, vmem_limit_bytes=LIMIT),
            name="adjoint",
        )(topic_word, dense, interleaved(doc_weights), filter_decay, smooth_gain)
        return separated(grad, slices, topics, words), separated(own, slices, topics, docs // shares)

    return local


def solution(mesh):
    return jax.shard_map(
        make_local(mesh.shape["tm"] // 2, mesh.shape["word"]),
        mesh=mesh,
        in_specs=(
            P("tm", None, "word"),
            P("tm", None),
            P("tm", None),
            P("tm", None),
            P("tm", None, None),
            P("tm", "word"),
            P("tm", "word"),
            P("tm", "word"),
        ),
        out_specs=(P("tm", None, "word"), P("tm", None, "word")),
        check_vma=False,
    )
```

```python
import functools

import jax
import jax.numpy as jnp
from jax import lax
from jax.experimental import pallas as pl
from jax.experimental.pallas import tpu as pltpu
from jax.sharding import PartitionSpec as P

MESH = pl.DeviceIdType.MESH
ROWS = 8
LANES = 128
TILE_W = 256
TILE_D = 256
WORD_SPAN = 4096
SPARE = 136
DEEP = 4
TOGETHER = 5
SPAN = 2
ROTATE = 0
CHUNKS = 2
M_IN, A1, M_OUT, B0, B1, N_IN, C0, N_OUT, E0, E1, X0, X1, DEV_D, DEV_G, DEV_Q = range(15)


def greet(peers):
    barrier = pltpu.get_barrier_semaphore()
    for count, peer in peers:
        def hello(k, _, peer=peer):
            pl.semaphore_signal(barrier, inc=1, device_id=peer(k), device_id_type=MESH)
            return 0
        lax.fori_loop(0, count, hello, 0)
    return lambda: pl.semaphore_wait(barrier, sum(count for count, _ in peers))


def spread_coefs(rows, table, spread):
    entry = rows[A1] * rows[M_IN]
    rows = rows + [
        rows[M_OUT] * entry,
        rows[N_OUT] * rows[C0] * rows[N_IN],
        rows[N_OUT] * (rows[C0] * (rows[E1] * entry) + rows[E0] * rows[M_IN]),
    ]
    table[...] = jnp.zeros_like(table)
    for i, row in enumerate(rows):
        table[i : i + 1, 0 : row.shape[1]] = row
    spread[...] = table[...].T


def keep_rows(gain_ref, slices_all):
    slices = gain_ref.shape[0]
    at = lax.axis_index("tm") * slices
    return [
        jnp.where(at + s == slices_all - 1, 1.0, 1.0 - gain_ref[s : s + 1, :]) for s in range(slices)
    ]


def owner_maps(chips, tiles, turn):
    if chips == 16 and tiles == 13:
        def around(c, by):
            return c // 4 * 4 + lax.rem(c + by, 4)

        def tile_of(c):
            c = around(c, 4 - turn)
            return c - (c + 3) // 5

        return lambda r: around(r + (r + 3) // 4, turn), tile_of, lambda c: lax.rem(around(c, 4 - turn), 5) != 1
    return lambda r: r, lambda c: c, lambda c: c < tiles


def two_sided(chips, chip, core, half, tiles, spread, source, finish, meanwhile, meet, bufs):
    (psend, precv, mine, cbuf, rbuf, obuf, wbuf, gsend, grecv,
     pair_send, pair_recv, out_send, out_recv, back_send, back_recv, give_send, give_recv) = bufs
    first = core == 0
    width = half // CHUNKS
    partner = {"tm": 2 * chip + 1 - core}
    chip_of, my_tile, is_owner = [], [], []
    for ch in range(CHUNKS):
        to_chip, to_tile, owns = owner_maps(chips, tiles, lax.rem(ROTATE * (2 * core + ch), 4))
        chip_of.append(to_chip)
        my_tile.append(to_tile(chip))
        is_owner.append(owns(chip))
    lane = lax.broadcasted_iota(jnp.int32, (ROWS, LANES), 1)

    def rows_of(r):
        return pl.ds(pl.multiple_of(r * ROWS, ROWS), ROWS)

    def col(r, i):
        return spread[rows_of(r), i : i + 1]

    def span(ch):
        return 2 * width + (LANES if ch == 0 else 0)

    def ends(r, side, ch):
        p0 = col(r, B0) * source(0, r, side, ch)
        p1 = col(r, A1) * p0 + col(r, B1) * source(1, r, side, ch)
        q0 = col(r, C0) * (col(r, E1) * p1) + col(r, E0) * p0
        return col(r, M_OUT) * p1, col(r, N_OUT) * q0

    def swap(ch):
        return pltpu.make_async_remote_copy(
            src_ref=psend.at[ch, :, 0 : span(ch)], dst_ref=precv.at[ch, :, 0 : span(ch)],
            send_sem=pair_send.at[ch], recv_sem=pair_recv.at[ch], device_id=partner, device_id_type=MESH)

    for ch in range(CHUNKS):
        def give_ends(r, _, ch=ch):
            f, b = ends(r, 1 - core, ch)
            psend[ch, rows_of(r), 0:width] = f
            psend[ch, rows_of(r), width : 2 * width] = b
            if ch == 0:
                psend[ch, rows_of(r), 2 * width :] = spread[rows_of(r), :]
            return 0

        lax.fori_loop(0, tiles, give_ends, 0)
        if ch == 0 and meet is not None:
            meet()
        swap(ch).start()

    for ch in range(CHUNKS):
        def keep_ends(r, _, ch=ch):
            f, b = ends(r, core, ch)
            mine[ch, rows_of(r), 0:width] = f
            mine[ch, rows_of(r), width : 2 * width] = b
            return 0

        lax.fori_loop(0, tiles, keep_ends, 0)

    def scalars(r):
        def both(i):
            a = col(r, i)
            b = precv[0, rows_of(r), 2 * width + i : 2 * width + i + 1]
            return jnp.where(first, a, b), jnp.where(first, b, a)
        return both(DEV_D), both(DEV_G), both(DEV_Q)

    def ordered_pair(r, ch, lo, hi):
        a = mine[ch, rows_of(r), lo:hi]
        b = precv[ch, rows_of(r), lo:hi]
        return jnp.where(first, a, b), jnp.where(first, b, a)

    def out_copy(r, ch):
        return pltpu.make_async_remote_copy(
            src_ref=cbuf.at[ch, rows_of(r), 0 : span(ch)], dst_ref=rbuf.at[ch, chip, :, 0 : span(ch)],
            send_sem=out_send.at[ch, r], recv_sem=out_recv.at[ch, chip],
            device_id={"tm": 2 * chip_of[ch](r) + core}, device_id_type=MESH)

    for ch in range(CHUNKS):
        swap(ch).wait_recv()

        def send_chip(k, _, ch=ch):
            r = lax.rem(my_tile[ch] + 1 + k, tiles)
            (d0, d1), (g0, g1), (q0, q1) = scalars(r)
            f0, f1 = ordered_pair(r, ch, 0, width)
            b0, b1 = ordered_pair(r, ch, width, 2 * width)
            f_chip = d1 * f0 + f1
            b_chip = g0 * (b1 + q1 * f0) + b0
            cbuf[ch, rows_of(r), 0:width] = f_chip
            cbuf[ch, rows_of(r), width : 2 * width] = b_chip
            if ch == 0:
                cbuf[ch, rows_of(r), 2 * width :] = jnp.where(
                    lane == 0, d0 * d1, jnp.where(lane == 1, g0 * g1, g0 * q1 * d0 + q0))

            @pl.when(chip_of[ch](r) != chip)
            def _():
                out_copy(r, ch).start()

            return 0

        lax.fori_loop(0, tiles, send_chip, 0)

    meanwhile()

    def back_copy(c, ch):
        return pltpu.make_async_remote_copy(
            src_ref=obuf.at[ch, c], dst_ref=wbuf.at[ch, rows_of(my_tile[ch])],
            send_sem=back_send.at[ch, c], recv_sem=back_recv.at[ch, my_tile[ch]],
            device_id={"tm": 2 * c + core}, device_id_type=MESH)

    for ch in range(CHUNKS):
        @pl.when(is_owner[ch])
        def _(ch=ch):
            rbuf[ch, chip, :, 0 : span(ch)] = cbuf[ch, rows_of(my_tile[ch]), 0 : span(ch)]

            def arrive(k, _, ch=ch):
                src = lax.rem(chip + k, chips)
                pltpu.make_async_remote_copy(
                    src_ref=cbuf.at[ch, 0:ROWS, 0 : span(ch)], dst_ref=rbuf.at[ch, src, :, 0 : span(ch)],
                    send_sem=out_send.at[ch, 0], recv_sem=out_recv.at[ch, src],
                    device_id={"tm": 2 * src + core}, device_id_type=MESH).wait_recv()
                return 0

            lax.fori_loop(1, chips, arrive, 0)

            def scalar(c, i):
                return rbuf[0, c, :, 2 * width + i : 2 * width + i + 1]

            def onward(c, f, ch=ch):
                obuf[ch, c, :, 0:width] = f
                return scalar(c, 0) * f + rbuf[ch, c, :, 0:width]

            lax.fori_loop(0, chips, onward, jnp.zeros((ROWS, width), jnp.float32))

            def homeward(k, s, ch=ch):
                c = chips - 1 - k
                f = obuf[ch, c, :, 0:width]
                obuf[ch, c, :, width : 2 * width] = s

                @pl.when(c != chip)
                def _():
                    back_copy(c, ch).start()

                return scalar(c, 1) * s + rbuf[ch, c, :, width : 2 * width] + scalar(c, 2) * f

            lax.fori_loop(0, chips, homeward, jnp.zeros((ROWS, width), jnp.float32))
            wbuf[ch, rows_of(my_tile[ch]), :] = obuf[ch, chip]

    def give_copy(r, ch):
        return pltpu.make_async_remote_copy(
            src_ref=gsend.at[ch, rows_of(r)], dst_ref=grecv.at[ch, rows_of(r)], send_sem=give_send.at[ch, r],
            recv_sem=give_recv.at[ch, r], device_id=partner, device_id_type=MESH)

    def resolve(r, side, ch, f, s):
        p0 = col(r, M_IN) * f + col(r, B0) * source(0, r, side, ch)
        p1 = col(r, A1) * p0 + col(r, B1) * source(1, r, side, ch)
        q1 = col(r, N_IN) * s + col(r, E1) * p1
        finish(1, r, side, ch, q1)
        finish(0, r, side, ch, col(r, C0) * q1 + col(r, E0) * p0)

    def turn(k, ch):
        return lax.rem(my_tile[ch] + tiles - k, tiles)

    for ch in range(CHUNKS):
        def own_half(k, _, ch=ch):
            r = turn(k, ch)

            @pl.when(chip_of[ch](r) != chip)
            def _():
                pltpu.make_async_remote_copy(
                    src_ref=obuf.at[ch, 0], dst_ref=wbuf.at[ch, rows_of(r)], send_sem=back_send.at[ch, 0],
                    recv_sem=back_recv.at[ch, r], device_id=partner, device_id_type=MESH).wait_recv()

            (d0, _), (_, g1), (_, q1) = scalars(r)
            f = wbuf[ch, rows_of(r), 0:width]
            s = wbuf[ch, rows_of(r), width : 2 * width]
            f_mid = d0 * f + ordered_pair(r, ch, 0, width)[0]
            s_mid = g1 * s + ordered_pair(r, ch, width, 2 * width)[1] + q1 * f_mid
            gsend[ch, rows_of(r), 0:width] = jnp.where(first, f_mid, f)
            gsend[ch, rows_of(r), width : 2 * width] = jnp.where(first, s, s_mid)
            give_copy(r, ch).start()
            resolve(r, core, ch, jnp.where(first, f, f_mid), jnp.where(first, s_mid, s))
            return 0

        lax.fori_loop(0, tiles, own_half, 0)

        def other_half(k, _, ch=ch):
            r = turn(k, ch)
            give_copy(r, ch).wait_recv()
            resolve(r, 1 - core, ch, grecv[ch, rows_of(r), 0:width], grecv[ch, rows_of(r), width : 2 * width])
            return 0

        lax.fori_loop(0, tiles, other_half, 0)

    for ch in range(CHUNKS):
        swap(ch).wait_send()

        def drain(r, _, ch=ch):
            give_copy(r, ch).wait_send()

            @pl.when(chip_of[ch](r) != chip)
            def _():
                out_copy(r, ch).wait_send()

            return 0

        lax.fori_loop(0, tiles, drain, 0)

        @pl.when(is_owner[ch])
        def _(ch=ch):
            def drain_back(k, _):
                back_copy(lax.rem(chip + k, chips), ch).wait_send()
                return 0

            lax.fori_loop(1, chips, drain_back, 0)


def chain_peers(chips, chip, core):
    return [
        (chips - 1, lambda k: {"tm": 2 * lax.rem(chip + 1 + k, chips) + core}),
        (1, lambda k: {"tm": 2 * chip + 1 - core}),
    ]


def chain_scratch(chips, half, tiles):
    width, full = half // CHUNKS, tiles * ROWS
    wide = 2 * width + LANES
    f32 = jnp.float32
    dma = pltpu.SemaphoreType.DMA
    return [
        pltpu.VMEM((LANES, LANES), f32), pltpu.VMEM((LANES, LANES), f32),
        pltpu.VMEM((CHUNKS, full, wide), f32), pltpu.VMEM((CHUNKS, full, wide), f32),
        pltpu.VMEM((CHUNKS, full, 2 * width), f32),
        pltpu.VMEM((CHUNKS, full, wide), f32), pltpu.VMEM((CHUNKS, chips, ROWS, wide), f32),
        pltpu.VMEM((CHUNKS, chips, ROWS, 2 * width), f32), pltpu.VMEM((CHUNKS, full, 2 * width), f32),
        pltpu.VMEM((CHUNKS, full, 2 * width), f32), pltpu.VMEM((CHUNKS, full, 2 * width), f32),
        dma((CHUNKS,)), dma((CHUNKS,)), dma((CHUNKS, tiles)), dma((CHUNKS, chips)), dma((CHUNKS, chips)),
        dma((CHUNKS, tiles)), dma((CHUNKS, tiles)), dma((CHUNKS, tiles)),
    ]


def lanes_of(side, ch, half):
    width = half // CHUNKS
    return pl.ds(pl.multiple_of(side * half + ch * width, LANES), width)


def smooth_kernel(chips, x_hbm, decay_ref, gain_ref, norm_ref, doc_ref, word_ref, count_ref,
                  tw_ref, order_ref, edge_ref, raw, xs, load_sem, flat, table, spread, *bufs):
    core, chip = lax.rem(lax.axis_index("tm"), 2), lax.axis_index("tm") // 2
    slices, full, words = xs.shape
    half, tiles, blocks = words // 2, full // ROWS, words // LANES
    pitch = slices * blocks
    meet = greet(chain_peers(chips, chip, core))
    load = pltpu.make_async_copy(x_hbm, raw.at[0 : x_hbm.shape[0]], load_sem.at[0])
    load.start()
    decay = [decay_ref[s : s + 1, :] for s in range(2)]
    gain = [gain_ref[s : s + 1, :] for s in range(2)]
    norm = [norm_ref[s : s + 1, :] for s in range(2)]
    keep = keep_rows(gain_ref, slices * 2 * chips)
    one = jnp.ones_like(decay[0])
    spread_coefs(
        [decay[0], decay[1], one, 1.0 - decay[0], 1.0 - decay[1], gain[1], gain[0], one,
         keep[0], keep[1], norm[0], norm[1]], table, spread)
    if x_hbm.shape[0] < raw.shape[0]:
        raw[x_hbm.shape[0] :, :] = jnp.zeros((raw.shape[0] - x_hbm.shape[0], LANES), jnp.float32)
    load.wait()

    def move(r, _):
        rows = pl.ds(pl.multiple_of(r * ROWS, ROWS), ROWS)
        for s in range(slices):
            for i in range(blocks):
                xs[s, rows, i * LANES : (i + 1) * LANES] = raw[
                    pl.ds(r * (ROWS * pitch) + i * slices + s, ROWS, stride=pitch), :]
        return 0

    lax.fori_loop(0, tiles, move, 0)

    def source(s, r, side, ch):
        return xs[s, pl.ds(pl.multiple_of(r * ROWS, ROWS), ROWS), lanes_of(side, ch, half)]

    def finish(s, r, side, ch, q):
        rows = pl.ds(pl.multiple_of(r * ROWS, ROWS), ROWS)
        tw_ref[s, rows, lanes_of(side, ch, half)] = jnp.exp(q - spread[rows, X0 + s : X0 + s + 1])

    def order():
        word = word_ref[...] - lax.axis_index("word") * words
        doc = doc_ref[...]
        keys = (((doc >> 8) * WORD_SPAN + word) << 12) | ((doc & 255) << 4) | count_ref[...]
        keys = sort_entries(keys)
        edge_ref[0:8, :] = keys[0:8]
        edge_ref[8:16, :] = keys[-8:]
        flat[...] = keys
        for s in range(slices):
            order_ref[s, 0:128, :] = flat[pl.ds(s, 128, stride=slices), :].T
            order_ref[s, 128:, :] = jnp.full((SPARE - 128, 128), -1, jnp.int32)

    two_sided(chips, chip, core, half, tiles, spread, source, finish, order, meet, bufs)


def adjoint_kernel(chips, shares, t_hbm, dense_hbm, w_ref, decay_ref, gain_ref, out_ref, own_ref,
                   es, ts, tot_ref, sums_ref, load_sem, dense, dense_sem, wraw, w32, wb, wt, tr, ratio, sums, tots,
                   totals, tot_in, sums_in, tot_sem, sum_sem, table, spread, *bufs):
    core, chip = lax.rem(lax.axis_index("tm"), 2), lax.axis_index("tm") // 2
    share = lax.axis_index("word")
    slices, full, words = es.shape
    half, tiles, blocks = words // 2, full // ROWS, words // LANES
    pitch = slices * blocks
    neighbour = lambda k: {"word": lax.rem(share + 1 + k, shares)}
    meet = greet(chain_peers(chips, chip, core) + [(shares - 1, neighbour)])
    expect(t_hbm, dense_hbm, w_ref, es, ts, tot_ref, sums_ref, load_sem, dense, dense_sem,
           wraw, w32, wb, wt, tr, ratio, sums, tots, table)
    decay = [decay_ref[s : s + 1, :] for s in range(2)]
    gain = [gain_ref[s : s + 1, :] for s in range(2)]
    keep = keep_rows(gain_ref, slices * 2 * chips)
    one = jnp.ones_like(decay[0])
    spread_coefs(
        [one, gain[0], gain[1], one, one, one, decay[1], decay[0],
         keep[0], keep[1], 1.0 - decay[0], 1.0 - decay[1]], table, spread)
    meet()

    def tot_copy(k):
        return pltpu.make_async_remote_copy(
            src_ref=tot_ref, dst_ref=tot_in.at[shares - 2 - k], send_sem=tot_sem.at[0, k],
            recv_sem=tot_sem.at[1, shares - 2 - k], device_id=neighbour(k), device_id_type=MESH)

    def sum_copy(k):
        return pltpu.make_async_remote_copy(
            src_ref=sums_ref.at[lax.rem(share + 1 + k, shares)], dst_ref=sums_in.at[shares - 2 - k],
            send_sem=sum_sem.at[0, k], recv_sem=sum_sem.at[1, shares - 2 - k],
            device_id=neighbour(k), device_id_type=MESH)

    for k in range(shares - 1):
        tot_copy(k).start()
    total = tot_ref[...]
    for k in range(shares - 1):
        tot_copy(shares - 2 - k).wait_recv()
        total = total + tot_in[k]
    table[...] = jnp.zeros_like(table)
    table[0:ROWS, :] = total
    totals[...] = table[...].T

    def source(s, r, side, ch):
        rows, lanes = pl.ds(pl.multiple_of(r * ROWS, ROWS), ROWS), lanes_of(side, ch, half)
        return es[s, rows, lanes] - totals[rows, s : s + 1] * ts[s, rows, lanes]

    def finish(s, r, side, ch, q):
        rows = pl.ds(pl.multiple_of(r * ROWS, ROWS), ROWS)
        grad = spread[rows, X0 + s : X0 + s + 1] * q
        width = half // CHUNKS
        at = r * (ROWS * pitch) + (side * half + ch * width) // LANES * slices + s
        for i in range(width // LANES):
            out_ref[pl.ds(at + i * slices, ROWS, stride=pitch), :] = grad[:, i * LANES : (i + 1) * LANES]

    def gather_sums():
        for k in range(shares - 1):
            sum_copy(k).start()

    def take_sums():
        for s in range(slices):
            sums = sums_ref[share, s]
            for k in range(shares - 1):
                if s == 0:
                    sum_copy(shares - 2 - k).wait_recv()
                sums = sums + sums_in[k, s]
            own_ref[pl.ds(s, full, stride=slices), :] = sums

    two_sided(chips, chip, core, half, tiles, spread, source, finish, gather_sums, None, bufs)
    take_sums()
    for k in range(shares - 1):
        tot_copy(k).wait_send()
        sum_copy(k).wait_send()


def sort_entries(x):
    shape = (x.shape[0] // 8, 8, 128)
    x = x.reshape(shape)
    high = shape[0].bit_length() - 1
    depth = high + 2 + 7
    sub = lax.broadcasted_iota(jnp.int32, (8, 128), 0)
    lane = lax.broadcasted_iota(jnp.int32, (8, 128), 1)

    def bit_of(j):
        return (sub >> (j - high + 1)) & 1 if j < high + 2 else (lane >> (j - high - 2)) & 1

    def parts(x, j):
        pieces = x.reshape((shape[0] >> (j + 1), 2, 1 << j, 8, 128))
        return pieces[:, 0], pieces[:, 1]

    def joined(a, b):
        return jnp.stack([a, b], axis=1).reshape(shape)

    def flip(x, k):
        if k >= depth:
            return x
        if k >= high:
            return x ^ (-bit_of(k))[None]
        a, b = parts(x, k)
        return joined(a, ~b)

    def exchange(x, j):
        if j < high:
            a, b = parts(x, j)
            return joined(jnp.minimum(a, b), jnp.maximum(a, b))
        low = (bit_of(j) == 0)[None]
        if j < high + 2:
            step, size = 1 << (j - high + 1), 8
            y = x
        else:
            step, size = 1 << (j - high - 2), 128
            y = x.reshape((shape[0] * 8, 128))
        partner = ahead = pltpu.roll(y, size - step, 1).reshape(shape)
        if 2 * step != size:
            partner = jnp.where(low, ahead, pltpu.roll(y, step, 1).reshape(shape))
        return jnp.where(low, jnp.minimum(x, partner), jnp.maximum(x, partner))

    for k in range(1, depth + 1):
        x = flip(x, k)
        for j in range(k - 1, -1, -1):
            x = exchange(x, j)
        x = flip(x, k)
    return x.reshape((shape[0] * 8, 128))


def count_kernel(words, order_ref, edge_ref, dense_hbm, bounds, place, acc, save_sem):
    slices = order_ref.shape[0]
    tiles, blocks = words // TILE_W, acc.shape[1] // TILE_D
    together = acc.shape[0] // 2
    for s in range(slices):
        least, most = edge_ref[s : s + 1, :], edge_ref[16 - slices + s : 17 - slices + s, :]
        for h in range(blocks):
            for j in range(tiles):
                low = (h * WORD_SPAN + j * TILE_W) << 12
                bounds[s * tiles + j, h, 0] = jnp.sum((most < low).astype(jnp.int32))
                bounds[s * tiles + j, h, 1] = jnp.sum((least < low + (TILE_W << 12)).astype(jnp.int32))
    place[...] = lax.broadcasted_iota(jnp.int32, place.shape, 0).astype(jnp.float32).astype(jnp.bfloat16)

    def save(t, slot):
        return pltpu.make_async_copy(
            acc.at[pl.ds(slot * together, together)], dense_hbm.at[pl.ds(t * together, together)], save_sem.at[slot])

    def step(t, _):
        slot = lax.rem(t, 2)
        s = lax.div(t * together, tiles)

        @pl.when(t >= 2)
        def _():
            save(t - 2, slot).wait()

        acc[pl.ds(slot * together, together)] = jnp.zeros((together,) + acc.shape[1:], jnp.float32)
        groups = [(n, h) for n in range(together) for h in range(blocks)]
        starts = [bounds[t * together + n, h, 0] for n, h in groups]
        longest = starts[0] * 0
        for start, (n, h) in zip(starts, groups):
            longest = jnp.maximum(longest, (bounds[t * together + n, h, 1] - start + DEEP - 1) // DEEP)

        def batch(i, _):
            for start, (n, h) in zip(starts, groups):
                base = h * WORD_SPAN + (t * together + n - s * tiles) * TILE_W
                at = jnp.minimum(start + DEEP * i, SPARE - DEEP)
                key = jnp.concatenate([order_ref[s, pl.ds(at + m, 1), :] for m in range(DEEP)], axis=1)
                word = ((key >> 12) - base).astype(jnp.float32).astype(jnp.bfloat16)
                doc = ((key >> 4) & 255).astype(jnp.float32).astype(jnp.bfloat16)
                count = (key & 15).astype(jnp.float32).astype(jnp.bfloat16)
                docs_hot = jnp.where(place[...] == doc, count, jnp.bfloat16(0))
                words_hot = jnp.where(place[...] == word, jnp.bfloat16(1), jnp.bfloat16(0))
                acc[slot * together + n, h * TILE_D : (h + 1) * TILE_D, :] += lax.dot_general(
                    docs_hot, words_hot, (((1,), (1,)), ((), ())), preferred_element_type=jnp.float32)
            return 0

        lax.fori_loop(0, longest, batch, 0)
        save(t, slot).start()
        return 0

    steps = slices * tiles // together
    lax.fori_loop(0, steps, step, 0)
    for t in (steps - 2, steps - 1):
        save(t, t % 2).wait()


def fill_slice(s, wraw, w32, wb, wt):
    slices, pieces = 2, w32.shape[1] // LANES
    full = wraw.shape[0] // (slices * pieces)
    for i in range(pieces):
        w32[0:full, i * LANES : (i + 1) * LANES] = wraw[pl.ds(i * slices + s, full, stride=slices * pieces), :]
    wb[...] = w32[...].astype(jnp.bfloat16)
    wt[...] = w32[...].T.astype(jnp.bfloat16)


def expect(t_hbm, dense_hbm, w_ref, es, ts, tot, sums_out, load_sem, dense, dense_sem,
           wraw, w32, wb, wt, tr, ratio, sums, tots, turned):
    slices, full, words = ts.shape
    shares, docs = sums_out.shape[0], w32.shape[1]
    tiles, blocks = words // TILE_W, docs // TILE_D

    def load(s):
        return pltpu.make_async_copy(t_hbm.at[s], ts.at[s], load_sem.at[s])

    def fetch(t):
        return pltpu.make_async_copy(dense_hbm.at[t], dense.at[t], dense_sem.at[t])

    for s in range(slices):
        load(s).start()

        def ask(j, _, s=s):
            fetch(s * tiles + j).start()
            return 0

        lax.fori_loop(0, tiles, ask, 0)
    wraw[w_ref.shape[0] :, :] = jnp.zeros((wraw.shape[0] - w_ref.shape[0], LANES), jnp.float32)
    wraw[0 : w_ref.shape[0], :] = w_ref[...].astype(jnp.float32)
    w32[...] = jnp.zeros_like(w32)
    tr[full // 16 * 16 :, :] = jnp.zeros((128 - full // 16 * 16, words), jnp.bfloat16)
    lane = lax.broadcasted_iota(jnp.int32, (full, LANES), 1)
    turned[...] = jnp.zeros_like(turned)

    for s in range(slices):
        fill_slice(s, wraw, w32, wb, wt)
        load(s).wait()
        tr[0:full, :] = ts[s].astype(jnp.bfloat16)
        sums[...] = jnp.zeros_like(sums)
        tots[...] = jnp.zeros_like(tots)

        def one_tile(j, _, s=s):
            lanes = pl.ds(pl.multiple_of(j * SPAN * TILE_W, TILE_W), SPAN * TILE_W)
            topic = tr[:, lanes]
            for n in range(SPAN):
                t = s * tiles + j * SPAN + n
                part = slice(n * TILE_W, (n + 1) * TILE_W)
                fetch(t).wait()
                for h in range(blocks):
                    rows = slice(h * TILE_D, (h + 1) * TILE_D)
                    mixture = jnp.dot(wt[rows, :], topic[:, part], preferred_element_type=jnp.float32)
                    ratio[rows, part] = (dense[t, rows, :] / mixture).astype(jnp.bfloat16)
            sums[...] += lax.dot_general(
                topic, ratio[...], (((1,), (1,)), ((), ())), preferred_element_type=jnp.float32)
            weighted = jnp.dot(wb[...], ratio[...], preferred_element_type=jnp.float32)
            expected = topic[0:full].astype(jnp.float32) * weighted[0:full]
            es[s, :, lanes] = expected
            for n in range(SPAN):
                tots[...] += expected[:, n * TILE_W : (n + 1) * TILE_W]
            return 0

        lax.fori_loop(0, tiles // SPAN, one_tile, 0)
        for y in range(shares):
            own = slice(y * (docs // shares), (y + 1) * (docs // shares))
            sums_out[y, s] = sums[0:full, own] * w32[0:full, own]
        turned[0:full, :] = jnp.where(lane == s, jnp.sum(tots[...], axis=1, keepdims=True), turned[0:full, :])
    tot[...] = turned[...].T[0:ROWS, :]


VMEM_SPEC = pl.BlockSpec(memory_space=pltpu.VMEM)
ANY_SPEC = pl.BlockSpec(memory_space=pl.ANY)
LIMIT = 60 * 1024 * 1024


def count_entries(order, edges, words, docs):
    slices = order.shape[0]
    tiles = words // TILE_W
    return pl.pallas_call(
        functools.partial(count_kernel, words),
        out_shape=jax.ShapeDtypeStruct((slices * tiles, docs, TILE_W), jnp.float32),
        in_specs=[VMEM_SPEC] * 2,
        out_specs=ANY_SPEC,
        scratch_shapes=[
            pltpu.SMEM((slices * tiles, docs // TILE_D, 2), jnp.int32),
            pltpu.VMEM((TILE_W, DEEP * 128), jnp.bfloat16),
            pltpu.VMEM((2 * TOGETHER, docs, TILE_W), jnp.float32),
            pltpu.SemaphoreType.DMA((2,)),
        ],
        compiler_params=pltpu.CompilerParams(vmem_limit_bytes=LIMIT),
        name="count",
    )(order, edges)


def interleaved(x):
    slices, rows, columns = x.shape
    group = 4 if columns % (4 * LANES) == 0 else 1
    x = x.transpose((1, 0, 2)).reshape((rows, slices, columns // LANES // group, group, LANES))
    x = x.transpose((0, 2, 3, 1, 4))
    return x.reshape((rows * columns // LANES * slices, LANES))


def separated(x, slices, rows, columns):
    x = x[: rows * columns // LANES * slices].reshape((rows, columns // LANES, slices, LANES))
    return x.transpose((0, 2, 1, 3)).reshape((rows, slices, columns)).transpose((1, 0, 2))


def make_local(chips, shares):
    def local(pseudo_obs, filter_decay, smooth_gain, log_norm, doc_weights, doc_ids, word_ids, counts):
        slices, topics, words = pseudo_obs.shape
        tiles, half = -(-topics // ROWS), words // 2
        full = tiles * ROWS
        docs = doc_weights.shape[2]
        entries = doc_ids.shape[1]
        f32, bf16 = jnp.float32, jnp.bfloat16
        dma = pltpu.SemaphoreType.DMA
        flat_rows = full * slices * words // LANES
        ids = [interleaved(a[:, None, :]) for a in (doc_ids, word_ids, counts)]
        topic_word, order, edges = pl.pallas_call(
            functools.partial(smooth_kernel, chips),
            out_shape=(
                jax.ShapeDtypeStruct((slices, full, words), f32),
                jax.ShapeDtypeStruct((slices, SPARE, LANES), jnp.int32),
                jax.ShapeDtypeStruct((16, LANES), jnp.int32),
            ),
            in_specs=[ANY_SPEC] + [VMEM_SPEC] * 6,
            out_specs=(VMEM_SPEC,) * 3,
            scratch_shapes=[
                pltpu.VMEM((flat_rows, LANES), f32), pltpu.VMEM((slices, full, words), f32), dma((1,)),
                pltpu.VMEM((slices * entries // LANES, LANES), jnp.int32),
            ] + chain_scratch(chips, half, tiles),
            compiler_params=pltpu.CompilerParams(
                collective_id=0, has_side_effects=True, vmem_limit_bytes=LIMIT),
            name="smooth",
        )(interleaved(pseudo_obs), filter_decay, smooth_gain, log_norm, *ids)
        dense = count_entries(order, edges, words, docs)
        grad, own = pl.pallas_call(
            functools.partial(adjoint_kernel, chips, shares),
            out_shape=(
                jax.ShapeDtypeStruct((flat_rows, LANES), f32),
                jax.ShapeDtypeStruct((slices * full, docs // shares), f32),
            ),
            in_specs=[ANY_SPEC, ANY_SPEC] + [VMEM_SPEC] * 3,
            out_specs=(VMEM_SPEC, VMEM_SPEC),
            scratch_shapes=[
                pltpu.VMEM((slices, full, words), f32), pltpu.VMEM((slices, full, words), f32),
                pltpu.VMEM((ROWS, LANES), f32), pltpu.VMEM((shares, slices, full, docs // shares), f32),
                dma((slices,)), pltpu.VMEM(dense.shape, f32), dma((dense.shape[0],)),
                pltpu.VMEM((full * slices * docs // LANES, LANES), f32), pltpu.VMEM((128, docs), f32),
                pltpu.VMEM((128, docs), bf16), pltpu.VMEM((docs, 128), bf16), pltpu.VMEM((128, words), bf16),
                pltpu.VMEM((docs, SPAN * TILE_W), bf16), pltpu.VMEM((128, docs), f32), pltpu.VMEM((full, TILE_W), f32),
                pltpu.VMEM((LANES, LANES), f32), pltpu.VMEM((shares - 1, ROWS, LANES), f32),
                pltpu.VMEM((shares - 1, slices, full, docs // shares), f32),
                dma((2, shares - 1)), dma((2, shares - 1)),
            ] + chain_scratch(chips, half, tiles),
            compiler_params=pltpu.CompilerParams(
                collective_id=1, has_side_effects=True, vmem_limit_bytes=LIMIT),
            name="adjoint",
        )(topic_word, dense, interleaved(doc_weights), filter_decay, smooth_gain)
        return separated(grad, slices, topics, words), separated(own, slices, topics, docs // shares)

    return local


def solution(mesh):
    return jax.shard_map(
        make_local(mesh.shape["tm"] // 2, mesh.shape["word"]),
        mesh=mesh,
        in_specs=(
            P("tm", None, "word"),
            P("tm", None),
            P("tm", None),
            P("tm", None),
            P("tm", None, None),
            P("tm", "word"),
            P("tm", "word"),
            P("tm", "word"),
        ),
        out_specs=(P("tm", None, "word"), P("tm", None, "word")),
        check_vma=False,
    )
```

```python
import functools

import jax
import jax.numpy as jnp
from jax import lax
from jax.experimental import pallas as pl
from jax.experimental.pallas import tpu as pltpu
from jax.sharding import PartitionSpec as P

MESH = pl.DeviceIdType.MESH
ROWS = 8
LANES = 128
TILE_W = 256
TILE_D = 256
WORD_SPAN = 4096
SPARE = 136
DEEP = 4
TOGETHER = 5
SPAN = 2
ROTATE = 0
CHUNKS = 2
M_IN, A1, M_OUT, B0, B1, N_IN, C0, N_OUT, E0, E1, X0, X1, DEV_D, DEV_G, DEV_Q = range(15)


def greet(peers):
    barrier = pltpu.get_barrier_semaphore()
    for count, peer in peers:
        def hello(k, _, peer=peer):
            pl.semaphore_signal(barrier, inc=1, device_id=peer(k), device_id_type=MESH)
            return 0
        lax.fori_loop(0, count, hello, 0)
    return lambda: pl.semaphore_wait(barrier, sum(count for count, _ in peers))


def spread_coefs(rows, table, spread):
    entry = rows[A1] * rows[M_IN]
    rows = rows + [
        rows[M_OUT] * entry,
        rows[N_OUT] * rows[C0] * rows[N_IN],
        rows[N_OUT] * (rows[C0] * (rows[E1] * entry) + rows[E0] * rows[M_IN]),
    ]
    table[...] = jnp.zeros_like(table)
    for i, row in enumerate(rows):
        table[i : i + 1, 0 : row.shape[1]] = row
    spread[...] = table[...].T


def keep_rows(gain_ref, slices_all):
    slices = gain_ref.shape[0]
    at = lax.axis_index("tm") * slices
    return [
        jnp.where(at + s == slices_all - 1, 1.0, 1.0 - gain_ref[s : s + 1, :]) for s in range(slices)
    ]


def owner_maps(chips, tiles, turn):
    if chips == 16 and tiles == 13:
        def around(c, by):
            return c // 4 * 4 + lax.rem(c + by, 4)

        def tile_of(c):
            c = around(c, 4 - turn)
            return c - (c + 3) // 5

        return lambda r: around(r + (r + 3) // 4, turn), tile_of, lambda c: lax.rem(around(c, 4 - turn), 5) != 1
    return lambda r: r, lambda c: c, lambda c: c < tiles


def two_sided(chips, chip, core, half, tiles, spread, source, finish, meanwhile, meet, bufs):
    (psend, precv, mine, cbuf, rbuf, obuf, wbuf, gsend, grecv,
     pair_send, pair_recv, out_send, out_recv, back_send, back_recv, give_send, give_recv) = bufs
    first = core == 0
    width = half // CHUNKS
    partner = {"tm": 2 * chip + 1 - core}
    chip_of, my_tile, is_owner = [], [], []
    for ch in range(CHUNKS):
        to_chip, to_tile, owns = owner_maps(chips, tiles, lax.rem(ROTATE * (2 * core + ch), 4))
        chip_of.append(to_chip)
        my_tile.append(to_tile(chip))
        is_owner.append(owns(chip))
    lane = lax.broadcasted_iota(jnp.int32, (ROWS, LANES), 1)

    def rows_of(r):
        return pl.ds(pl.multiple_of(r * ROWS, ROWS), ROWS)

    def col(r, i):
        return spread[rows_of(r), i : i + 1]

    def span(ch):
        return 2 * width + (LANES if ch == 0 else 0)

    def ends(r, side, ch):
        p0 = col(r, B0) * source(0, r, side, ch)
        p1 = col(r, A1) * p0 + col(r, B1) * source(1, r, side, ch)
        q0 = col(r, C0) * (col(r, E1) * p1) + col(r, E0) * p0
        return col(r, M_OUT) * p1, col(r, N_OUT) * q0

    def swap(ch):
        return pltpu.make_async_remote_copy(
            src_ref=psend.at[ch, :, 0 : span(ch)], dst_ref=precv.at[ch, :, 0 : span(ch)],
            send_sem=pair_send.at[ch], recv_sem=pair_recv.at[ch], device_id=partner, device_id_type=MESH)

    for ch in range(CHUNKS):
        def give_ends(r, _, ch=ch):
            f, b = ends(r, 1 - core, ch)
            psend[ch, rows_of(r), 0:width] = f
            psend[ch, rows_of(r), width : 2 * width] = b
            if ch == 0:
                psend[ch, rows_of(r), 2 * width :] = spread[rows_of(r), :]
            return 0

        lax.fori_loop(0, tiles, give_ends, 0)
        if ch == 0 and meet is not None:
            meet()
        swap(ch).start()

    for ch in range(CHUNKS):
        def keep_ends(r, _, ch=ch):
            f, b = ends(r, core, ch)
            mine[ch, rows_of(r), 0:width] = f
            mine[ch, rows_of(r), width : 2 * width] = b
            return 0

        lax.fori_loop(0, tiles, keep_ends, 0)

    def scalars(r):
        def both(i):
            a = col(r, i)
            b = precv[0, rows_of(r), 2 * width + i : 2 * width + i + 1]
            return jnp.where(first, a, b), jnp.where(first, b, a)
        return both(DEV_D), both(DEV_G), both(DEV_Q)

    def ordered_pair(r, ch, lo, hi):
        a = mine[ch, rows_of(r), lo:hi]
        b = precv[ch, rows_of(r), lo:hi]
        return jnp.where(first, a, b), jnp.where(first, b, a)

    def out_copy(r, ch):
        return pltpu.make_async_remote_copy(
            src_ref=cbuf.at[ch, rows_of(r), 0 : span(ch)], dst_ref=rbuf.at[ch, chip, :, 0 : span(ch)],
            send_sem=out_send.at[ch, r], recv_sem=out_recv.at[ch, chip],
            device_id={"tm": 2 * chip_of[ch](r) + core}, device_id_type=MESH)

    for ch in range(CHUNKS):
        swap(ch).wait_recv()

        def send_chip(k, _, ch=ch):
            r = lax.rem(my_tile[ch] + 1 + k, tiles)
            (d0, d1), (g0, g1), (q0, q1) = scalars(r)
            f0, f1 = ordered_pair(r, ch, 0, width)
            b0, b1 = ordered_pair(r, ch, width, 2 * width)
            f_chip = d1 * f0 + f1
            b_chip = g0 * (b1 + q1 * f0) + b0
            cbuf[ch, rows_of(r), 0:width] = f_chip
            cbuf[ch, rows_of(r), width : 2 * width] = b_chip
            if ch == 0:
                cbuf[ch, rows_of(r), 2 * width :] = jnp.where(
                    lane == 0, d0 * d1, jnp.where(lane == 1, g0 * g1, g0 * q1 * d0 + q0))

            @pl.when(chip_of[ch](r) != chip)
            def _():
                out_copy(r, ch).start()

            return 0

        lax.fori_loop(0, tiles, send_chip, 0)

    meanwhile()

    def back_copy(c, ch):
        return pltpu.make_async_remote_copy(
            src_ref=obuf.at[ch, c], dst_ref=wbuf.at[ch, rows_of(my_tile[ch])],
            send_sem=back_send.at[ch, c], recv_sem=back_recv.at[ch, my_tile[ch]],
            device_id={"tm": 2 * c + core}, device_id_type=MESH)

    for ch in range(CHUNKS):
        @pl.when(is_owner[ch])
        def _(ch=ch):
            rbuf[ch, chip, :, 0 : span(ch)] = cbuf[ch, rows_of(my_tile[ch]), 0 : span(ch)]

            def arrive(k, _, ch=ch):
                src = lax.rem(chip + k, chips)
                pltpu.make_async_remote_copy(
                    src_ref=cbuf.at[ch, 0:ROWS, 0 : span(ch)], dst_ref=rbuf.at[ch, src, :, 0 : span(ch)],
                    send_sem=out_send.at[ch, 0], recv_sem=out_recv.at[ch, src],
                    device_id={"tm": 2 * src + core}, device_id_type=MESH).wait_recv()
                return 0

            lax.fori_loop(1, chips, arrive, 0)

            def scalar(c, i):
                return rbuf[0, c, :, 2 * width + i : 2 * width + i + 1]

            def onward(c, f, ch=ch):
                obuf[ch, c, :, 0:width] = f
                return scalar(c, 0) * f + rbuf[ch, c, :, 0:width]

            lax.fori_loop(0, chips, onward, jnp.zeros((ROWS, width), jnp.float32))

            def homeward(k, s, ch=ch):
                c = chips - 1 - k
                f = obuf[ch, c, :, 0:width]
                obuf[ch, c, :, width : 2 * width] = s

                return scalar(c, 1) * s + rbuf[ch, c, :, width : 2 * width] + scalar(c, 2) * f

            lax.fori_loop(0, chips, homeward, jnp.zeros((ROWS, width), jnp.float32))

            def send_back(k, _, ch=ch):
                back_copy(lax.rem(chip + k, chips), ch).start()
                return 0

            lax.fori_loop(1, chips, send_back, 0)
            wbuf[ch, rows_of(my_tile[ch]), :] = obuf[ch, chip]

    def give_copy(r, ch):
        return pltpu.make_async_remote_copy(
            src_ref=gsend.at[ch, rows_of(r)], dst_ref=grecv.at[ch, rows_of(r)], send_sem=give_send.at[ch, r],
            recv_sem=give_recv.at[ch, r], device_id=partner, device_id_type=MESH)

    def resolve(r, side, ch, f, s):
        p0 = col(r, M_IN) * f + col(r, B0) * source(0, r, side, ch)
        p1 = col(r, A1) * p0 + col(r, B1) * source(1, r, side, ch)
        q1 = col(r, N_IN) * s + col(r, E1) * p1
        finish(1, r, side, ch, q1)
        finish(0, r, side, ch, col(r, C0) * q1 + col(r, E0) * p0)

    def turn(k, ch):
        return lax.rem(my_tile[ch] + tiles - k, tiles)

    for ch in range(CHUNKS):
        def own_half(k, _, ch=ch):
            r = turn(k, ch)

            @pl.when(chip_of[ch](r) != chip)
            def _():
                pltpu.make_async_remote_copy(
                    src_ref=obuf.at[ch, 0], dst_ref=wbuf.at[ch, rows_of(r)], send_sem=back_send.at[ch, 0],
                    recv_sem=back_recv.at[ch, r], device_id=partner, device_id_type=MESH).wait_recv()

            (d0, _), (_, g1), (_, q1) = scalars(r)
            f = wbuf[ch, rows_of(r), 0:width]
            s = wbuf[ch, rows_of(r), width : 2 * width]
            f_mid = d0 * f + ordered_pair(r, ch, 0, width)[0]
            s_mid = g1 * s + ordered_pair(r, ch, width, 2 * width)[1] + q1 * f_mid
            gsend[ch, rows_of(r), 0:width] = jnp.where(first, f_mid, f)
            gsend[ch, rows_of(r), width : 2 * width] = jnp.where(first, s, s_mid)
            give_copy(r, ch).start()
            wbuf[ch, rows_of(r), 0:width] = jnp.where(first, f, f_mid)
            wbuf[ch, rows_of(r), width : 2 * width] = jnp.where(first, s_mid, s)
            return 0

        lax.fori_loop(0, tiles, own_half, 0)

        def settle(r, _, ch=ch):
            resolve(r, core, ch, wbuf[ch, rows_of(r), 0:width], wbuf[ch, rows_of(r), width : 2 * width])
            return 0

        lax.fori_loop(0, tiles, settle, 0)

        def other_half(k, _, ch=ch):
            r = turn(k, ch)
            give_copy(r, ch).wait_recv()
            resolve(r, 1 - core, ch, grecv[ch, rows_of(r), 0:width], grecv[ch, rows_of(r), width : 2 * width])
            return 0

        lax.fori_loop(0, tiles, other_half, 0)

    for ch in range(CHUNKS):
        swap(ch).wait_send()

        def drain(r, _, ch=ch):
            give_copy(r, ch).wait_send()

            @pl.when(chip_of[ch](r) != chip)
            def _():
                out_copy(r, ch).wait_send()

            return 0

        lax.fori_loop(0, tiles, drain, 0)

        @pl.when(is_owner[ch])
        def _(ch=ch):
            def drain_back(k, _):
                back_copy(lax.rem(chip + k, chips), ch).wait_send()
                return 0

            lax.fori_loop(1, chips, drain_back, 0)


def chain_peers(chips, chip, core):
    return [
        (chips - 1, lambda k: {"tm": 2 * lax.rem(chip + 1 + k, chips) + core}),
        (1, lambda k: {"tm": 2 * chip + 1 - core}),
    ]


def chain_scratch(chips, half, tiles):
    width, full = half // CHUNKS, tiles * ROWS
    wide = 2 * width + LANES
    f32 = jnp.float32
    dma = pltpu.SemaphoreType.DMA
    return [
        pltpu.VMEM((LANES, LANES), f32), pltpu.VMEM((LANES, LANES), f32),
        pltpu.VMEM((CHUNKS, full, wide), f32), pltpu.VMEM((CHUNKS, full, wide), f32),
        pltpu.VMEM((CHUNKS, full, 2 * width), f32),
        pltpu.VMEM((CHUNKS, full, wide), f32), pltpu.VMEM((CHUNKS, chips, ROWS, wide), f32),
        pltpu.VMEM((CHUNKS, chips, ROWS, 2 * width), f32), pltpu.VMEM((CHUNKS, full, 2 * width), f32),
        pltpu.VMEM((CHUNKS, full, 2 * width), f32), pltpu.VMEM((CHUNKS, full, 2 * width), f32),
        dma((CHUNKS,)), dma((CHUNKS,)), dma((CHUNKS, tiles)), dma((CHUNKS, chips)), dma((CHUNKS, chips)),
        dma((CHUNKS, tiles)), dma((CHUNKS, tiles)), dma((CHUNKS, tiles)),
    ]


def lanes_of(side, ch, half):
    width = half // CHUNKS
    return pl.ds(pl.multiple_of(side * half + ch * width, LANES), width)


def smooth_kernel(chips, x_hbm, decay_ref, gain_ref, norm_ref, doc_ref, word_ref, count_ref,
                  tw_ref, order_ref, edge_ref, raw, xs, load_sem, flat, table, spread, *bufs):
    core, chip = lax.rem(lax.axis_index("tm"), 2), lax.axis_index("tm") // 2
    slices, full, words = xs.shape
    half, tiles, blocks = words // 2, full // ROWS, words // LANES
    pitch = slices * blocks
    meet = greet(chain_peers(chips, chip, core))
    load = pltpu.make_async_copy(x_hbm, raw.at[0 : x_hbm.shape[0]], load_sem.at[0])
    load.start()
    decay = [decay_ref[s : s + 1, :] for s in range(2)]
    gain = [gain_ref[s : s + 1, :] for s in range(2)]
    norm = [norm_ref[s : s + 1, :] for s in range(2)]
    keep = keep_rows(gain_ref, slices * 2 * chips)
    one = jnp.ones_like(decay[0])
    spread_coefs(
        [decay[0], decay[1], one, 1.0 - decay[0], 1.0 - decay[1], gain[1], gain[0], one,
         keep[0], keep[1], norm[0], norm[1]], table, spread)
    if x_hbm.shape[0] < raw.shape[0]:
        raw[x_hbm.shape[0] :, :] = jnp.zeros((raw.shape[0] - x_hbm.shape[0], LANES), jnp.float32)
    load.wait()

    def move(r, _):
        rows = pl.ds(pl.multiple_of(r * ROWS, ROWS), ROWS)
        for s in range(slices):
            for i in range(blocks):
                xs[s, rows, i * LANES : (i + 1) * LANES] = raw[
                    pl.ds(r * (ROWS * pitch) + i * slices + s, ROWS, stride=pitch), :]
        return 0

    lax.fori_loop(0, tiles, move, 0)

    def source(s, r, side, ch):
        return xs[s, pl.ds(pl.multiple_of(r * ROWS, ROWS), ROWS), lanes_of(side, ch, half)]

    def finish(s, r, side, ch, q):
        rows = pl.ds(pl.multiple_of(r * ROWS, ROWS), ROWS)
        tw_ref[s, rows, lanes_of(side, ch, half)] = jnp.exp(q - spread[rows, X0 + s : X0 + s + 1])

    def order():
        word = word_ref[...] - lax.axis_index("word") * words
        doc = doc_ref[...]
        keys = (((doc >> 8) * WORD_SPAN + word) << 12) | ((doc & 255) << 4) | count_ref[...]
        keys = sort_entries(keys)
        edge_ref[0:8, :] = keys[0:8]
        edge_ref[8:16, :] = keys[-8:]
        flat[...] = keys
        for s in range(slices):
            order_ref[s, 0:128, :] = flat[pl.ds(s, 128, stride=slices), :].T
            order_ref[s, 128:, :] = jnp.full((SPARE - 128, 128), -1, jnp.int32)

    two_sided(chips, chip, core, half, tiles, spread, source, finish, order, meet, bufs)


def adjoint_kernel(chips, shares, t_hbm, dense_hbm, w_ref, decay_ref, gain_ref, out_ref, own_ref,
                   es, ts, tot_ref, sums_ref, load_sem, dense, dense_sem, wraw, w32, wb, wt, tr, ratio, sums, tots,
                   totals, tot_in, sums_in, tot_sem, sum_sem, table, spread, *bufs):
    core, chip = lax.rem(lax.axis_index("tm"), 2), lax.axis_index("tm") // 2
    share = lax.axis_index("word")
    slices, full, words = es.shape
    half, tiles, blocks = words // 2, full // ROWS, words // LANES
    pitch = slices * blocks
    neighbour = lambda k: {"word": lax.rem(share + 1 + k, shares)}
    meet = greet(chain_peers(chips, chip, core) + [(shares - 1, neighbour)])
    expect(t_hbm, dense_hbm, w_ref, es, ts, tot_ref, sums_ref, load_sem, dense, dense_sem,
           wraw, w32, wb, wt, tr, ratio, sums, tots, table)
    decay = [decay_ref[s : s + 1, :] for s in range(2)]
    gain = [gain_ref[s : s + 1, :] for s in range(2)]
    keep = keep_rows(gain_ref, slices * 2 * chips)
    one = jnp.ones_like(decay[0])
    spread_coefs(
        [one, gain[0], gain[1], one, one, one, decay[1], decay[0],
         keep[0], keep[1], 1.0 - decay[0], 1.0 - decay[1]], table, spread)
    meet()

    def tot_copy(k):
        return pltpu.make_async_remote_copy(
            src_ref=tot_ref, dst_ref=tot_in.at[shares - 2 - k], send_sem=tot_sem.at[0, k],
            recv_sem=tot_sem.at[1, shares - 2 - k], device_id=neighbour(k), device_id_type=MESH)

    def sum_copy(k):
        return pltpu.make_async_remote_copy(
            src_ref=sums_ref.at[lax.rem(share + 1 + k, shares)], dst_ref=sums_in.at[shares - 2 - k],
            send_sem=sum_sem.at[0, k], recv_sem=sum_sem.at[1, shares - 2 - k],
            device_id=neighbour(k), device_id_type=MESH)

    for k in range(shares - 1):
        tot_copy(k).start()
    total = tot_ref[...]
    for k in range(shares - 1):
        tot_copy(shares - 2 - k).wait_recv()
        total = total + tot_in[k]
    table[...] = jnp.zeros_like(table)
    table[0:ROWS, :] = total
    totals[...] = table[...].T

    def source(s, r, side, ch):
        rows, lanes = pl.ds(pl.multiple_of(r * ROWS, ROWS), ROWS), lanes_of(side, ch, half)
        return es[s, rows, lanes] - totals[rows, s : s + 1] * ts[s, rows, lanes]

    def finish(s, r, side, ch, q):
        rows = pl.ds(pl.multiple_of(r * ROWS, ROWS), ROWS)
        grad = spread[rows, X0 + s : X0 + s + 1] * q
        width = half // CHUNKS
        at = r * (ROWS * pitch) + (side * half + ch * width) // LANES * slices + s
        for i in range(width // LANES):
            out_ref[pl.ds(at + i * slices, ROWS, stride=pitch), :] = grad[:, i * LANES : (i + 1) * LANES]

    def gather_sums():
        for k in range(shares - 1):
            sum_copy(k).start()

    def take_sums():
        for s in range(slices):
            sums = sums_ref[share, s]
            for k in range(shares - 1):
                if s == 0:
                    sum_copy(shares - 2 - k).wait_recv()
                sums = sums + sums_in[k, s]
            own_ref[pl.ds(s, full, stride=slices), :] = sums

    two_sided(chips, chip, core, half, tiles, spread, source, finish, gather_sums, None, bufs)
    take_sums()
    for k in range(shares - 1):
        tot_copy(k).wait_send()
        sum_copy(k).wait_send()


def sort_entries(x):
    shape = (x.shape[0] // 8, 8, 128)
    x = x.reshape(shape)
    high = shape[0].bit_length() - 1
    depth = high + 2 + 7
    sub = lax.broadcasted_iota(jnp.int32, (8, 128), 0)
    lane = lax.broadcasted_iota(jnp.int32, (8, 128), 1)

    def bit_of(j):
        return (sub >> (j - high + 1)) & 1 if j < high + 2 else (lane >> (j - high - 2)) & 1

    def parts(x, j):
        pieces = x.reshape((shape[0] >> (j + 1), 2, 1 << j, 8, 128))
        return pieces[:, 0], pieces[:, 1]

    def joined(a, b):
        return jnp.stack([a, b], axis=1).reshape(shape)

    def flip(x, k):
        if k >= depth:
            return x
        if k >= high:
            return x ^ (-bit_of(k))[None]
        a, b = parts(x, k)
        return joined(a, ~b)

    def exchange(x, j):
        if j < high:
            a, b = parts(x, j)
            return joined(jnp.minimum(a, b), jnp.maximum(a, b))
        low = (bit_of(j) == 0)[None]
        if j < high + 2:
            step, size = 1 << (j - high + 1), 8
            y = x
        else:
            step, size = 1 << (j - high - 2), 128
            y = x.reshape((shape[0] * 8, 128))
        partner = ahead = pltpu.roll(y, size - step, 1).reshape(shape)
        if 2 * step != size:
            partner = jnp.where(low, ahead, pltpu.roll(y, step, 1).reshape(shape))
        return jnp.where(low, jnp.minimum(x, partner), jnp.maximum(x, partner))

    for k in range(1, depth + 1):
        x = flip(x, k)
        for j in range(k - 1, -1, -1):
            x = exchange(x, j)
        x = flip(x, k)
    return x.reshape((shape[0] * 8, 128))


def count_kernel(words, order_ref, edge_ref, dense_hbm, bounds, place, acc, save_sem):
    slices = order_ref.shape[0]
    tiles, blocks = words // TILE_W, acc.shape[1] // TILE_D
    together = acc.shape[0] // 2
    for s in range(slices):
        least, most = edge_ref[s : s + 1, :], edge_ref[16 - slices + s : 17 - slices + s, :]
        for h in range(blocks):
            for j in range(tiles):
                low = (h * WORD_SPAN + j * TILE_W) << 12
                bounds[s * tiles + j, h, 0] = jnp.sum((most < low).astype(jnp.int32))
                bounds[s * tiles + j, h, 1] = jnp.sum((least < low + (TILE_W << 12)).astype(jnp.int32))
    place[...] = lax.broadcasted_iota(jnp.int32, place.shape, 0).astype(jnp.float32).astype(jnp.bfloat16)

    def save(t, slot):
        return pltpu.make_async_copy(
            acc.at[pl.ds(slot * together, together)], dense_hbm.at[pl.ds(t * together, together)], save_sem.at[slot])

    def step(t, _):
        slot = lax.rem(t, 2)
        s = lax.div(t * together, tiles)

        @pl.when(t >= 2)
        def _():
            save(t - 2, slot).wait()

        acc[pl.ds(slot * together, together)] = jnp.zeros((together,) + acc.shape[1:], jnp.float32)
        groups = [(n, h) for n in range(together) for h in range(blocks)]
        starts = [bounds[t * together + n, h, 0] for n, h in groups]
        longest = starts[0] * 0
        for start, (n, h) in zip(starts, groups):
            longest = jnp.maximum(longest, (bounds[t * together + n, h, 1] - start + DEEP - 1) // DEEP)

        def batch(i, _):
            for start, (n, h) in zip(starts, groups):
                base = h * WORD_SPAN + (t * together + n - s * tiles) * TILE_W
                at = jnp.minimum(start + DEEP * i, SPARE - DEEP)
                key = jnp.concatenate([order_ref[s, pl.ds(at + m, 1), :] for m in range(DEEP)], axis=1)
                word = ((key >> 12) - base).astype(jnp.float32).astype(jnp.bfloat16)
                doc = ((key >> 4) & 255).astype(jnp.float32).astype(jnp.bfloat16)
                count = (key & 15).astype(jnp.float32).astype(jnp.bfloat16)
                docs_hot = jnp.where(place[...] == doc, count, jnp.bfloat16(0))
                words_hot = jnp.where(place[...] == word, jnp.bfloat16(1), jnp.bfloat16(0))
                acc[slot * together + n, h * TILE_D : (h + 1) * TILE_D, :] += lax.dot_general(
                    docs_hot, words_hot, (((1,), (1,)), ((), ())), preferred_element_type=jnp.float32)
            return 0

        lax.fori_loop(0, longest, batch, 0)
        save(t, slot).start()
        return 0

    steps = slices * tiles // together
    lax.fori_loop(0, steps, step, 0)
    for t in (steps - 2, steps - 1):
        save(t, t % 2).wait()


def fill_slice(s, wraw, w32, wb, wt):
    slices, pieces = 2, w32.shape[1] // LANES
    full = wraw.shape[0] // (slices * pieces)
    for i in range(pieces):
        w32[0:full, i * LANES : (i + 1) * LANES] = wraw[pl.ds(i * slices + s, full, stride=slices * pieces), :]
    wb[...] = w32[...].astype(jnp.bfloat16)
    wt[...] = w32[...].T.astype(jnp.bfloat16)


def expect(t_hbm, dense_hbm, w_ref, es, ts, tot, sums_out, load_sem, dense, dense_sem,
           wraw, w32, wb, wt, tr, ratio, sums, tots, turned):
    slices, full, words = ts.shape
    shares, docs = sums_out.shape[0], w32.shape[1]
    tiles, blocks = words // TILE_W, docs // TILE_D

    def load(s):
        return pltpu.make_async_copy(t_hbm.at[s], ts.at[s], load_sem.at[s])

    def fetch(t):
        return pltpu.make_async_copy(dense_hbm.at[t], dense.at[t], dense_sem.at[t])

    for s in range(slices):
        load(s).start()

        def ask(j, _, s=s):
            fetch(s * tiles + j).start()
            return 0

        lax.fori_loop(0, tiles, ask, 0)
    wraw[w_ref.shape[0] :, :] = jnp.zeros((wraw.shape[0] - w_ref.shape[0], LANES), jnp.float32)
    wraw[0 : w_ref.shape[0], :] = w_ref[...].astype(jnp.float32)
    w32[...] = jnp.zeros_like(w32)
    tr[full // 16 * 16 :, :] = jnp.zeros((128 - full // 16 * 16, words), jnp.bfloat16)
    lane = lax.broadcasted_iota(jnp.int32, (full, LANES), 1)
    turned[...] = jnp.zeros_like(turned)

    for s in range(slices):
        fill_slice(s, wraw, w32, wb, wt)
        load(s).wait()
        tr[0:full, :] = ts[s].astype(jnp.bfloat16)
        sums[...] = jnp.zeros_like(sums)
        tots[...] = jnp.zeros_like(tots)

        def one_tile(j, _, s=s):
            lanes = pl.ds(pl.multiple_of(j * SPAN * TILE_W, TILE_W), SPAN * TILE_W)
            topic = tr[:, lanes]
            for n in range(SPAN):
                t = s * tiles + j * SPAN + n
                part = slice(n * TILE_W, (n + 1) * TILE_W)
                fetch(t).wait()
                for h in range(blocks):
                    rows = slice(h * TILE_D, (h + 1) * TILE_D)
                    mixture = jnp.dot(wt[rows, :], topic[:, part], preferred_element_type=jnp.float32)
                    ratio[rows, part] = (dense[t, rows, :] / mixture).astype(jnp.bfloat16)
            sums[...] += lax.dot_general(
                topic, ratio[...], (((1,), (1,)), ((), ())), preferred_element_type=jnp.float32)
            weighted = jnp.dot(wb[...], ratio[...], preferred_element_type=jnp.float32)
            expected = topic[0:full].astype(jnp.float32) * weighted[0:full]
            es[s, :, lanes] = expected
            for n in range(SPAN):
                tots[...] += expected[:, n * TILE_W : (n + 1) * TILE_W]
            return 0

        lax.fori_loop(0, tiles // SPAN, one_tile, 0)
        for y in range(shares):
            own = slice(y * (docs // shares), (y + 1) * (docs // shares))
            sums_out[y, s] = sums[0:full, own] * w32[0:full, own]
        turned[0:full, :] = jnp.where(lane == s, jnp.sum(tots[...], axis=1, keepdims=True), turned[0:full, :])
    tot[...] = turned[...].T[0:ROWS, :]


VMEM_SPEC = pl.BlockSpec(memory_space=pltpu.VMEM)
ANY_SPEC = pl.BlockSpec(memory_space=pl.ANY)
LIMIT = 60 * 1024 * 1024


def count_entries(order, edges, words, docs):
    slices = order.shape[0]
    tiles = words // TILE_W
    return pl.pallas_call(
        functools.partial(count_kernel, words),
        out_shape=jax.ShapeDtypeStruct((slices * tiles, docs, TILE_W), jnp.float32),
        in_specs=[VMEM_SPEC] * 2,
        out_specs=ANY_SPEC,
        scratch_shapes=[
            pltpu.SMEM((slices * tiles, docs // TILE_D, 2), jnp.int32),
            pltpu.VMEM((TILE_W, DEEP * 128), jnp.bfloat16),
            pltpu.VMEM((2 * TOGETHER, docs, TILE_W), jnp.float32),
            pltpu.SemaphoreType.DMA((2,)),
        ],
        compiler_params=pltpu.CompilerParams(vmem_limit_bytes=LIMIT),
        name="count",
    )(order, edges)


def interleaved(x):
    slices, rows, columns = x.shape
    group = 4 if columns % (4 * LANES) == 0 else 1
    x = x.transpose((1, 0, 2)).reshape((rows, slices, columns // LANES // group, group, LANES))
    x = x.transpose((0, 2, 3, 1, 4))
    return x.reshape((rows * columns // LANES * slices, LANES))


def separated(x, slices, rows, columns):
    x = x[: rows * columns // LANES * slices].reshape((rows, columns // LANES, slices, LANES))
    return x.transpose((0, 2, 1, 3)).reshape((rows, slices, columns)).transpose((1, 0, 2))


def make_local(chips, shares):
    def local(pseudo_obs, filter_decay, smooth_gain, log_norm, doc_weights, doc_ids, word_ids, counts):
        slices, topics, words = pseudo_obs.shape
        tiles, half = -(-topics // ROWS), words // 2
        full = tiles * ROWS
        docs = doc_weights.shape[2]
        entries = doc_ids.shape[1]
        f32, bf16 = jnp.float32, jnp.bfloat16
        dma = pltpu.SemaphoreType.DMA
        flat_rows = full * slices * words // LANES
        ids = [interleaved(a[:, None, :]) for a in (doc_ids, word_ids, counts)]
        topic_word, order, edges = pl.pallas_call(
            functools.partial(smooth_kernel, chips),
            out_shape=(
                jax.ShapeDtypeStruct((slices, full, words), f32),
                jax.ShapeDtypeStruct((slices, SPARE, LANES), jnp.int32),
                jax.ShapeDtypeStruct((16, LANES), jnp.int32),
            ),
            in_specs=[ANY_SPEC] + [VMEM_SPEC] * 6,
            out_specs=(VMEM_SPEC,) * 3,
            scratch_shapes=[
                pltpu.VMEM((flat_rows, LANES), f32), pltpu.VMEM((slices, full, words), f32), dma((1,)),
                pltpu.VMEM((slices * entries // LANES, LANES), jnp.int32),
            ] + chain_scratch(chips, half, tiles),
            compiler_params=pltpu.CompilerParams(
                collective_id=0, has_side_effects=True, vmem_limit_bytes=LIMIT),
            name="smooth",
        )(interleaved(pseudo_obs), filter_decay, smooth_gain, log_norm, *ids)
        dense = count_entries(order, edges, words, docs)
        grad, own = pl.pallas_call(
            functools.partial(adjoint_kernel, chips, shares),
            out_shape=(
                jax.ShapeDtypeStruct((flat_rows, LANES), f32),
                jax.ShapeDtypeStruct((slices * full, docs // shares), f32),
            ),
            in_specs=[ANY_SPEC, ANY_SPEC] + [VMEM_SPEC] * 3,
            out_specs=(VMEM_SPEC, VMEM_SPEC),
            scratch_shapes=[
                pltpu.VMEM((slices, full, words), f32), pltpu.VMEM((slices, full, words), f32),
                pltpu.VMEM((ROWS, LANES), f32), pltpu.VMEM((shares, slices, full, docs // shares), f32),
                dma((slices,)), pltpu.VMEM(dense.shape, f32), dma((dense.shape[0],)),
                pltpu.VMEM((full * slices * docs // LANES, LANES), f32), pltpu.VMEM((128, docs), f32),
                pltpu.VMEM((128, docs), bf16), pltpu.VMEM((docs, 128), bf16), pltpu.VMEM((128, words), bf16),
                pltpu.VMEM((docs, SPAN * TILE_W), bf16), pltpu.VMEM((128, docs), f32), pltpu.VMEM((full, TILE_W), f32),
                pltpu.VMEM((LANES, LANES), f32), pltpu.VMEM((shares - 1, ROWS, LANES), f32),
                pltpu.VMEM((shares - 1, slices, full, docs // shares), f32),
                dma((2, shares - 1)), dma((2, shares - 1)),
            ] + chain_scratch(chips, half, tiles),
            compiler_params=pltpu.CompilerParams(
                collective_id=1, has_side_effects=True, vmem_limit_bytes=LIMIT),
            name="adjoint",
        )(topic_word, dense, interleaved(doc_weights), filter_decay, smooth_gain)
        return separated(grad, slices, topics, words), separated(own, slices, topics, docs // shares)

    return local


def solution(mesh):
    return jax.shard_map(
        make_local(mesh.shape["tm"] // 2, mesh.shape["word"]),
        mesh=mesh,
        in_specs=(
            P("tm", None, "word"),
            P("tm", None),
            P("tm", None),
            P("tm", None),
            P("tm", None, None),
            P("tm", "word"),
            P("tm", "word"),
            P("tm", "word"),
        ),
        out_specs=(P("tm", None, "word"), P("tm", None, "word")),
        check_vma=False,
    )
```

```python
import functools

import jax
import jax.numpy as jnp
from jax import lax
from jax.experimental import pallas as pl
from jax.experimental.pallas import tpu as pltpu
from jax.sharding import PartitionSpec as P

MESH = pl.DeviceIdType.MESH
ROWS = 8
LANES = 128
TILE_W = 256
TILE_D = 256
WORD_SPAN = 4096
SPARE = 136
DEEP = 8
TOGETHER = 5
SPAN = 2
ROTATE = 0
CHUNKS = 2
M_IN, A1, M_OUT, B0, B1, N_IN, C0, N_OUT, E0, E1, X0, X1, DEV_D, DEV_G, DEV_Q = range(15)


def greet(peers):
    barrier = pltpu.get_barrier_semaphore()
    for count, peer in peers:
        def hello(k, _, peer=peer):
            pl.semaphore_signal(barrier, inc=1, device_id=peer(k), device_id_type=MESH)
            return 0
        lax.fori_loop(0, count, hello, 0)
    return lambda: pl.semaphore_wait(barrier, sum(count for count, _ in peers))


def spread_coefs(rows, table, spread):
    entry = rows[A1] * rows[M_IN]
    rows = rows + [
        rows[M_OUT] * entry,
        rows[N_OUT] * rows[C0] * rows[N_IN],
        rows[N_OUT] * (rows[C0] * (rows[E1] * entry) + rows[E0] * rows[M_IN]),
    ]
    table[...] = jnp.zeros_like(table)
    for i, row in enumerate(rows):
        table[i : i + 1, 0 : row.shape[1]] = row
    spread[...] = table[...].T


def keep_rows(gain_ref, slices_all):
    slices = gain_ref.shape[0]
    at = lax.axis_index("tm") * slices
    return [
        jnp.where(at + s == slices_all - 1, 1.0, 1.0 - gain_ref[s : s + 1, :]) for s in range(slices)
    ]


def owner_maps(chips, tiles, turn):
    if chips == 16 and tiles == 13:
        def around(c, by):
            return c // 4 * 4 + lax.rem(c + by, 4)

        def tile_of(c):
            c = around(c, 4 - turn)
            return c - (c + 3) // 5

        return lambda r: around(r + (r + 3) // 4, turn), tile_of, lambda c: lax.rem(around(c, 4 - turn), 5) != 1
    return lambda r: r, lambda c: c, lambda c: c < tiles


def two_sided(chips, chip, core, half, tiles, spread, source, finish, meanwhile, meet, bufs):
    (psend, precv, mine, cbuf, rbuf, obuf, wbuf, gsend, grecv,
     pair_send, pair_recv, out_send, out_recv, back_send, back_recv, give_send, give_recv) = bufs
    first = core == 0
    width = half // CHUNKS
    partner = {"tm": 2 * chip + 1 - core}
    chip_of, my_tile, is_owner = [], [], []
    for ch in range(CHUNKS):
        to_chip, to_tile, owns = owner_maps(chips, tiles, lax.rem(ROTATE * (2 * core + ch), 4))
        chip_of.append(to_chip)
        my_tile.append(to_tile(chip))
        is_owner.append(owns(chip))
    lane = lax.broadcasted_iota(jnp.int32, (ROWS, LANES), 1)

    def rows_of(r):
        return pl.ds(pl.multiple_of(r * ROWS, ROWS), ROWS)

    def col(r, i):
        return spread[rows_of(r), i : i + 1]

    def span(ch):
        return 2 * width + (LANES if ch == 0 else 0)

    def ends(r, side, ch):
        p0 = col(r, B0) * source(0, r, side, ch)
        p1 = col(r, A1) * p0 + col(r, B1) * source(1, r, side, ch)
        q0 = col(r, C0) * (col(r, E1) * p1) + col(r, E0) * p0
        return col(r, M_OUT) * p1, col(r, N_OUT) * q0

    def swap(ch):
        return pltpu.make_async_remote_copy(
            src_ref=psend.at[ch, :, 0 : span(ch)], dst_ref=precv.at[ch, :, 0 : span(ch)],
            send_sem=pair_send.at[ch], recv_sem=pair_recv.at[ch], device_id=partner, device_id_type=MESH)

    for ch in range(CHUNKS):
        def give_ends(r, _, ch=ch):
            f, b = ends(r, 1 - core, ch)
            psend[ch, rows_of(r), 0:width] = f
            psend[ch, rows_of(r), width : 2 * width] = b
            if ch == 0:
                psend[ch, rows_of(r), 2 * width :] = spread[rows_of(r), :]
            return 0

        lax.fori_loop(0, tiles, give_ends, 0)
        if ch == 0 and meet is not None:
            meet()
        swap(ch).start()

    for ch in range(CHUNKS):
        def keep_ends(r, _, ch=ch):
            f, b = ends(r, core, ch)
            mine[ch, rows_of(r), 0:width] = f
            mine[ch, rows_of(r), width : 2 * width] = b
            return 0

        lax.fori_loop(0, tiles, keep_ends, 0)

    def scalars(r):
        def both(i):
            a = col(r, i)
            b = precv[0, rows_of(r), 2 * width + i : 2 * width + i + 1]
            return jnp.where(first, a, b), jnp.where(first, b, a)
        return both(DEV_D), both(DEV_G), both(DEV_Q)

    def ordered_pair(r, ch, lo, hi):
        a = mine[ch, rows_of(r), lo:hi]
        b = precv[ch, rows_of(r), lo:hi]
        return jnp.where(first, a, b), jnp.where(first, b, a)

    def out_copy(r, ch):
        return pltpu.make_async_remote_copy(
            src_ref=cbuf.at[ch, rows_of(r), 0 : span(ch)], dst_ref=rbuf.at[ch, chip, :, 0 : span(ch)],
            send_sem=out_send.at[ch, r], recv_sem=out_recv.at[ch, chip],
            device_id={"tm": 2 * chip_of[ch](r) + core}, device_id_type=MESH)

    for ch in range(CHUNKS):
        swap(ch).wait_recv()

        def send_chip(k, _, ch=ch):
            r = lax.rem(my_tile[ch] + 1 + k, tiles)
            (d0, d1), (g0, g1), (q0, q1) = scalars(r)
            f0, f1 = ordered_pair(r, ch, 0, width)
            b0, b1 = ordered_pair(r, ch, width, 2 * width)
            f_chip = d1 * f0 + f1
            b_chip = g0 * (b1 + q1 * f0) + b0
            cbuf[ch, rows_of(r), 0:width] = f_chip
            cbuf[ch, rows_of(r), width : 2 * width] = b_chip
            if ch == 0:
                cbuf[ch, rows_of(r), 2 * width :] = jnp.where(
                    lane == 0, d0 * d1, jnp.where(lane == 1, g0 * g1, g0 * q1 * d0 + q0))

            @pl.when(chip_of[ch](r) != chip)
            def _():
                out_copy(r, ch).start()

            return 0

        lax.fori_loop(0, tiles, send_chip, 0)

    meanwhile()

    def back_copy(c, ch):
        return pltpu.make_async_remote_copy(
            src_ref=obuf.at[ch, c], dst_ref=wbuf.at[ch, rows_of(my_tile[ch])],
            send_sem=back_send.at[ch, c], recv_sem=back_recv.at[ch, my_tile[ch]],
            device_id={"tm": 2 * c + core}, device_id_type=MESH)

    for ch in range(CHUNKS):
        @pl.when(is_owner[ch])
        def _(ch=ch):
            rbuf[ch, chip, :, 0 : span(ch)] = cbuf[ch, rows_of(my_tile[ch]), 0 : span(ch)]

            def arrive(k, _, ch=ch):
                src = lax.rem(chip + k, chips)
                pltpu.make_async_remote_copy(
                    src_ref=cbuf.at[ch, 0:ROWS, 0 : span(ch)], dst_ref=rbuf.at[ch, src, :, 0 : span(ch)],
                    send_sem=out_send.at[ch, 0], recv_sem=out_recv.at[ch, src],
                    device_id={"tm": 2 * src + core}, device_id_type=MESH).wait_recv()
                return 0

            lax.fori_loop(1, chips, arrive, 0)

            def scalar(c, i):
                return rbuf[0, c, :, 2 * width + i : 2 * width + i + 1]

            def onward(c, f, ch=ch):
                obuf[ch, c, :, 0:width] = f
                return scalar(c, 0) * f + rbuf[ch, c, :, 0:width]

            lax.fori_loop(0, chips, onward, jnp.zeros((ROWS, width), jnp.float32))

            def homeward(k, s, ch=ch):
                c = chips - 1 - k
                f = obuf[ch, c, :, 0:width]
                obuf[ch, c, :, width : 2 * width] = s

                return scalar(c, 1) * s + rbuf[ch, c, :, width : 2 * width] + scalar(c, 2) * f

            lax.fori_loop(0, chips, homeward, jnp.zeros((ROWS, width), jnp.float32))

            def send_back(k, _, ch=ch):
                back_copy(lax.rem(chip + k, chips), ch).start()
                return 0

            lax.fori_loop(1, chips, send_back, 0)
            wbuf[ch, rows_of(my_tile[ch]), :] = obuf[ch, chip]

    def give_copy(r, ch):
        return pltpu.make_async_remote_copy(
            src_ref=gsend.at[ch, rows_of(r)], dst_ref=grecv.at[ch, rows_of(r)], send_sem=give_send.at[ch, r],
            recv_sem=give_recv.at[ch, r], device_id=partner, device_id_type=MESH)

    def resolve(r, side, ch, f, s):
        p0 = col(r, M_IN) * f + col(r, B0) * source(0, r, side, ch)
        p1 = col(r, A1) * p0 + col(r, B1) * source(1, r, side, ch)
        q1 = col(r, N_IN) * s + col(r, E1) * p1
        finish(1, r, side, ch, q1)
        finish(0, r, side, ch, col(r, C0) * q1 + col(r, E0) * p0)

    def turn(k, ch):
        return lax.rem(my_tile[ch] + tiles - k, tiles)

    for ch in range(CHUNKS):
        def own_half(k, _, ch=ch):
            r = turn(k, ch)

            @pl.when(chip_of[ch](r) != chip)
            def _():
                pltpu.make_async_remote_copy(
                    src_ref=obuf.at[ch, 0], dst_ref=wbuf.at[ch, rows_of(r)], send_sem=back_send.at[ch, 0],
                    recv_sem=back_recv.at[ch, r], device_id=partner, device_id_type=MESH).wait_recv()

            (d0, _), (_, g1), (_, q1) = scalars(r)
            f = wbuf[ch, rows_of(r), 0:width]
            s = wbuf[ch, rows_of(r), width : 2 * width]
            f_mid = d0 * f + ordered_pair(r, ch, 0, width)[0]
            s_mid = g1 * s + ordered_pair(r, ch, width, 2 * width)[1] + q1 * f_mid
            gsend[ch, rows_of(r), 0:width] = jnp.where(first, f_mid, f)
            gsend[ch, rows_of(r), width : 2 * width] = jnp.where(first, s, s_mid)
            give_copy(r, ch).start()
            wbuf[ch, rows_of(r), 0:width] = jnp.where(first, f, f_mid)
            wbuf[ch, rows_of(r), width : 2 * width] = jnp.where(first, s_mid, s)
            return 0

        lax.fori_loop(0, tiles, own_half, 0)

        def settle(r, _, ch=ch):
            resolve(r, core, ch, wbuf[ch, rows_of(r), 0:width], wbuf[ch, rows_of(r), width : 2 * width])
            return 0

        lax.fori_loop(0, tiles, settle, 0)

        def other_half(k, _, ch=ch):
            r = turn(k, ch)
            give_copy(r, ch).wait_recv()
            resolve(r, 1 - core, ch, grecv[ch, rows_of(r), 0:width], grecv[ch, rows_of(r), width : 2 * width])
            return 0

        lax.fori_loop(0, tiles, other_half, 0)

    for ch in range(CHUNKS):
        swap(ch).wait_send()

        def drain(r, _, ch=ch):
            give_copy(r, ch).wait_send()

            @pl.when(chip_of[ch](r) != chip)
            def _():
                out_copy(r, ch).wait_send()

            return 0

        lax.fori_loop(0, tiles, drain, 0)

        @pl.when(is_owner[ch])
        def _(ch=ch):
            def drain_back(k, _):
                back_copy(lax.rem(chip + k, chips), ch).wait_send()
                return 0

            lax.fori_loop(1, chips, drain_back, 0)


def chain_peers(chips, chip, core):
    return [
        (chips - 1, lambda k: {"tm": 2 * lax.rem(chip + 1 + k, chips) + core}),
        (1, lambda k: {"tm": 2 * chip + 1 - core}),
    ]


def chain_scratch(chips, half, tiles):
    width, full = half // CHUNKS, tiles * ROWS
    wide = 2 * width + LANES
    f32 = jnp.float32
    dma = pltpu.SemaphoreType.DMA
    return [
        pltpu.VMEM((LANES, LANES), f32), pltpu.VMEM((LANES, LANES), f32),
        pltpu.VMEM((CHUNKS, full, wide), f32), pltpu.VMEM((CHUNKS, full, wide), f32),
        pltpu.VMEM((CHUNKS, full, 2 * width), f32),
        pltpu.VMEM((CHUNKS, full, wide), f32), pltpu.VMEM((CHUNKS, chips, ROWS, wide), f32),
        pltpu.VMEM((CHUNKS, chips, ROWS, 2 * width), f32), pltpu.VMEM((CHUNKS, full, 2 * width), f32),
        pltpu.VMEM((CHUNKS, full, 2 * width), f32), pltpu.VMEM((CHUNKS, full, 2 * width), f32),
        dma((CHUNKS,)), dma((CHUNKS,)), dma((CHUNKS, tiles)), dma((CHUNKS, chips)), dma((CHUNKS, chips)),
        dma((CHUNKS, tiles)), dma((CHUNKS, tiles)), dma((CHUNKS, tiles)),
    ]


def lanes_of(side, ch, half):
    width = half // CHUNKS
    return pl.ds(pl.multiple_of(side * half + ch * width, LANES), width)


def smooth_kernel(chips, x_hbm, decay_ref, gain_ref, norm_ref, doc_ref, word_ref, count_ref,
                  tw_ref, order_ref, edge_ref, raw, xs, load_sem, flat, table, spread, *bufs):
    core, chip = lax.rem(lax.axis_index("tm"), 2), lax.axis_index("tm") // 2
    slices, full, words = xs.shape
    half, tiles, blocks = words // 2, full // ROWS, words // LANES
    pitch = slices * blocks
    meet = greet(chain_peers(chips, chip, core))
    load = pltpu.make_async_copy(x_hbm, raw.at[0 : x_hbm.shape[0]], load_sem.at[0])
    load.start()
    decay = [decay_ref[s : s + 1, :] for s in range(2)]
    gain = [gain_ref[s : s + 1, :] for s in range(2)]
    norm = [norm_ref[s : s + 1, :] for s in range(2)]
    keep = keep_rows(gain_ref, slices * 2 * chips)
    one = jnp.ones_like(decay[0])
    spread_coefs(
        [decay[0], decay[1], one, 1.0 - decay[0], 1.0 - decay[1], gain[1], gain[0], one,
         keep[0], keep[1], norm[0], norm[1]], table, spread)
    if x_hbm.shape[0] < raw.shape[0]:
        raw[x_hbm.shape[0] :, :] = jnp.zeros((raw.shape[0] - x_hbm.shape[0], LANES), jnp.float32)
    load.wait()

    def move(r, _):
        rows = pl.ds(pl.multiple_of(r * ROWS, ROWS), ROWS)
        for s in range(slices):
            for i in range(blocks):
                xs[s, rows, i * LANES : (i + 1) * LANES] = raw[
                    pl.ds(r * (ROWS * pitch) + i * slices + s, ROWS, stride=pitch), :]
        return 0

    lax.fori_loop(0, tiles, move, 0)

    def source(s, r, side, ch):
        return xs[s, pl.ds(pl.multiple_of(r * ROWS, ROWS), ROWS), lanes_of(side, ch, half)]

    def finish(s, r, side, ch, q):
        rows = pl.ds(pl.multiple_of(r * ROWS, ROWS), ROWS)
        tw_ref[s, rows, lanes_of(side, ch, half)] = jnp.exp(q - spread[rows, X0 + s : X0 + s + 1])

    def order():
        word = word_ref[...] - lax.axis_index("word") * words
        doc = doc_ref[...]
        keys = (((doc >> 8) * WORD_SPAN + word) << 12) | ((doc & 255) << 4) | count_ref[...]
        keys = sort_entries(keys)
        edge_ref[0:8, :] = keys[0:8]
        edge_ref[8:16, :] = keys[-8:]
        flat[...] = keys
        for s in range(slices):
            order_ref[s, 0:128, :] = flat[pl.ds(s, 128, stride=slices), :].T
            order_ref[s, 128:, :] = jnp.full((SPARE - 128, 128), -1, jnp.int32)

    two_sided(chips, chip, core, half, tiles, spread, source, finish, order, meet, bufs)


def adjoint_kernel(chips, shares, t_hbm, dense_hbm, w_ref, decay_ref, gain_ref, out_ref, own_ref,
                   es, ts, tot_ref, sums_ref, load_sem, dense, dense_sem, wraw, w32, wb, wt, tr, ratio, sums, tots,
                   totals, tot_in, sums_in, tot_sem, sum_sem, table, spread, *bufs):
    core, chip = lax.rem(lax.axis_index("tm"), 2), lax.axis_index("tm") // 2
    share = lax.axis_index("word")
    slices, full, words = es.shape
    half, tiles, blocks = words // 2, full // ROWS, words // LANES
    pitch = slices * blocks
    neighbour = lambda k: {"word": lax.rem(share + 1 + k, shares)}
    meet = greet(chain_peers(chips, chip, core) + [(shares - 1, neighbour)])
    expect(t_hbm, dense_hbm, w_ref, es, ts, tot_ref, sums_ref, load_sem, dense, dense_sem,
           wraw, w32, wb, wt, tr, ratio, sums, tots, table)
    decay = [decay_ref[s : s + 1, :] for s in range(2)]
    gain = [gain_ref[s : s + 1, :] for s in range(2)]
    keep = keep_rows(gain_ref, slices * 2 * chips)
    one = jnp.ones_like(decay[0])
    spread_coefs(
        [one, gain[0], gain[1], one, one, one, decay[1], decay[0],
         keep[0], keep[1], 1.0 - decay[0], 1.0 - decay[1]], table, spread)
    meet()

    def tot_copy(k):
        return pltpu.make_async_remote_copy(
            src_ref=tot_ref, dst_ref=tot_in.at[shares - 2 - k], send_sem=tot_sem.at[0, k],
            recv_sem=tot_sem.at[1, shares - 2 - k], device_id=neighbour(k), device_id_type=MESH)

    def sum_copy(k):
        return pltpu.make_async_remote_copy(
            src_ref=sums_ref.at[lax.rem(share + 1 + k, shares)], dst_ref=sums_in.at[shares - 2 - k],
            send_sem=sum_sem.at[0, k], recv_sem=sum_sem.at[1, shares - 2 - k],
            device_id=neighbour(k), device_id_type=MESH)

    for k in range(shares - 1):
        tot_copy(k).start()
    total = tot_ref[...]
    for k in range(shares - 1):
        tot_copy(shares - 2 - k).wait_recv()
        total = total + tot_in[k]
    table[...] = jnp.zeros_like(table)
    table[0:ROWS, :] = total
    totals[...] = table[...].T

    def source(s, r, side, ch):
        rows, lanes = pl.ds(pl.multiple_of(r * ROWS, ROWS), ROWS), lanes_of(side, ch, half)
        return es[s, rows, lanes] - totals[rows, s : s + 1] * ts[s, rows, lanes]

    def finish(s, r, side, ch, q):
        rows = pl.ds(pl.multiple_of(r * ROWS, ROWS), ROWS)
        grad = spread[rows, X0 + s : X0 + s + 1] * q
        width = half // CHUNKS
        at = r * (ROWS * pitch) + (side * half + ch * width) // LANES * slices + s
        for i in range(width // LANES):
            out_ref[pl.ds(at + i * slices, ROWS, stride=pitch), :] = grad[:, i * LANES : (i + 1) * LANES]

    def gather_sums():
        for k in range(shares - 1):
            sum_copy(k).start()

    def take_sums():
        for s in range(slices):
            sums = sums_ref[share, s]
            for k in range(shares - 1):
                if s == 0:
                    sum_copy(shares - 2 - k).wait_recv()
                sums = sums + sums_in[k, s]
            own_ref[pl.ds(s, full, stride=slices), :] = sums

    two_sided(chips, chip, core, half, tiles, spread, source, finish, gather_sums, None, bufs)
    take_sums()
    for k in range(shares - 1):
        tot_copy(k).wait_send()
        sum_copy(k).wait_send()


def sort_entries(x):
    shape = (x.shape[0] // 8, 8, 128)
    x = x.reshape(shape)
    high = shape[0].bit_length() - 1
    depth = high + 2 + 7
    sub = lax.broadcasted_iota(jnp.int32, (8, 128), 0)
    lane = lax.broadcasted_iota(jnp.int32, (8, 128), 1)

    def bit_of(j):
        return (sub >> (j - high + 1)) & 1 if j < high + 2 else (lane >> (j - high - 2)) & 1

    def parts(x, j):
        pieces = x.reshape((shape[0] >> (j + 1), 2, 1 << j, 8, 128))
        return pieces[:, 0], pieces[:, 1]

    def joined(a, b):
        return jnp.stack([a, b], axis=1).reshape(shape)

    def flip(x, k):
        if k >= depth:
            return x
        if k >= high:
            return x ^ (-bit_of(k))[None]
        a, b = parts(x, k)
        return joined(a, ~b)

    def exchange(x, j):
        if j < high:
            a, b = parts(x, j)
            return joined(jnp.minimum(a, b), jnp.maximum(a, b))
        low = (bit_of(j) == 0)[None]
        if j < high + 2:
            step, size = 1 << (j - high + 1), 8
            y = x
        else:
            step, size = 1 << (j - high - 2), 128
            y = x.reshape((shape[0] * 8, 128))
        partner = ahead = pltpu.roll(y, size - step, 1).reshape(shape)
        if 2 * step != size:
            partner = jnp.where(low, ahead, pltpu.roll(y, step, 1).reshape(shape))
        return jnp.where(low, jnp.minimum(x, partner), jnp.maximum(x, partner))

    for k in range(1, depth + 1):
        x = flip(x, k)
        for j in range(k - 1, -1, -1):
            x = exchange(x, j)
        x = flip(x, k)
    return x.reshape((shape[0] * 8, 128))


def count_kernel(words, order_ref, edge_ref, dense_hbm, bounds, place, acc, save_sem):
    slices = order_ref.shape[0]
    tiles, blocks = words // TILE_W, acc.shape[1] // TILE_D
    together = acc.shape[0] // 2
    for s in range(slices):
        least, most = edge_ref[s : s + 1, :], edge_ref[16 - slices + s : 17 - slices + s, :]
        for h in range(blocks):
            for j in range(tiles):
                low = (h * WORD_SPAN + j * TILE_W) << 12
                bounds[s * tiles + j, h, 0] = jnp.sum((most < low).astype(jnp.int32))
                bounds[s * tiles + j, h, 1] = jnp.sum((least < low + (TILE_W << 12)).astype(jnp.int32))
    place[...] = lax.broadcasted_iota(jnp.int32, place.shape, 0).astype(jnp.float32).astype(jnp.bfloat16)

    def save(t, slot):
        return pltpu.make_async_copy(
            acc.at[pl.ds(slot * together, together)], dense_hbm.at[pl.ds(t * together, together)], save_sem.at[slot])

    def step(t, _):
        slot = lax.rem(t, 2)
        s = lax.div(t * together, tiles)

        @pl.when(t >= 2)
        def _():
            save(t - 2, slot).wait()

        acc[pl.ds(slot * together, together)] = jnp.zeros((together,) + acc.shape[1:], jnp.float32)
        groups = [(n, h) for n in range(together) for h in range(blocks)]
        starts = [bounds[t * together + n, h, 0] for n, h in groups]
        longest = starts[0] * 0
        for start, (n, h) in zip(starts, groups):
            longest = jnp.maximum(longest, (bounds[t * together + n, h, 1] - start + DEEP - 1) // DEEP)

        def batch(i, _):
            for start, (n, h) in zip(starts, groups):
                base = h * WORD_SPAN + (t * together + n - s * tiles) * TILE_W
                at = jnp.minimum(start + DEEP * i, SPARE - DEEP)
                key = jnp.concatenate([order_ref[s, pl.ds(at + m, 1), :] for m in range(DEEP)], axis=1)
                word = ((key >> 12) - base).astype(jnp.float32).astype(jnp.bfloat16)
                doc = ((key >> 4) & 255).astype(jnp.float32).astype(jnp.bfloat16)
                count = (key & 15).astype(jnp.float32).astype(jnp.bfloat16)
                docs_hot = jnp.where(place[...] == doc, count, jnp.bfloat16(0))
                words_hot = jnp.where(place[...] == word, jnp.bfloat16(1), jnp.bfloat16(0))
                acc[slot * together + n, h * TILE_D : (h + 1) * TILE_D, :] += lax.dot_general(
                    docs_hot, words_hot, (((1,), (1,)), ((), ())), preferred_element_type=jnp.float32)
            return 0

        lax.fori_loop(0, longest, batch, 0)
        save(t, slot).start()
        return 0

    steps = slices * tiles // together
    lax.fori_loop(0, steps, step, 0)
    for t in (steps - 2, steps - 1):
        save(t, t % 2).wait()


def fill_slice(s, wraw, w32, wb, wt):
    slices, pieces = 2, w32.shape[1] // LANES
    full = wraw.shape[0] // (slices * pieces)
    for i in range(pieces):
        w32[0:full, i * LANES : (i + 1) * LANES] = wraw[pl.ds(i * slices + s, full, stride=slices * pieces), :]
    wb[...] = w32[...].astype(jnp.bfloat16)
    wt[...] = w32[...].T.astype(jnp.bfloat16)


def expect(t_hbm, dense_hbm, w_ref, es, ts, tot, sums_out, load_sem, dense, dense_sem,
           wraw, w32, wb, wt, tr, ratio, sums, tots, turned):
    slices, full, words = ts.shape
    shares, docs = sums_out.shape[0], w32.shape[1]
    tiles, blocks = words // TILE_W, docs // TILE_D

    def load(s):
        return pltpu.make_async_copy(t_hbm.at[s], ts.at[s], load_sem.at[s])

    def fetch(t):
        return pltpu.make_async_copy(dense_hbm.at[t], dense.at[t], dense_sem.at[t])

    for s in range(slices):
        load(s).start()

        def ask(j, _, s=s):
            fetch(s * tiles + j).start()
            return 0

        lax.fori_loop(0, tiles, ask, 0)
    wraw[w_ref.shape[0] :, :] = jnp.zeros((wraw.shape[0] - w_ref.shape[0], LANES), jnp.float32)
    wraw[0 : w_ref.shape[0], :] = w_ref[...].astype(jnp.float32)
    w32[...] = jnp.zeros_like(w32)
    tr[full // 16 * 16 :, :] = jnp.zeros((128 - full // 16 * 16, words), jnp.bfloat16)
    lane = lax.broadcasted_iota(jnp.int32, (full, LANES), 1)
    turned[...] = jnp.zeros_like(turned)

    for s in range(slices):
        fill_slice(s, wraw, w32, wb, wt)
        load(s).wait()
        tr[0:full, :] = ts[s].astype(jnp.bfloat16)
        sums[...] = jnp.zeros_like(sums)
        tots[...] = jnp.zeros_like(tots)

        def one_tile(j, _, s=s):
            lanes = pl.ds(pl.multiple_of(j * SPAN * TILE_W, TILE_W), SPAN * TILE_W)
            topic = tr[:, lanes]
            for n in range(SPAN):
                t = s * tiles + j * SPAN + n
                part = slice(n * TILE_W, (n + 1) * TILE_W)
                fetch(t).wait()
                for h in range(blocks):
                    rows = slice(h * TILE_D, (h + 1) * TILE_D)
                    mixture = jnp.dot(wt[rows, :], topic[:, part], preferred_element_type=jnp.float32)
                    ratio[rows, part] = (dense[t, rows, :] / mixture).astype(jnp.bfloat16)
            sums[...] += lax.dot_general(
                topic, ratio[...], (((1,), (1,)), ((), ())), preferred_element_type=jnp.float32)
            weighted = jnp.dot(wb[...], ratio[...], preferred_element_type=jnp.float32)
            expected = topic[0:full].astype(jnp.float32) * weighted[0:full]
            es[s, :, lanes] = expected
            for n in range(SPAN):
                tots[...] += expected[:, n * TILE_W : (n + 1) * TILE_W]
            return 0

        lax.fori_loop(0, tiles // SPAN, one_tile, 0)
        for y in range(shares):
            own = slice(y * (docs // shares), (y + 1) * (docs // shares))
            sums_out[y, s] = sums[0:full, own] * w32[0:full, own]
        turned[0:full, :] = jnp.where(lane == s, jnp.sum(tots[...], axis=1, keepdims=True), turned[0:full, :])
    tot[...] = turned[...].T[0:ROWS, :]


VMEM_SPEC = pl.BlockSpec(memory_space=pltpu.VMEM)
ANY_SPEC = pl.BlockSpec(memory_space=pl.ANY)
LIMIT = 60 * 1024 * 1024


def count_entries(order, edges, words, docs):
    slices = order.shape[0]
    tiles = words // TILE_W
    return pl.pallas_call(
        functools.partial(count_kernel, words),
        out_shape=jax.ShapeDtypeStruct((slices * tiles, docs, TILE_W), jnp.float32),
        in_specs=[VMEM_SPEC] * 2,
        out_specs=ANY_SPEC,
        scratch_shapes=[
            pltpu.SMEM((slices * tiles, docs // TILE_D, 2), jnp.int32),
            pltpu.VMEM((TILE_W, DEEP * 128), jnp.bfloat16),
            pltpu.VMEM((2 * TOGETHER, docs, TILE_W), jnp.float32),
            pltpu.SemaphoreType.DMA((2,)),
        ],
        compiler_params=pltpu.CompilerParams(vmem_limit_bytes=LIMIT),
        name="count",
    )(order, edges)


def interleaved(x):
    slices, rows, columns = x.shape
    group = 4 if columns % (4 * LANES) == 0 else 1
    x = x.transpose((1, 0, 2)).reshape((rows, slices, columns // LANES // group, group, LANES))
    x = x.transpose((0, 2, 3, 1, 4))
    return x.reshape((rows * columns // LANES * slices, LANES))


def separated(x, slices, rows, columns):
    x = x[: rows * columns // LANES * slices].reshape((rows, columns // LANES, slices, LANES))
    return x.transpose((0, 2, 1, 3)).reshape((rows, slices, columns)).transpose((1, 0, 2))


def make_local(chips, shares):
    def local(pseudo_obs, filter_decay, smooth_gain, log_norm, doc_weights, doc_ids, word_ids, counts):
        slices, topics, words = pseudo_obs.shape
        tiles, half = -(-topics // ROWS), words // 2
        full = tiles * ROWS
        docs = doc_weights.shape[2]
        entries = doc_ids.shape[1]
        f32, bf16 = jnp.float32, jnp.bfloat16
        dma = pltpu.SemaphoreType.DMA
        flat_rows = full * slices * words // LANES
        ids = [interleaved(a[:, None, :]) for a in (doc_ids, word_ids, counts)]
        topic_word, order, edges = pl.pallas_call(
            functools.partial(smooth_kernel, chips),
            out_shape=(
                jax.ShapeDtypeStruct((slices, full, words), f32),
                jax.ShapeDtypeStruct((slices, SPARE, LANES), jnp.int32),
                jax.ShapeDtypeStruct((16, LANES), jnp.int32),
            ),
            in_specs=[ANY_SPEC] + [VMEM_SPEC] * 6,
            out_specs=(VMEM_SPEC,) * 3,
            scratch_shapes=[
                pltpu.VMEM((flat_rows, LANES), f32), pltpu.VMEM((slices, full, words), f32), dma((1,)),
                pltpu.VMEM((slices * entries // LANES, LANES), jnp.int32),
            ] + chain_scratch(chips, half, tiles),
            compiler_params=pltpu.CompilerParams(
                collective_id=0, has_side_effects=True, vmem_limit_bytes=LIMIT),
            name="smooth",
        )(interleaved(pseudo_obs), filter_decay, smooth_gain, log_norm, *ids)
        dense = count_entries(order, edges, words, docs)
        grad, own = pl.pallas_call(
            functools.partial(adjoint_kernel, chips, shares),
            out_shape=(
                jax.ShapeDtypeStruct((flat_rows, LANES), f32),
                jax.ShapeDtypeStruct((slices * full, docs // shares), f32),
            ),
            in_specs=[ANY_SPEC, ANY_SPEC] + [VMEM_SPEC] * 3,
            out_specs=(VMEM_SPEC, VMEM_SPEC),
            scratch_shapes=[
                pltpu.VMEM((slices, full, words), f32), pltpu.VMEM((slices, full, words), f32),
                pltpu.VMEM((ROWS, LANES), f32), pltpu.VMEM((shares, slices, full, docs // shares), f32),
                dma((slices,)), pltpu.VMEM(dense.shape, f32), dma((dense.shape[0],)),
                pltpu.VMEM((full * slices * docs // LANES, LANES), f32), pltpu.VMEM((128, docs), f32),
                pltpu.VMEM((128, docs), bf16), pltpu.VMEM((docs, 128), bf16), pltpu.VMEM((128, words), bf16),
                pltpu.VMEM((docs, SPAN * TILE_W), bf16), pltpu.VMEM((128, docs), f32), pltpu.VMEM((full, TILE_W), f32),
                pltpu.VMEM((LANES, LANES), f32), pltpu.VMEM((shares - 1, ROWS, LANES), f32),
                pltpu.VMEM((shares - 1, slices, full, docs // shares), f32),
                dma((2, shares - 1)), dma((2, shares - 1)),
            ] + chain_scratch(chips, half, tiles),
            compiler_params=pltpu.CompilerParams(
                collective_id=1, has_side_effects=True, vmem_limit_bytes=LIMIT),
            name="adjoint",
        )(topic_word, dense, interleaved(doc_weights), filter_decay, smooth_gain)
        return separated(grad, slices, topics, words), separated(own, slices, topics, docs // shares)

    return local


def solution(mesh):
    return jax.shard_map(
        make_local(mesh.shape["tm"] // 2, mesh.shape["word"]),
        mesh=mesh,
        in_specs=(
            P("tm", None, "word"),
            P("tm", None),
            P("tm", None),
            P("tm", None),
            P("tm", None, None),
            P("tm", "word"),
            P("tm", "word"),
            P("tm", "word"),
        ),
        out_specs=(P("tm", None, "word"), P("tm", None, "word")),
        check_vma=False,
    )
```
